512 devices in a mesh: gx: 4 (over z_lo, core), gy: 16 (over z_hi, x), gz: 8 (over y).
Axes of the slice: x: 4, y: 8, z: 8 (z_hi: 4, z_lo: 2; z = z_hi * 2 + z_lo), core: 2. Of those that a mesh axis runs over, the one named last changes fastest.
Arguments:
- body_force: float32 [3, 64, 32, 2048], P(None, 'gz', 'gx', 'gy'), may hold values from -6 to 6
- viscosity: float32 [64, 32, 2048], P('gz', 'gx', 'gy'), may hold values from 0.05 to 0.5
- topography: float32 [256, 16384], P('gx', 'gy'), may hold values from -6 to 6
- kappa: bfloat16 [256, 16384], P('gx', 'gy'), may hold values from 0.019897461 to 0.19921875
Outputs:
- velocity: float32 [3, 64, 32, 2048], P(None, 'gz', 'gx', 'gy')
- surface: float32 [256, 16384], P('gx', ('gy', 'gz'))
The draws below stay inside these ranges and needn't reach their ends.
All inputs are finite; a program needn't handle non-finite values.
Results may differ from the reference program's by a relative error of at most 0.0008.
Values may be sent and summed in bfloat16 or wider, within the bound.
No kernel may reach another device: no remote copies, remote signals or barrier semaphores. Data moves between devices by JAX's collectives and lax.ppermute only.
A program may use at most 64 MiB of HBM per device.

```python
import math
import jax
import jax.numpy as jnp

ITERS = 2
STEPS = 8
FR = 8
FC = 8
NX = 32
NY = 2048
NZ = 64
NR = 256
NC = 16384


def level_of(stream_key, dims, pieces, least, largest):
    gain = 1.0
    for dim, parts in pieces:
        draws = jax.random.uniform(jax.random.fold_in(jax.random.fold_in(stream_key, 6), dim), (parts,), jnp.float32, least / len(pieces), largest / len(pieces))
        gain = gain * jnp.repeat(jnp.exp(draws), dims[dim] // parts).reshape((-1,) + (1,) * (len(dims) - 1 - dim))
    return gain


def noise(own_key, dims, width, limit, shards=(), kind=jnp.bfloat16):
    drawn = jax.random.normal(own_key, dims, jnp.float32) * width
    if len(shards) > 0:
        drawn = level_of(own_key, dims, shards, -0.22, 0.18) * drawn
    return jnp.clip(drawn, min=-limit, max=limit).astype(kind)


def setup_inputs(seed: int = 0) -> dict:
    keys = jax.random.split(jax.random.key(seed), 5)
    return {
        "body_force": noise(keys[0], (3, NZ, NX, NY), 1.0, 6.0, ((1, 8), (2, 4), (3, 16)), jnp.float32),
        "viscosity": jnp.clip(jnp.exp(math.log(0.5) - 2.3025851 * jax.random.uniform(keys[1], (NZ, NX, NY), jnp.float32) ** level_of(keys[1], (NZ, NX, NY), ((0, 8), (1, 4), (2, 16)), -0.2, 0.2)), 0.05, 0.5),
        "topography": noise(keys[2], (NR, NC), 1.0, 6.0, ((0, 4), (1, 16)), jnp.float32),
        "kappa": jnp.clip(jnp.exp(math.log(0.19921875) - 2.3038113 * jax.random.uniform(keys[3], (NR, NC), jnp.float32) ** level_of(keys[3], (NR, NC), ((0, 4), (1, 16)), -0.2, 0.2)), 0.019897461, 0.19921875).astype(jnp.bfloat16),
    }


drag = 1.0
time_step = 1.0
load_gain = 4.0

def shifts():
    found = []
    for depth in (-1, 0, 1):
        for across in (-1, 0, 1):
            for along in (-1, 0, 1):
                if depth != 0 or across != 0 or along != 0:
                    found.append((depth, across, along))
    return found

def window(array, depth, across, along):
    inner_depth = array.shape[-3] - 2
    inner_rows = array.shape[-2] - 2
    inner_cols = array.shape[-1] - 2
    return array[..., 1 + depth:1 + depth + inner_depth, 1 + across:1 + across + inner_rows, 1 + along:1 + along + inner_cols]

def apply_operator(padded, viscous):
    center = window(padded, 0, 0, 0)
    eta_center = window(viscous, 0, 0, 0)
    total = drag * center
    for depth, across, along in shifts():
        weight = 0.5 / (depth * depth + across * across + along * along)
        coupling = weight * (eta_center + window(viscous, depth, across, along))
        total = total + coupling * (center - window(padded, depth, across, along))
    return total

def pad_cells(field):
    return jnp.pad(field, ((0, 0), (1, 1), (1, 1), (1, 1)))

def flux(slope, conduct):
    return conduct * slope / jnp.sqrt(1.0 + slope * slope)

def diffuse_step(extended, conduct):
    along = flux(extended[:, 1:] - extended[:, :-1], 0.5 * (conduct[:, 1:] + conduct[:, :-1]))
    across = flux(extended[1:, :] - extended[:-1, :], 0.5 * (conduct[1:, :] + conduct[:-1, :]))
    change = along[1:-1, 1:] - along[1:-1, :-1] + across[1:, 1:-1] - across[:-1, 1:-1]
    return extended[1:-1, 1:-1] + time_step * change

def reference(body_force, viscosity, topography, kappa):
    load = topography.reshape(NX, FR, NY, FC).mean(axis=(1, 3))
    force = body_force.at[2, NZ - 1].add(-load_gain * load)
    viscous = pad_cells(viscosity[None])
    velocity = jnp.zeros_like(force)
    residual = force
    direction = force
    norm_now = jnp.sum(residual * residual)
    for step in range(ITERS):
        image = apply_operator(pad_cells(direction), viscous)
        alpha = norm_now / jnp.sum(direction * image)
        velocity = velocity + alpha * direction
        if step + 1 < ITERS:
            residual = residual - alpha * image
            norm_next = jnp.sum(residual * residual)
            direction = residual + norm_next / norm_now * direction
            norm_now = norm_next
    top = velocity[2, NZ - 1]
    rise = jnp.broadcast_to(top[:, None, :, None], (NX, FR, NY, FC)).reshape(NR, NC)
    conduct = jnp.pad(kappa.astype(jnp.float32), 1)
    height = topography
    for step in range(STEPS):
        height = diffuse_step(jnp.pad(height, 1), conduct)
    surface = height + STEPS * time_step * rise
    return (velocity, surface)
```

```python
import jax
import jax.numpy as jnp
from jax import lax
from jax.experimental import pallas as pl
from jax.experimental.pallas import tpu as pltpu
from jax.sharding import PartitionSpec as P

STEPS = 8
DRAG = 1.0
TIME_STEP = 1.0
LOAD_GAIN = 4.0
FACE, EDGE, CORNER = 0.5, 0.25, 0.5 / 3.0
TOTAL = 6 * FACE + 12 * EDGE + 8 * CORNER

DEPTHS = 12
PLANES = 4 * DEPTHS
PAIRS_ROW = 2 * PLANES
SURFACE_ROW = PAIRS_ROW + 8
GX_ROWS = SURFACE_ROW + 32

f32 = jnp.float32


def vmem():
    return pl.BlockSpec(memory_space=pltpu.VMEM)


def call(body, outs, ins, scratch=(), cost=20000):
    return pl.pallas_call(
        body,
        out_shape=[jax.ShapeDtypeStruct(s, f32) for s in outs],
        in_specs=[vmem() for _ in ins],
        out_specs=[vmem() for _ in outs],
        scratch_shapes=list(scratch),
        cost_estimate=pl.CostEstimate(flops=cost * 1024, bytes_accessed=1 << 18, transcendentals=0),
    )(*ins)


def lanes(shape):
    return lax.broadcasted_iota(jnp.int32, shape, len(shape) - 1)


def rolled(x, amount, axis=1):
    amount = amount % x.shape[axis]
    return x if amount == 0 else pltpu.roll(x, amount, axis)


def surface_own(topo_ref, kappa_ref, load_ref, height_ref, conduct_ref, left_ref, right_ref):
    g = lax.axis_index("gz")
    last = lax.axis_size("gz") - 1
    lane = lanes((8, 128))
    pieces = []
    for v in range(8):
        piece = topo_ref[:, 128 * v : 128 * v + 128].reshape(8, 8, 128)
        pieces.append(jnp.sum(piece, axis=1))
    stacked = jnp.concatenate(pieces, axis=0)
    pick = (
        lax.broadcasted_iota(jnp.int32, (128, 128), 0) // 8 == lax.broadcasted_iota(jnp.int32, (128, 128), 1)
    ).astype(f32)
    sums = jnp.dot(stacked, pick, precision=lax.Precision.HIGHEST, preferred_element_type=f32)
    load = jnp.zeros((8, 128), f32)
    for v in range(8):
        load = load + rolled(sums[8 * v : 8 * v + 8], 16 * v)
    load_ref[...] = jnp.where(g == last, load * (-LOAD_GAIN / 64.0), 0.0)
    wide = lanes((64, 128))
    own = pl.ds(pl.multiple_of(g * 128, 128), 128)
    before = pl.ds(pl.multiple_of(jnp.maximum(g - 1, 0) * 128, 128), 128)
    after = pl.ds(pl.multiple_of(jnp.minimum(g + 1, last) * 128, 128), 128)
    for source, target in ((topo_ref, height_ref), (kappa_ref, conduct_ref)):
        target[:, 0:128] = source[:, own].astype(f32)
        side = jnp.where((wide < 8) & (g < last), source[:, after].astype(f32), 0.0)
        side = jnp.where((wide >= 120) & (g > 0), source[:, before].astype(f32), side)
        target[:, 128:256] = side
    width = topo_ref.shape[1]
    left = jnp.zeros((8, 128), f32)
    right = jnp.zeros((8, 128), f32)
    slot = 0
    for source in (topo_ref, kappa_ref):
        head = source[:, 0:128].astype(f32)
        tail = source[:, width - 128 : width].astype(f32)
        for r in range(8):
            mask = lane // 8 == slot
            left = jnp.where(mask, rolled(head[8 * r : 8 * r + 8], 8 * slot), left)
            right = jnp.where(mask, rolled(tail[8 * r : 8 * r + 8], 8 * slot - 120), right)
            slot += 1
    left_ref[...] = left
    right_ref[...] = right


def assemble(force_ref, visc_ref, load_ref, low_ref, high_ref, sl_ref, sr_ref, planes_ref, left_ref, right_ref):
    lane = lanes((8, 128))
    left = jnp.zeros((8, 128), f32)
    right = jnp.zeros((8, 128), f32)
    for field in range(4):
        for depth in range(DEPTHS):
            if depth < 2:
                plane = low_ref[2 * field + depth]
            elif depth >= DEPTHS - 2:
                plane = high_ref[2 * field + depth - (DEPTHS - 2)]
            elif field == 3:
                plane = visc_ref[depth - 2]
            else:
                plane = force_ref[field, depth - 2]
                if field == 2 and depth == DEPTHS - 3:
                    plane = plane + load_ref[...]
            p = field * DEPTHS + depth
            planes_ref[p] = plane
            mask = lane // 2 == p
            left = jnp.where(mask, rolled(plane, 2 * p), left)
            right = jnp.where(mask, rolled(plane, 2 * p - 126), right)
    left_ref[0] = left
    right_ref[0] = right
    left_ref[1] = sl_ref[...]
    right_ref[1] = sr_ref[...]


def prepare_rows(planes_ref, rl_ref, rr_ref, height_ref, conduct_ref, down_ref, up_ref, height_out, conduct_out):
    g = lax.axis_index("gz")
    last = lax.axis_size("gz") - 1
    lane = lanes((8, 128))
    for p in range(PLANES):
        down_ref[2 * p : 2 * p + 2, :] = planes_ref[p, 6:8, :]
        up_ref[2 * p : 2 * p + 2, :] = planes_ref[p, 0:2, :]
    down_ref[PAIRS_ROW : PAIRS_ROW + 4, :] = jnp.concatenate([rl_ref[0, 6:8, :], rr_ref[0, 6:8, :]], axis=0)
    up_ref[PAIRS_ROW : PAIRS_ROW + 4, :] = jnp.concatenate([rl_ref[0, 0:2, :], rr_ref[0, 0:2, :]], axis=0)
    down_ref[PAIRS_ROW + 4 : SURFACE_ROW, :] = jnp.zeros((4, 128), f32)
    up_ref[PAIRS_ROW + 4 : SURFACE_ROW, :] = jnp.zeros((4, 128), f32)
    slot = 0
    for index, (source, target) in enumerate(((height_ref, height_out), (conduct_ref, conduct_out))):
        base = SURFACE_ROW + 16 * index
        for r in range(8):
            rows = slice(8 * r, 8 * r + 8)
            main = source[rows, 0:128]
            side = source[rows, 128:256]
            side = jnp.where((g == 0) & (lane >= 120), rolled(rl_ref[1], 120 - 8 * slot), side)
            side = jnp.where((g == last) & (lane < 8), rolled(rr_ref[1], -8 * slot), side)
            target[rows, 0:128] = main
            target[rows, 128:256] = side
            if r == 0:
                up_ref[base : base + 8, :] = main
                up_ref[base + 8 : base + 16, :] = side
            if r == 7:
                down_ref[base : base + 8, :] = main
                down_ref[base + 8 : base + 16, :] = side
            slot += 1


def stencil(before, here, after):
    outer = before + after
    a = FACE * here + EDGE * outer
    b = EDGE * here + CORNER * outer
    both = a + rolled(b, 1, 0) + rolled(b, 15, 0)
    rows = rolled(a, 1, 0) + rolled(a, 15, 0)
    return FACE * outer + rows + rolled(both, 1, 1) + rolled(both, 255, 1)


def operate(planes_ref, rl_ref, rr_ref, before_ref, after_ref, image_ref, sums_ref, top_ref, x, w, diag):
    lane = lanes((8, 128))
    row = lax.broadcasted_iota(jnp.int32, (8, 128), 0)
    pad = jnp.zeros((4, 128), f32)
    lower_l = jnp.concatenate([after_ref[PAIRS_ROW : PAIRS_ROW + 2, :], pad, before_ref[PAIRS_ROW : PAIRS_ROW + 2, :]], 0)
    lower_r = jnp.concatenate(
        [after_ref[PAIRS_ROW + 2 : PAIRS_ROW + 4, :], pad, before_ref[PAIRS_ROW + 2 : PAIRS_ROW + 4, :]], 0
    )
    for p in range(PLANES):
        x[p, 0:8, 0:128] = planes_ref[p]
        x[p, 8:16, 0:128] = jnp.concatenate(
            [after_ref[2 * p : 2 * p + 2, :], pad, before_ref[2 * p : 2 * p + 2, :]], 0
        )
        for start, l, r in ((0, rl_ref[0], rr_ref[0]), (8, lower_l, lower_r)):
            side = jnp.where(lane < 2, rolled(r, -2 * p), 0.0)
            side = jnp.where(lane >= 126, rolled(l, 126 - 2 * p), side)
            x[p, start : start + 8, 128:256] = side
    for depth in range(1, DEPTHS - 1):
        e = [x[3 * DEPTHS + depth + i] for i in (-1, 0, 1)]
        d = (DRAG + TOTAL * e[1]) + stencil(*e)
        diag[depth] = d[0:8, 0:128]
        inside = e[1] > 0.0
        for c in range(3):
            v = [x[c * DEPTHS + depth + i] for i in (-1, 0, 1)]
            ev = [e[i] * v[i] for i in range(3)]
            out = v[1] * d - e[1] * stencil(*v) - stencil(*ev)
            w[c * DEPTHS + depth] = jnp.where(inside, out, 0.0)
    m = [jnp.zeros((8, 128), f32) for _ in range(4)]
    for depth in range(2, DEPTHS - 2):
        e = x[3 * DEPTHS + depth, 0:8, 0:128]
        d = diag[depth]
        for c in range(3):
            p = c * DEPTHS + depth
            s = stencil(w[p - 1], w[p], w[p + 1])[0:8, 0:128]
            v = x[p, 0:8, 0:128]
            q = w[p, 0:8, 0:128]
            image_ref[c, depth - 2] = q
            m[0] = m[0] + v * v
            m[1] = m[1] + v * q
            m[2] = m[2] + q * q
            m[3] = m[3] + q * (q * d - 2.0 * (e * s))
    total = jnp.zeros((8, 128), f32)
    for k in range(4):
        total = jnp.where(lane == k, jnp.sum(m[k]), total)
    for i in range(sums_ref.shape[0] // 8):
        sums_ref[8 * i : 8 * i + 8, :] = total
    p = 2 * DEPTHS + DEPTHS - 3
    top_ref[0] = x[p, 0:8, 0:128]
    top_ref[1] = w[p, 0:8, 0:128]


def diffuse(height_ref, conduct_ref, before_ref, after_ref, out_ref):
    def extended(source, base):
        def joined(ref):
            return jnp.concatenate([ref[base : base + 8, :], ref[base + 8 : base + 16, :]], axis=1)

        return jnp.concatenate([source[...], joined(after_ref), joined(before_ref)], axis=0)

    h = extended(height_ref, SURFACE_ROW)
    k = extended(conduct_ref, SURFACE_ROW + 16)
    inside = k > 0.0
    along = 0.5 * (k + rolled(k, 255, 1))
    across = 0.5 * (k + rolled(k, 79, 0))
    for step in range(STEPS):
        s = rolled(h, 255, 1) - h
        q = along * s * lax.rsqrt(1.0 + s * s)
        t = rolled(h, 79, 0) - h
        r = across * t * lax.rsqrt(1.0 + t * t)
        change = (q - rolled(q, 1, 1)) + (r - rolled(r, 1, 0))
        h = jnp.where(inside, h + TIME_STEP * change, 0.0)
    out_ref[...] = h[0:64, 0:128]


def middle(sums_ref, top_ref, out_ref):
    lane = lanes((8, 128))
    part = jnp.sum(sums_ref[...], axis=0, keepdims=True)
    base = jnp.broadcast_to(rolled(part, 32), (8, 128))
    base = jnp.where((lane >= 32) & (lane < 36), base, 0.0)
    for j in range(out_ref.shape[0]):
        piece = jnp.where(lane < 16, rolled(top_ref[0], -16 * j), base)
        out_ref[j] = jnp.where(lane // 16 == 1, rolled(top_ref[1], 16 - 16 * j), piece)


def finish(parts_ref, planes_ref, image_ref, height_ref, velocity_ref, surface_ref):
    count = parts_ref.shape[0]
    lane = lanes((1, 128))
    total = parts_ref[0, 0:1, :]
    for j in range(1, count):
        total = total + parts_ref[j, 0:1, :]

    def moment(k):
        return jnp.sum(jnp.where(lane == 32 + k, total, 0.0), axis=1, keepdims=True)

    m0, m1, m2, m3 = (moment(k) for k in range(4))
    first = m0 / m1
    later = first * first * m2 - m0
    gain = 1.0 + later / m0
    second = later / (gain * gain * m1 - 2.0 * first * gain * m2 + first * first * m3)
    on_force = first + second * gain
    on_image = -(second * first)
    for c in range(3):
        for depth in range(8):
            velocity_ref[c, depth] = on_force * planes_ref[c * DEPTHS + depth + 2] + on_image * image_ref[c, depth]
    top = parts_ref[count - 1]
    rise = on_force * top + on_image * rolled(top, -16)
    spread = (
        lax.broadcasted_iota(jnp.int32, (128, 128), 1) // 8 == lax.broadcasted_iota(jnp.int32, (128, 128), 0)
    ).astype(f32)
    rise = jnp.where(lanes((8, 128)) < 16, rise, 0.0)
    wide = (STEPS * TIME_STEP) * jnp.dot(rise, spread, precision=lax.Precision.HIGHEST, preferred_element_type=f32)
    for r in range(8):
        rows = slice(8 * r, 8 * r + 8)
        surface_ref[rows, :] = height_ref[rows, :] + jnp.broadcast_to(wide[r : r + 1, :], (8, 128))


def shift(value, axis):
    ends = lax.axis_size(axis) - 1
    return value, [(i, i + 1) for i in range(ends)], [(i + 1, i) for i in range(ends)]


def exchange(to_next, to_before, axis):
    ends = lax.axis_size(axis) - 1
    from_before = lax.ppermute(to_next, axis, [(i, i + 1) for i in range(ends)])
    from_after = lax.ppermute(to_before, axis, [(i + 1, i) for i in range(ends)])
    return from_before, from_after


def local(body_force, viscosity, topography, kappa):
    depth = viscosity.shape[0]

    def layers(start):
        fields = [body_force[c, start : start + 2] for c in range(3)] + [viscosity[start : start + 2]]
        return jnp.concatenate(fields, axis=0)

    low, high = exchange(layers(depth - 2), layers(0), "gz")
    load, height, conduct, left, right = call(
        surface_own,
        [(8, 128), (64, 256), (64, 256), (8, 128), (8, 128)],
        (topography, kappa),
    )
    planes, left, right = call(
        assemble,
        [(PLANES, 8, 128), (2, 8, 128), (2, 8, 128)],
        (body_force, viscosity, load, low, high, left, right),
    )
    from_left, from_right = exchange(right, left, "gy")
    down, up, height, conduct = call(
        prepare_rows,
        [(GX_ROWS, 128), (GX_ROWS, 128), (64, 256), (64, 256)],
        (planes, from_left, from_right, height, conduct),
    )
    before, after = exchange(down, up, "gx")
    group = lax.axis_size("gx") * lax.axis_size("gy")
    image, sums, top = call(
        operate,
        [(3, 8, 8, 128), (group, 128), (2, 8, 128)],
        (planes, from_left, from_right, before, after),
        [
            pltpu.VMEM((PLANES, 16, 256), f32),
            pltpu.VMEM((3 * DEPTHS, 16, 256), f32),
            pltpu.VMEM((DEPTHS, 8, 128), f32),
        ],
    )
    sums = lax.all_to_all(sums.reshape(group, 1, 128), ("gx", "gy"), 0, 0)
    (height,) = call(diffuse, [(64, 128)], (height, conduct, before, after))
    (parts,) = call(middle, [(lax.axis_size("gz"), 8, 128)], (sums.reshape(group, 128), top))
    parts = lax.all_to_all(parts, "gz", 0, 0)
    velocity, surface = call(
        finish, [(3, 8, 8, 128), (64, 128)], (parts, planes, image, height)
    )
    return velocity, surface


def solution(mesh):
    in_specs = (P(None, "gz", "gx", "gy"), P("gz", "gx", "gy"), P("gx", "gy"), P("gx", "gy"))
    out_specs = (P(None, "gz", "gx", "gy"), P("gx", ("gy", "gz")))
    return jax.shard_map(local, mesh=mesh, in_specs=in_specs, out_specs=out_specs, check_vma=False)
```

```python
import jax
import jax.numpy as jnp
from jax import lax
from jax.experimental import pallas as pl
from jax.experimental.pallas import tpu as pltpu
from jax.sharding import PartitionSpec as P

STEPS = 8
DRAG = 1.0
TIME_STEP = 1.0
LOAD_GAIN = 4.0
FACE, EDGE, CORNER = 0.5, 0.25, 0.5 / 3.0
TOTAL = 6 * FACE + 12 * EDGE + 8 * CORNER

DEPTHS = 12
PLANES = 4 * DEPTHS
PAIRS_ROW = 2 * PLANES
SURFACE_ROW = PAIRS_ROW + 8
GX_ROWS = SURFACE_ROW + 32

f32 = jnp.float32


def vmem():
    return pl.BlockSpec(memory_space=pltpu.VMEM)


def call(body, outs, ins, scratch=(), cost=20000, limit=8 << 20):
    return pl.pallas_call(
        body,
        out_shape=[jax.ShapeDtypeStruct(s, f32) for s in outs],
        in_specs=[vmem() for _ in ins],
        out_specs=[vmem() for _ in outs],
        scratch_shapes=list(scratch),
        compiler_params=pltpu.CompilerParams(vmem_limit_bytes=limit),
        cost_estimate=pl.CostEstimate(flops=cost * 1024, bytes_accessed=1 << 18, transcendentals=0),
    )(*ins)


def lanes(shape):
    return lax.broadcasted_iota(jnp.int32, shape, len(shape) - 1)


def rolled(x, amount, axis=1):
    amount = amount % x.shape[axis]
    return x if amount == 0 else pltpu.roll(x, amount, axis)


def surface_own(topo_ref, kappa_ref, load_ref, height_ref, conduct_ref, left_ref, right_ref):
    g = lax.axis_index("gz")
    last = lax.axis_size("gz") - 1
    lane = lanes((8, 128))
    pieces = []
    for v in range(8):
        piece = topo_ref[:, 128 * v : 128 * v + 128].reshape(8, 8, 128)
        pieces.append(jnp.sum(piece, axis=1))
    stacked = jnp.concatenate(pieces, axis=0)
    pick = (
        lax.broadcasted_iota(jnp.int32, (128, 128), 0) // 8 == lax.broadcasted_iota(jnp.int32, (128, 128), 1)
    ).astype(f32)
    sums = jnp.dot(stacked, pick, precision=lax.Precision.HIGHEST, preferred_element_type=f32)
    load = jnp.zeros((8, 128), f32)
    for v in range(8):
        load = load + rolled(sums[8 * v : 8 * v + 8], 16 * v)
    load_ref[...] = jnp.where(g == last, load * (-LOAD_GAIN / 64.0), 0.0)
    wide = lanes((64, 128))
    own = pl.ds(pl.multiple_of(g * 128, 128), 128)
    before = pl.ds(pl.multiple_of(jnp.maximum(g - 1, 0) * 128, 128), 128)
    after = pl.ds(pl.multiple_of(jnp.minimum(g + 1, last) * 128, 128), 128)
    for source, target in ((topo_ref, height_ref), (kappa_ref, conduct_ref)):
        target[:, 0:128] = source[:, own].astype(f32)
        side = jnp.where((wide < 8) & (g < last), source[:, after].astype(f32), 0.0)
        side = jnp.where((wide >= 120) & (g > 0), source[:, before].astype(f32), side)
        target[:, 128:256] = side
    width = topo_ref.shape[1]
    left = jnp.zeros((8, 128), f32)
    right = jnp.zeros((8, 128), f32)
    slot = 0
    for source in (topo_ref, kappa_ref):
        head = source[:, 0:128].astype(f32)
        tail = source[:, width - 128 : width].astype(f32)
        for r in range(8):
            mask = lane // 8 == slot
            left = jnp.where(mask, rolled(head[8 * r : 8 * r + 8], 8 * slot), left)
            right = jnp.where(mask, rolled(tail[8 * r : 8 * r + 8], 8 * slot - 120), right)
            slot += 1
    left_ref[...] = left
    right_ref[...] = right


def assemble(force_ref, visc_ref, load_ref, low_ref, high_ref, sl_ref, sr_ref, planes_ref, left_ref, right_ref):
    lane = lanes((8, 128))
    left = jnp.zeros((8, 128), f32)
    right = jnp.zeros((8, 128), f32)
    for field in range(4):
        for depth in range(DEPTHS):
            if depth < 2:
                plane = low_ref[2 * field + depth]
            elif depth >= DEPTHS - 2:
                plane = high_ref[2 * field + depth - (DEPTHS - 2)]
            elif field == 3:
                plane = visc_ref[depth - 2]
            else:
                plane = force_ref[field, depth - 2]
                if field == 2 and depth == DEPTHS - 3:
                    plane = plane + load_ref[...]
            p = field * DEPTHS + depth
            planes_ref[p] = plane
            mask = lane // 2 == p
            left = jnp.where(mask, rolled(plane, 2 * p), left)
            right = jnp.where(mask, rolled(plane, 2 * p - 126), right)
    left_ref[0] = left
    right_ref[0] = right
    left_ref[1] = sl_ref[...]
    right_ref[1] = sr_ref[...]


def prepare_rows(planes_ref, rl_ref, rr_ref, height_ref, conduct_ref, down_ref, up_ref, height_out, conduct_out):
    g = lax.axis_index("gz")
    last = lax.axis_size("gz") - 1
    lane = lanes((8, 128))
    for p in range(PLANES):
        down_ref[2 * p : 2 * p + 2, :] = planes_ref[p, 6:8, :]
        up_ref[2 * p : 2 * p + 2, :] = planes_ref[p, 0:2, :]
    down_ref[PAIRS_ROW : PAIRS_ROW + 4, :] = jnp.concatenate([rl_ref[0, 6:8, :], rr_ref[0, 6:8, :]], axis=0)
    up_ref[PAIRS_ROW : PAIRS_ROW + 4, :] = jnp.concatenate([rl_ref[0, 0:2, :], rr_ref[0, 0:2, :]], axis=0)
    down_ref[PAIRS_ROW + 4 : SURFACE_ROW, :] = jnp.zeros((4, 128), f32)
    up_ref[PAIRS_ROW + 4 : SURFACE_ROW, :] = jnp.zeros((4, 128), f32)
    slot = 0
    for index, (source, target) in enumerate(((height_ref, height_out), (conduct_ref, conduct_out))):
        base = SURFACE_ROW + 16 * index
        for r in range(8):
            rows = slice(8 * r, 8 * r + 8)
            main = source[rows, 0:128]
            side = source[rows, 128:256]
            side = jnp.where((g == 0) & (lane >= 120), rolled(rl_ref[1], 120 - 8 * slot), side)
            side = jnp.where((g == last) & (lane < 8), rolled(rr_ref[1], -8 * slot), side)
            target[rows, 0:128] = main
            target[rows, 128:256] = side
            if r == 0:
                up_ref[base : base + 8, :] = main
                up_ref[base + 8 : base + 16, :] = side
            if r == 7:
                down_ref[base : base + 8, :] = main
                down_ref[base + 8 : base + 16, :] = side
            slot += 1


def stencil(before, here, after):
    outer = before + after
    a = FACE * here + EDGE * outer
    b = EDGE * here + CORNER * outer
    both = a + rolled(b, 1, 0) + rolled(b, 15, 0)
    rows = rolled(a, 1, 0) + rolled(a, 15, 0)
    return FACE * outer + rows + rolled(both, 1, 1) + rolled(both, 255, 1)


def operate(planes_ref, rl_ref, rr_ref, before_ref, after_ref, image_ref, sums_ref, top_ref, x, w, diag):
    lane = lanes((8, 128))
    row = lax.broadcasted_iota(jnp.int32, (8, 128), 0)
    pad = jnp.zeros((4, 128), f32)
    lower_l = jnp.concatenate([after_ref[PAIRS_ROW : PAIRS_ROW + 2, :], pad, before_ref[PAIRS_ROW : PAIRS_ROW + 2, :]], 0)
    lower_r = jnp.concatenate(
        [after_ref[PAIRS_ROW + 2 : PAIRS_ROW + 4, :], pad, before_ref[PAIRS_ROW + 2 : PAIRS_ROW + 4, :]], 0
    )
    for p in range(PLANES):
        x[p, 0:8, 0:128] = planes_ref[p]
        x[p, 8:16, 0:128] = jnp.concatenate(
            [after_ref[2 * p : 2 * p + 2, :], pad, before_ref[2 * p : 2 * p + 2, :]], 0
        )
        for start, l, r in ((0, rl_ref[0], rr_ref[0]), (8, lower_l, lower_r)):
            side = jnp.where(lane < 2, rolled(r, -2 * p), 0.0)
            side = jnp.where(lane >= 126, rolled(l, 126 - 2 * p), side)
            x[p, start : start + 8, 128:256] = side
    for depth in range(1, DEPTHS - 1):
        e = [x[3 * DEPTHS + depth + i] for i in (-1, 0, 1)]
        d = (DRAG + TOTAL * e[1]) + stencil(*e)
        diag[depth] = d[0:8, 0:128]
        inside = e[1] > 0.0
        for c in range(3):
            v = [x[c * DEPTHS + depth + i] for i in (-1, 0, 1)]
            ev = [e[i] * v[i] for i in range(3)]
            out = v[1] * d - e[1] * stencil(*v) - stencil(*ev)
            w[c * DEPTHS + depth] = jnp.where(inside, out, 0.0)
    m = [jnp.zeros((8, 128), f32) for _ in range(4)]
    for depth in range(2, DEPTHS - 2):
        e = x[3 * DEPTHS + depth, 0:8, 0:128]
        d = diag[depth]
        for c in range(3):
            p = c * DEPTHS + depth
            s = stencil(w[p - 1], w[p], w[p + 1])[0:8, 0:128]
            v = x[p, 0:8, 0:128]
            q = w[p, 0:8, 0:128]
            image_ref[c, depth - 2] = q
            m[0] = m[0] + v * v
            m[1] = m[1] + v * q
            m[2] = m[2] + q * q
            m[3] = m[3] + q * (q * d - 2.0 * (e * s))
    total = jnp.zeros((8, 128), f32)
    for k in range(4):
        total = jnp.where(lane == k, jnp.sum(m[k]), total)
    for i in range(sums_ref.shape[0] // 8):
        sums_ref[8 * i : 8 * i + 8, :] = total
    p = 2 * DEPTHS + DEPTHS - 3
    top_ref[0] = x[p, 0:8, 0:128]
    top_ref[1] = w[p, 0:8, 0:128]


def diffuse(height_ref, conduct_ref, before_ref, after_ref, out_ref):
    def extended(source, base):
        def joined(ref):
            return jnp.concatenate([ref[base : base + 8, :], ref[base + 8 : base + 16, :]], axis=1)

        return jnp.concatenate([source[...], joined(after_ref), joined(before_ref)], axis=0)

    h = extended(height_ref, SURFACE_ROW)
    k = extended(conduct_ref, SURFACE_ROW + 16)
    inside = k > 0.0
    along = 0.5 * (k + rolled(k, 255, 1))
    across = 0.5 * (k + rolled(k, 79, 0))
    for step in range(STEPS):
        s = rolled(h, 255, 1) - h
        q = along * s * lax.rsqrt(1.0 + s * s)
        t = rolled(h, 79, 0) - h
        r = across * t * lax.rsqrt(1.0 + t * t)
        change = (q - rolled(q, 1, 1)) + (r - rolled(r, 1, 0))
        h = jnp.where(inside, h + TIME_STEP * change, 0.0)
    out_ref[...] = h[0:64, 0:128]


def middle(sums_ref, top_ref, out_ref):
    lane = lanes((8, 128))
    part = jnp.sum(sums_ref[...], axis=0, keepdims=True)
    base = jnp.broadcast_to(rolled(part, 32), (8, 128))
    base = jnp.where((lane >= 32) & (lane < 36), base, 0.0)
    for j in range(out_ref.shape[0]):
        piece = jnp.where(lane < 16, rolled(top_ref[0], -16 * j), base)
        out_ref[j] = jnp.where(lane // 16 == 1, rolled(top_ref[1], 16 - 16 * j), piece)


def finish(parts_ref, planes_ref, image_ref, height_ref, velocity_ref, surface_ref):
    count = parts_ref.shape[0]
    lane = lanes((1, 128))
    total = parts_ref[0, 0:1, :]
    for j in range(1, count):
        total = total + parts_ref[j, 0:1, :]

    def moment(k):
        return jnp.sum(jnp.where(lane == 32 + k, total, 0.0), axis=1, keepdims=True)

    m0, m1, m2, m3 = (moment(k) for k in range(4))
    first = m0 / m1
    later = first * first * m2 - m0
    gain = 1.0 + later / m0
    second = later / (gain * gain * m1 - 2.0 * first * gain * m2 + first * first * m3)
    on_force = first + second * gain
    on_image = -(second * first)
    for c in range(3):
        for depth in range(8):
            velocity_ref[c, depth] = on_force * planes_ref[c * DEPTHS + depth + 2] + on_image * image_ref[c, depth]
    top = parts_ref[count - 1]
    rise = on_force * top + on_image * rolled(top, -16)
    spread = (
        lax.broadcasted_iota(jnp.int32, (128, 128), 1) // 8 == lax.broadcasted_iota(jnp.int32, (128, 128), 0)
    ).astype(f32)
    rise = jnp.where(lanes((8, 128)) < 16, rise, 0.0)
    wide = (STEPS * TIME_STEP) * jnp.dot(rise, spread, precision=lax.Precision.HIGHEST, preferred_element_type=f32)
    for r in range(8):
        rows = slice(8 * r, 8 * r + 8)
        surface_ref[rows, :] = height_ref[rows, :] + jnp.broadcast_to(wide[r : r + 1, :], (8, 128))


def shift(value, axis):
    ends = lax.axis_size(axis) - 1
    return value, [(i, i + 1) for i in range(ends)], [(i + 1, i) for i in range(ends)]


def exchange(to_next, to_before, axis):
    ends = lax.axis_size(axis) - 1
    from_before = lax.ppermute(to_next, axis, [(i, i + 1) for i in range(ends)])
    from_after = lax.ppermute(to_before, axis, [(i + 1, i) for i in range(ends)])
    return from_before, from_after


def local(body_force, viscosity, topography, kappa):
    depth = viscosity.shape[0]

    def layers(start):
        fields = [body_force[c, start : start + 2] for c in range(3)] + [viscosity[start : start + 2]]
        return jnp.concatenate(fields, axis=0)

    low, high = exchange(layers(depth - 2), layers(0), "gz")
    load, height, conduct, left, right = call(
        surface_own,
        [(8, 128), (64, 256), (64, 256), (8, 128), (8, 128)],
        (topography, kappa),
    )
    planes, left, right = call(
        assemble,
        [(PLANES, 8, 128), (2, 8, 128), (2, 8, 128)],
        (body_force, viscosity, load, low, high, left, right),
    )
    from_left, from_right = exchange(right, left, "gy")
    down, up, height, conduct = call(
        prepare_rows,
        [(GX_ROWS, 128), (GX_ROWS, 128), (64, 256), (64, 256)],
        (planes, from_left, from_right, height, conduct),
    )
    before, after = exchange(down, up, "gx")
    group = lax.axis_size("gx") * lax.axis_size("gy")
    image, sums, top = call(
        operate,
        [(3, 8, 8, 128), (group, 128), (2, 8, 128)],
        (planes, from_left, from_right, before, after),
        [
            pltpu.VMEM((PLANES, 16, 256), f32),
            pltpu.VMEM((3 * DEPTHS, 16, 256), f32),
            pltpu.VMEM((DEPTHS, 8, 128), f32),
        ],
    )
    sums = lax.all_to_all(sums.reshape(group, 1, 128), ("gx", "gy"), 0, 0)
    (height,) = call(diffuse, [(64, 128)], (height, conduct, before, after))
    (parts,) = call(middle, [(lax.axis_size("gz"), 8, 128)], (sums.reshape(group, 128), top))
    parts = lax.all_to_all(parts, "gz", 0, 0)
    velocity, surface = call(
        finish, [(3, 8, 8, 128), (64, 128)], (parts, planes, image, height)
    )
    return velocity, surface


def solution(mesh):
    in_specs = (P(None, "gz", "gx", "gy"), P("gz", "gx", "gy"), P("gx", "gy"), P("gx", "gy"))
    out_specs = (P(None, "gz", "gx", "gy"), P("gx", ("gy", "gz")))
    return jax.shard_map(local, mesh=mesh, in_specs=in_specs, out_specs=out_specs, check_vma=False)
```

```python
import jax
import jax.numpy as jnp
from jax import lax
from jax.experimental import pallas as pl
from jax.experimental.pallas import tpu as pltpu
from jax.sharding import PartitionSpec as P

STEPS = 8
DRAG = 1.0
TIME_STEP = 1.0
LOAD_GAIN = 4.0
FACE, EDGE, CORNER = 0.5, 0.25, 0.5 / 3.0
TOTAL = 6 * FACE + 12 * EDGE + 8 * CORNER

DEPTHS = 12
PLANES = 4 * DEPTHS
PAIRS_ROW = 2 * PLANES
SURFACE_ROW = PAIRS_ROW + 8
GX_ROWS = SURFACE_ROW + 32

f32 = jnp.float32


def vmem():
    return pl.BlockSpec(memory_space=pltpu.VMEM)


def call(body, outs, ins, scratch=(), cost=20000, limit=8 << 20):
    return pl.pallas_call(
        body,
        out_shape=[jax.ShapeDtypeStruct(s, f32) for s in outs],
        in_specs=[vmem() for _ in ins],
        out_specs=[vmem() for _ in outs],
        scratch_shapes=list(scratch),
        compiler_params=pltpu.CompilerParams(vmem_limit_bytes=limit),
        cost_estimate=pl.CostEstimate(flops=cost * 1024, bytes_accessed=1 << 18, transcendentals=0),
    )(*ins)


def lanes(shape):
    return lax.broadcasted_iota(jnp.int32, shape, len(shape) - 1)


def rolled(x, amount, axis=1):
    amount = amount % x.shape[axis]
    return x if amount == 0 else pltpu.roll(x, amount, axis)


def surface_own(topo_ref, kappa_ref, load_ref, height_ref, conduct_ref, left_ref, right_ref):
    g = lax.axis_index("gz")
    last = lax.axis_size("gz") - 1
    lane = lanes((8, 128))
    pieces = []
    for v in range(8):
        piece = topo_ref[:, 128 * v : 128 * v + 128].reshape(8, 8, 128)
        pieces.append(jnp.sum(piece, axis=1))
    stacked = jnp.concatenate(pieces, axis=0)
    pick = (
        lax.broadcasted_iota(jnp.int32, (128, 128), 0) // 8 == lax.broadcasted_iota(jnp.int32, (128, 128), 1)
    ).astype(f32)
    sums = jnp.dot(stacked, pick, precision=lax.Precision.HIGHEST, preferred_element_type=f32)
    load = jnp.zeros((8, 128), f32)
    for v in range(8):
        load = load + rolled(sums[8 * v : 8 * v + 8], 16 * v)
    load_ref[...] = jnp.where(g == last, load * (-LOAD_GAIN / 64.0), 0.0)
    wide = lanes((64, 128))
    own = pl.ds(pl.multiple_of(g * 128, 128), 128)
    before = pl.ds(pl.multiple_of(jnp.maximum(g - 1, 0) * 128, 128), 128)
    after = pl.ds(pl.multiple_of(jnp.minimum(g + 1, last) * 128, 128), 128)
    for source, target in ((topo_ref, height_ref), (kappa_ref, conduct_ref)):
        target[:, 0:128] = source[:, own].astype(f32)
        side = jnp.where((wide < 8) & (g < last), source[:, after].astype(f32), 0.0)
        side = jnp.where((wide >= 120) & (g > 0), source[:, before].astype(f32), side)
        target[:, 128:256] = side
    width = topo_ref.shape[1]
    left = jnp.zeros((8, 128), f32)
    right = jnp.zeros((8, 128), f32)
    slot = 0
    for source in (topo_ref, kappa_ref):
        head = source[:, 0:128].astype(f32)
        tail = source[:, width - 128 : width].astype(f32)
        for r in range(8):
            mask = lane // 8 == slot
            left = jnp.where(mask, rolled(head[8 * r : 8 * r + 8], 8 * slot), left)
            right = jnp.where(mask, rolled(tail[8 * r : 8 * r + 8], 8 * slot - 120), right)
            slot += 1
    left_ref[...] = left
    right_ref[...] = right


def is_even(axis):
    return lax.rem(lax.axis_index(axis), 2) == 0


def fetch(force_ref, visc_ref, topo_ref, kappa_ref, odd_ref, even_ref, force_out, visc_out, topo_out, kappa_out, sems):
    depth = visc_ref.shape[0]
    start = jnp.where(is_even("gz"), 0, depth - 2)
    moves = []
    for target, first in ((odd_ref, start), (even_ref, depth - 2 - start)):
        moves.append((force_ref.at[:, pl.ds(first, 2)], target.at[0:3]))
        moves.append((visc_ref.at[pl.ds(first, 2)], target.at[3]))
    moves += [(force_ref, force_out), (visc_ref, visc_out), (topo_ref, topo_out), (kappa_ref, kappa_out)]
    copies = [pltpu.make_async_copy(source, target, sems.at[i]) for i, (source, target) in enumerate(moves)]
    for copy in copies:
        copy.start()
    for copy in copies:
        copy.wait()


def assemble(force_ref, visc_ref, load_ref, odd_ref, even_ref, sl_ref, sr_ref, planes_ref, odd_out, even_out):
    upward = is_even("gz")
    lane = lanes((8, 128))
    left = jnp.zeros((8, 128), f32)
    right = jnp.zeros((8, 128), f32)
    for field in range(4):
        for depth in range(DEPTHS):
            if depth < 2:
                plane = jnp.where(upward, odd_ref[field, depth], even_ref[field, depth])
            elif depth >= DEPTHS - 2:
                i = depth - (DEPTHS - 2)
                plane = jnp.where(upward, even_ref[field, i], odd_ref[field, i])
            elif field == 3:
                plane = visc_ref[depth - 2]
            else:
                plane = force_ref[field, depth - 2]
                if field == 2 and depth == DEPTHS - 3:
                    plane = plane + load_ref[...]
            p = field * DEPTHS + depth
            planes_ref[p] = plane
            mask = lane // 2 == p
            left = jnp.where(mask, rolled(plane, 2 * p), left)
            right = jnp.where(mask, rolled(plane, 2 * p - 126), right)
    rightward = is_even("gy")
    odd_out[0] = jnp.where(rightward, left, right)
    even_out[0] = jnp.where(rightward, right, left)
    odd_out[1] = jnp.where(rightward, sl_ref[...], sr_ref[...])
    even_out[1] = jnp.where(rightward, sr_ref[...], sl_ref[...])


def prepare_rows(planes_ref, odd_ref, even_ref, height_ref, conduct_ref, odd_out, even_out, rl_ref, rr_ref, height_out, conduct_out):
    rightward = is_even("gy")
    for i in range(2):
        rl_ref[i] = jnp.where(rightward, odd_ref[i], even_ref[i])
        rr_ref[i] = jnp.where(rightward, even_ref[i], odd_ref[i])
    downward = is_even("gx")

    def send(rows, low, high):
        odd_out[rows, :] = jnp.where(downward, low, high)
        even_out[rows, :] = jnp.where(downward, high, low)

    g = lax.axis_index("gz")
    last = lax.axis_size("gz") - 1
    lane = lanes((8, 128))
    for p in range(PLANES):
        send(slice(2 * p, 2 * p + 2), planes_ref[p, 0:2, :], planes_ref[p, 6:8, :])
    pad = jnp.zeros((4, 128), f32)
    send(
        slice(PAIRS_ROW, SURFACE_ROW),
        jnp.concatenate([rl_ref[0, 0:2, :], rr_ref[0, 0:2, :], pad], axis=0),
        jnp.concatenate([rl_ref[0, 6:8, :], rr_ref[0, 6:8, :], pad], axis=0),
    )
    slot = 0
    for index, (source, target) in enumerate(((height_ref, height_out), (conduct_ref, conduct_out))):
        base = SURFACE_ROW + 16 * index
        for r in range(8):
            rows = slice(8 * r, 8 * r + 8)
            main = source[rows, 0:128]
            side = source[rows, 128:256]
            side = jnp.where((g == 0) & (lane >= 120), rolled(rl_ref[1], 120 - 8 * slot), side)
            side = jnp.where((g == last) & (lane < 8), rolled(rr_ref[1], -8 * slot), side)
            target[rows, 0:128] = main
            target[rows, 128:256] = side
            if r == 0:
                first = (main, side)
            if r == 7:
                send(slice(base, base + 8), first[0], main)
                send(slice(base + 8, base + 16), first[1], side)
            slot += 1


def stencil(before, here, after):
    outer = before + after
    a = FACE * here + EDGE * outer
    b = EDGE * here + CORNER * outer
    both = a + rolled(b, 1, 0) + rolled(b, 15, 0)
    rows = rolled(a, 1, 0) + rolled(a, 15, 0)
    return FACE * outer + rows + rolled(both, 1, 1) + rolled(both, 255, 1)


def sided(odd_ref, even_ref, axis):
    first = is_even(axis)

    def before(rows):
        return jnp.where(first, odd_ref[rows, :], even_ref[rows, :])

    def after(rows):
        return jnp.where(first, even_ref[rows, :], odd_ref[rows, :])

    return before, after


def operate(planes_ref, rl_ref, rr_ref, odd_ref, even_ref, image_ref, sums_ref, top_ref, x, w, diag):
    lane = lanes((8, 128))
    row = lax.broadcasted_iota(jnp.int32, (8, 128), 0)
    pad = jnp.zeros((4, 128), f32)
    before, after = sided(odd_ref, even_ref, "gx")

    def around(start):
        rows = slice(start, start + 2)
        return jnp.concatenate([after(rows), pad, before(rows)], axis=0)

    lower_l = around(PAIRS_ROW)
    lower_r = around(PAIRS_ROW + 2)
    for p in range(PLANES):
        x[p, 0:8, 0:128] = planes_ref[p]
        x[p, 8:16, 0:128] = around(2 * p)
        for start, l, r in ((0, rl_ref[0], rr_ref[0]), (8, lower_l, lower_r)):
            side = jnp.where(lane < 2, rolled(r, -2 * p), 0.0)
            side = jnp.where(lane >= 126, rolled(l, 126 - 2 * p), side)
            x[p, start : start + 8, 128:256] = side
    for depth in range(1, DEPTHS - 1):
        e = [x[3 * DEPTHS + depth + i] for i in (-1, 0, 1)]
        d = (DRAG + TOTAL * e[1]) + stencil(*e)
        diag[depth] = d[0:8, 0:128]
        inside = e[1] > 0.0
        for c in range(3):
            v = [x[c * DEPTHS + depth + i] for i in (-1, 0, 1)]
            ev = [e[i] * v[i] for i in range(3)]
            out = v[1] * d - e[1] * stencil(*v) - stencil(*ev)
            w[c * DEPTHS + depth] = jnp.where(inside, out, 0.0)
    m = [jnp.zeros((8, 128), f32) for _ in range(4)]
    for depth in range(2, DEPTHS - 2):
        e = x[3 * DEPTHS + depth, 0:8, 0:128]
        d = diag[depth]
        for c in range(3):
            p = c * DEPTHS + depth
            s = stencil(w[p - 1], w[p], w[p + 1])[0:8, 0:128]
            v = x[p, 0:8, 0:128]
            q = w[p, 0:8, 0:128]
            image_ref[c, depth - 2] = q
            m[0] = m[0] + v * v
            m[1] = m[1] + v * q
            m[2] = m[2] + q * q
            m[3] = m[3] + q * (q * d - 2.0 * (e * s))
    total = jnp.zeros((8, 128), f32)
    for k in range(4):
        total = jnp.where(lane == k, jnp.sum(m[k]), total)
    for i in range(sums_ref.shape[0] // 8):
        sums_ref[8 * i : 8 * i + 8, :] = total
    p = 2 * DEPTHS + DEPTHS - 3
    top_ref[0] = x[p, 0:8, 0:128]
    top_ref[1] = w[p, 0:8, 0:128]


def diffuse(height_ref, conduct_ref, odd_ref, even_ref, out_ref):
    before, after = sided(odd_ref, even_ref, "gx")

    def extended(source, base):
        def joined(side):
            return jnp.concatenate([side(slice(base, base + 8)), side(slice(base + 8, base + 16))], axis=1)

        return jnp.concatenate([source[...], joined(after), joined(before)], axis=0)

    h = extended(height_ref, SURFACE_ROW)
    k = extended(conduct_ref, SURFACE_ROW + 16)
    inside = k > 0.0
    along = 0.5 * (k + rolled(k, 255, 1))
    across = 0.5 * (k + rolled(k, 79, 0))
    for step in range(STEPS):
        s = rolled(h, 255, 1) - h
        q = along * s * lax.rsqrt(1.0 + s * s)
        t = rolled(h, 79, 0) - h
        r = across * t * lax.rsqrt(1.0 + t * t)
        change = (q - rolled(q, 1, 1)) + (r - rolled(r, 1, 0))
        h = jnp.where(inside, h + TIME_STEP * change, 0.0)
    out_ref[...] = h[0:64, 0:128]


def middle(sums_ref, top_ref, out_ref):
    lane = lanes((8, 128))
    part = jnp.sum(sums_ref[...], axis=0, keepdims=True)
    base = jnp.broadcast_to(rolled(part, 32), (8, 128))
    base = jnp.where((lane >= 32) & (lane < 36), base, 0.0)
    for j in range(out_ref.shape[0]):
        piece = jnp.where(lane < 16, rolled(top_ref[0], -16 * j), base)
        out_ref[j] = jnp.where(lane // 16 == 1, rolled(top_ref[1], 16 - 16 * j), piece)


def finish(parts_ref, planes_ref, image_ref, height_ref, velocity_ref, surface_ref):
    count = parts_ref.shape[0]
    lane = lanes((1, 128))
    total = parts_ref[0, 0:1, :]
    for j in range(1, count):
        total = total + parts_ref[j, 0:1, :]

    def moment(k):
        return jnp.sum(jnp.where(lane == 32 + k, total, 0.0), axis=1, keepdims=True)

    m0, m1, m2, m3 = (moment(k) for k in range(4))
    first = m0 / m1
    later = first * first * m2 - m0
    gain = 1.0 + later / m0
    second = later / (gain * gain * m1 - 2.0 * first * gain * m2 + first * first * m3)
    on_force = first + second * gain
    on_image = -(second * first)
    for c in range(3):
        for depth in range(8):
            velocity_ref[c, depth] = on_force * planes_ref[c * DEPTHS + depth + 2] + on_image * image_ref[c, depth]
    top = parts_ref[count - 1]
    rise = on_force * top + on_image * rolled(top, -16)
    spread = (
        lax.broadcasted_iota(jnp.int32, (128, 128), 1) // 8 == lax.broadcasted_iota(jnp.int32, (128, 128), 0)
    ).astype(f32)
    rise = jnp.where(lanes((8, 128)) < 16, rise, 0.0)
    wide = (STEPS * TIME_STEP) * jnp.dot(rise, spread, precision=lax.Precision.HIGHEST, preferred_element_type=f32)
    for r in range(8):
        rows = slice(8 * r, 8 * r + 8)
        surface_ref[rows, :] = height_ref[rows, :] + jnp.broadcast_to(wide[r : r + 1, :], (8, 128))


def swap(odd, even, axis):
    count = lax.axis_size(axis)

    def pairs(start):
        found = []
        for i in range(start, count - 1, 2):
            found += [(i, i + 1), (i + 1, i)]
        return found

    return lax.ppermute(odd, axis, pairs(1)), lax.ppermute(even, axis, pairs(0))


def local(body_force, viscosity, topography, kappa):
    inputs = (body_force, viscosity, topography, kappa)
    odd, even, body_force, viscosity, topography, kappa = pl.pallas_call(
        fetch,
        out_shape=[jax.ShapeDtypeStruct((4, 2, 8, 128), f32)] * 2
        + [jax.ShapeDtypeStruct(x.shape, x.dtype) for x in inputs],
        in_specs=[pl.BlockSpec(memory_space=pltpu.HBM)] * 4,
        out_specs=[vmem()] * 6,
        scratch_shapes=[pltpu.SemaphoreType.DMA((8,))],
        compiler_params=pltpu.CompilerParams(vmem_limit_bytes=4 << 20),
    )(*[pltpu.with_memory_space_constraint(x, pltpu.HBM) for x in inputs])
    odd, even = swap(odd, even, "gz")
    load, height, conduct, left, right = call(
        surface_own,
        [(8, 128), (64, 256), (64, 256), (8, 128), (8, 128)],
        (topography, kappa),
    )
    planes, odd, even = call(
        assemble,
        [(PLANES, 8, 128), (2, 8, 128), (2, 8, 128)],
        (body_force, viscosity, load, odd, even, left, right),
    )
    odd, even = swap(odd, even, "gy")
    odd, even, from_left, from_right, height, conduct = call(
        prepare_rows,
        [(GX_ROWS, 128), (GX_ROWS, 128), (2, 8, 128), (2, 8, 128), (64, 256), (64, 256)],
        (planes, odd, even, height, conduct),
    )
    odd, even = swap(odd, even, "gx")
    group = lax.axis_size("gx") * lax.axis_size("gy")
    image, sums, top = call(
        operate,
        [(3, 8, 8, 128), (group, 128), (2, 8, 128)],
        (planes, from_left, from_right, odd, even),
        [
            pltpu.VMEM((PLANES, 16, 256), f32),
            pltpu.VMEM((3 * DEPTHS, 16, 256), f32),
            pltpu.VMEM((DEPTHS, 8, 128), f32),
        ],
    )
    (height,) = call(diffuse, [(64, 128)], (height, conduct, odd, even))
    sums = lax.all_to_all(sums.reshape(group, 1, 128), ("gx", "gy"), 0, 0)
    sums, height = lax.optimization_barrier((sums, height))
    (parts,) = call(middle, [(lax.axis_size("gz"), 8, 128)], (sums.reshape(group, 128), top))
    parts = lax.all_to_all(parts, "gz", 0, 0)
    velocity, surface = call(
        finish, [(3, 8, 8, 128), (64, 128)], (parts, planes, image, height)
    )
    return velocity, surface


def solution(mesh):
    in_specs = (P(None, "gz", "gx", "gy"), P("gz", "gx", "gy"), P("gx", "gy"), P("gx", "gy"))
    out_specs = (P(None, "gz", "gx", "gy"), P("gx", ("gy", "gz")))
    return jax.shard_map(local, mesh=mesh, in_specs=in_specs, out_specs=out_specs, check_vma=False)
```

```python
import jax
import jax.numpy as jnp
from jax import lax
from jax.experimental import pallas as pl
from jax.experimental.pallas import tpu as pltpu
from jax.sharding import PartitionSpec as P

STEPS = 8
DRAG = 1.0
TIME_STEP = 1.0
LOAD_GAIN = 4.0
FACE, EDGE, CORNER = 0.5, 0.25, 0.5 / 3.0
TOTAL = 6 * FACE + 12 * EDGE + 8 * CORNER

DEPTHS = 12
PLANES = 4 * DEPTHS
PAIRS_ROW = 2 * PLANES
SURFACE_ROW = PAIRS_ROW + 8
GX_ROWS = SURFACE_ROW + 32

f32 = jnp.float32


def vmem():
    return pl.BlockSpec(memory_space=pltpu.VMEM)


def call(body, outs, ins, scratch=(), cost=20000, limit=8 << 20):
    return pl.pallas_call(
        body,
        out_shape=[jax.ShapeDtypeStruct(s, f32) for s in outs],
        in_specs=[vmem() for _ in ins],
        out_specs=[vmem() for _ in outs],
        scratch_shapes=list(scratch),
        compiler_params=pltpu.CompilerParams(vmem_limit_bytes=limit),
        cost_estimate=pl.CostEstimate(flops=cost * 1024, bytes_accessed=1 << 18, transcendentals=0),
    )(*ins)


def lanes(shape):
    return lax.broadcasted_iota(jnp.int32, shape, len(shape) - 1)


def rolled(x, amount, axis=1):
    amount = amount % x.shape[axis]
    return x if amount == 0 else pltpu.roll(x, amount, axis)


def surface_own(topo_ref, kappa_ref, load_ref, height_ref, conduct_ref, left_ref, right_ref):
    g = lax.axis_index("gz")
    last = lax.axis_size("gz") - 1
    lane = lanes((8, 128))
    pieces = []
    for v in range(8):
        piece = topo_ref[:, 128 * v : 128 * v + 128].reshape(8, 8, 128)
        pieces.append(jnp.sum(piece, axis=1))
    stacked = jnp.concatenate(pieces, axis=0)
    pick = (
        lax.broadcasted_iota(jnp.int32, (128, 128), 0) // 8 == lax.broadcasted_iota(jnp.int32, (128, 128), 1)
    ).astype(f32)
    sums = jnp.dot(stacked, pick, precision=lax.Precision.HIGHEST, preferred_element_type=f32)
    load = jnp.zeros((8, 128), f32)
    for v in range(8):
        load = load + rolled(sums[8 * v : 8 * v + 8], 16 * v)
    load_ref[...] = jnp.where(g == last, load * (-LOAD_GAIN / 64.0), 0.0)
    wide = lanes((64, 128))
    own = pl.ds(pl.multiple_of(g * 128, 128), 128)
    before = pl.ds(pl.multiple_of(jnp.maximum(g - 1, 0) * 128, 128), 128)
    after = pl.ds(pl.multiple_of(jnp.minimum(g + 1, last) * 128, 128), 128)
    for source, target in ((topo_ref, height_ref), (kappa_ref, conduct_ref)):
        target[:, 0:128] = source[:, own].astype(f32)
        side = jnp.where((wide < 8) & (g < last), source[:, after].astype(f32), 0.0)
        side = jnp.where((wide >= 120) & (g > 0), source[:, before].astype(f32), side)
        target[:, 128:256] = side
    width = topo_ref.shape[1]
    left = jnp.zeros((8, 128), f32)
    right = jnp.zeros((8, 128), f32)
    slot = 0
    for source in (topo_ref, kappa_ref):
        head = source[:, 0:128].astype(f32)
        tail = source[:, width - 128 : width].astype(f32)
        for r in range(8):
            mask = lane // 8 == slot
            left = jnp.where(mask, rolled(head[8 * r : 8 * r + 8], 8 * slot), left)
            right = jnp.where(mask, rolled(tail[8 * r : 8 * r + 8], 8 * slot - 120), right)
            slot += 1
    left_ref[...] = left
    right_ref[...] = right


def is_even(axis):
    return lax.rem(lax.axis_index(axis), 2) == 0


def fetch(force_ref, visc_ref, odd_ref, even_ref, sems):
    depth = visc_ref.shape[0]
    start = jnp.where(is_even("gz"), 0, depth - 2)
    moves = []
    for target, first in ((odd_ref, start), (even_ref, depth - 2 - start)):
        moves.append((force_ref.at[:, pl.ds(first, 2)], target.at[0:3]))
        moves.append((visc_ref.at[pl.ds(first, 2)], target.at[3]))
    copies = [pltpu.make_async_copy(source, target, sems.at[i]) for i, (source, target) in enumerate(moves)]
    for copy in copies:
        copy.start()
    for copy in copies:
        copy.wait()


def assemble(force_ref, visc_ref, load_ref, odd_ref, even_ref, sl_ref, sr_ref, planes_ref, odd_out, even_out):
    upward = is_even("gz")
    lane = lanes((8, 128))
    left = jnp.zeros((8, 128), f32)
    right = jnp.zeros((8, 128), f32)
    for field in range(4):
        for depth in range(DEPTHS):
            if depth < 2:
                plane = jnp.where(upward, odd_ref[field, depth], even_ref[field, depth])
            elif depth >= DEPTHS - 2:
                i = depth - (DEPTHS - 2)
                plane = jnp.where(upward, even_ref[field, i], odd_ref[field, i])
            elif field == 3:
                plane = visc_ref[depth - 2]
            else:
                plane = force_ref[field, depth - 2]
                if field == 2 and depth == DEPTHS - 3:
                    plane = plane + load_ref[...]
            p = field * DEPTHS + depth
            planes_ref[p] = plane
            mask = lane // 2 == p
            left = jnp.where(mask, rolled(plane, 2 * p), left)
            right = jnp.where(mask, rolled(plane, 2 * p - 126), right)
    rightward = is_even("gy")
    odd_out[0] = jnp.where(rightward, left, right)
    even_out[0] = jnp.where(rightward, right, left)
    odd_out[1] = jnp.where(rightward, sl_ref[...], sr_ref[...])
    even_out[1] = jnp.where(rightward, sr_ref[...], sl_ref[...])


def prepare_rows(planes_ref, odd_ref, even_ref, height_ref, conduct_ref, odd_out, even_out, rl_ref, rr_ref, height_out, conduct_out):
    rightward = is_even("gy")
    for i in range(2):
        rl_ref[i] = jnp.where(rightward, odd_ref[i], even_ref[i])
        rr_ref[i] = jnp.where(rightward, even_ref[i], odd_ref[i])
    downward = is_even("gx")

    def send(rows, low, high):
        odd_out[rows, :] = jnp.where(downward, low, high)
        even_out[rows, :] = jnp.where(downward, high, low)

    g = lax.axis_index("gz")
    last = lax.axis_size("gz") - 1
    lane = lanes((8, 128))
    for p in range(PLANES):
        send(slice(2 * p, 2 * p + 2), planes_ref[p, 0:2, :], planes_ref[p, 6:8, :])
    pad = jnp.zeros((4, 128), f32)
    send(
        slice(PAIRS_ROW, SURFACE_ROW),
        jnp.concatenate([rl_ref[0, 0:2, :], rr_ref[0, 0:2, :], pad], axis=0),
        jnp.concatenate([rl_ref[0, 6:8, :], rr_ref[0, 6:8, :], pad], axis=0),
    )
    slot = 0
    for index, (source, target) in enumerate(((height_ref, height_out), (conduct_ref, conduct_out))):
        base = SURFACE_ROW + 16 * index
        for r in range(8):
            rows = slice(8 * r, 8 * r + 8)
            main = source[rows, 0:128]
            side = source[rows, 128:256]
            side = jnp.where((g == 0) & (lane >= 120), rolled(rl_ref[1], 120 - 8 * slot), side)
            side = jnp.where((g == last) & (lane < 8), rolled(rr_ref[1], -8 * slot), side)
            target[rows, 0:128] = main
            target[rows, 128:256] = side
            if r == 0:
                first = (main, side)
            if r == 7:
                send(slice(base, base + 8), first[0], main)
                send(slice(base + 8, base + 16), first[1], side)
            slot += 1


def stencil(before, here, after):
    outer = before + after
    a = FACE * here + EDGE * outer
    b = EDGE * here + CORNER * outer
    both = a + rolled(b, 1, 0) + rolled(b, 15, 0)
    rows = rolled(a, 1, 0) + rolled(a, 15, 0)
    return FACE * outer + rows + rolled(both, 1, 1) + rolled(both, 255, 1)


def sided(odd_ref, even_ref, axis):
    first = is_even(axis)

    def before(rows):
        return jnp.where(first, odd_ref[rows, :], even_ref[rows, :])

    def after(rows):
        return jnp.where(first, even_ref[rows, :], odd_ref[rows, :])

    return before, after


def steps(h, k):
    rows = h.shape[0]
    inside = k > 0.0
    along = 0.5 * (k + rolled(k, 255, 1))
    across = 0.5 * (k + rolled(k, rows - 1, 0))
    for step in range(STEPS):
        s = rolled(h, 255, 1) - h
        q = along * s * lax.rsqrt(1.0 + s * s)
        t = rolled(h, rows - 1, 0) - h
        r = across * t * lax.rsqrt(1.0 + t * t)
        change = (q - rolled(q, 1, 1)) + (r - rolled(r, 1, 0))
        h = jnp.where(inside, h + TIME_STEP * change, 0.0)
    return h


def inner_rows(height_ref, conduct_ref, out_ref):
    out_ref[...] = steps(height_ref[...], conduct_ref[...])[8:56, 0:128]


def operate(
    planes_ref, rl_ref, rr_ref, odd_ref, even_ref, height_ref, conduct_ref, inner_ref, image_ref, sums_ref, top_ref, out_ref, x, w, diag
):
    lane = lanes((8, 128))
    row = lax.broadcasted_iota(jnp.int32, (8, 128), 0)
    pad = jnp.zeros((4, 128), f32)
    before, after = sided(odd_ref, even_ref, "gx")

    def around(start):
        rows = slice(start, start + 2)
        return jnp.concatenate([after(rows), pad, before(rows)], axis=0)

    def banded(source, base):
        def joined(side):
            return jnp.concatenate([side(slice(base, base + 8)), side(slice(base + 8, base + 16))], axis=1)

        return jnp.concatenate([source[48:64, :], joined(after), joined(before), source[0:16, :]], axis=0)

    band = steps(banded(height_ref, SURFACE_ROW), banded(conduct_ref, SURFACE_ROW + 16))
    out_ref[0:8, :] = band[32:40, 0:128]
    out_ref[8:56, :] = inner_ref[...]
    out_ref[56:64, :] = band[8:16, 0:128]
    lower_l = around(PAIRS_ROW)
    lower_r = around(PAIRS_ROW + 2)
    for p in range(PLANES):
        x[p, 0:8, 0:128] = planes_ref[p]
        x[p, 8:16, 0:128] = around(2 * p)
        for start, l, r in ((0, rl_ref[0], rr_ref[0]), (8, lower_l, lower_r)):
            side = jnp.where(lane < 2, rolled(r, -2 * p), 0.0)
            side = jnp.where(lane >= 126, rolled(l, 126 - 2 * p), side)
            x[p, start : start + 8, 128:256] = side
    for depth in range(1, DEPTHS - 1):
        e = [x[3 * DEPTHS + depth + i] for i in (-1, 0, 1)]
        d = (DRAG + TOTAL * e[1]) + stencil(*e)
        diag[depth] = d[0:8, 0:128]
        inside = e[1] > 0.0
        for c in range(3):
            v = [x[c * DEPTHS + depth + i] for i in (-1, 0, 1)]
            ev = [e[i] * v[i] for i in range(3)]
            out = v[1] * d - e[1] * stencil(*v) - stencil(*ev)
            w[c * DEPTHS + depth] = jnp.where(inside, out, 0.0)
    m = [jnp.zeros((8, 128), f32) for _ in range(4)]
    for depth in range(2, DEPTHS - 2):
        e = x[3 * DEPTHS + depth, 0:8, 0:128]
        d = diag[depth]
        for c in range(3):
            p = c * DEPTHS + depth
            s = stencil(w[p - 1], w[p], w[p + 1])[0:8, 0:128]
            v = x[p, 0:8, 0:128]
            q = w[p, 0:8, 0:128]
            image_ref[c, depth - 2] = q
            m[0] = m[0] + v * v
            m[1] = m[1] + v * q
            m[2] = m[2] + q * q
            m[3] = m[3] + q * (q * d - 2.0 * (e * s))
    total = jnp.zeros((8, 128), f32)
    for k in range(4):
        total = jnp.where(lane == k, jnp.sum(m[k]), total)
    for i in range(sums_ref.shape[0] // 8):
        sums_ref[8 * i : 8 * i + 8, :] = total
    p = 2 * DEPTHS + DEPTHS - 3
    top_ref[0] = x[p, 0:8, 0:128]
    top_ref[1] = w[p, 0:8, 0:128]


def middle(sums_ref, top_ref, out_ref):
    lane = lanes((8, 128))
    part = jnp.sum(sums_ref[...], axis=0, keepdims=True)
    base = jnp.broadcast_to(rolled(part, 32), (8, 128))
    base = jnp.where((lane >= 32) & (lane < 36), base, 0.0)
    for j in range(out_ref.shape[0]):
        piece = jnp.where(lane < 16, rolled(top_ref[0], -16 * j), base)
        out_ref[j] = jnp.where(lane // 16 == 1, rolled(top_ref[1], 16 - 16 * j), piece)


def finish(parts_ref, planes_ref, image_ref, height_ref, velocity_ref, surface_ref):
    count = parts_ref.shape[0]
    lane = lanes((1, 128))
    total = parts_ref[0, 0:1, :]
    for j in range(1, count):
        total = total + parts_ref[j, 0:1, :]

    def moment(k):
        return jnp.sum(jnp.where(lane == 32 + k, total, 0.0), axis=1, keepdims=True)

    m0, m1, m2, m3 = (moment(k) for k in range(4))
    first = m0 / m1
    later = first * first * m2 - m0
    gain = 1.0 + later / m0
    second = later / (gain * gain * m1 - 2.0 * first * gain * m2 + first * first * m3)
    on_force = first + second * gain
    on_image = -(second * first)
    for c in range(3):
        for depth in range(8):
            velocity_ref[c, depth] = on_force * planes_ref[c * DEPTHS + depth + 2] + on_image * image_ref[c, depth]
    top = parts_ref[count - 1]
    rise = on_force * top + on_image * rolled(top, -16)
    spread = (
        lax.broadcasted_iota(jnp.int32, (128, 128), 1) // 8 == lax.broadcasted_iota(jnp.int32, (128, 128), 0)
    ).astype(f32)
    rise = jnp.where(lanes((8, 128)) < 16, rise, 0.0)
    wide = (STEPS * TIME_STEP) * jnp.dot(rise, spread, precision=lax.Precision.HIGHEST, preferred_element_type=f32)
    for r in range(8):
        rows = slice(8 * r, 8 * r + 8)
        surface_ref[rows, :] = height_ref[rows, :] + jnp.broadcast_to(wide[r : r + 1, :], (8, 128))


def swap(odd, even, axis):
    count = lax.axis_size(axis)

    def pairs(start):
        found = []
        for i in range(start, count - 1, 2):
            found += [(i, i + 1), (i + 1, i)]
        return found

    return lax.ppermute(odd, axis, pairs(1)), lax.ppermute(even, axis, pairs(0))


def local(body_force, viscosity, topography, kappa):
    odd, even = pl.pallas_call(
        fetch,
        out_shape=[jax.ShapeDtypeStruct((4, 2, 8, 128), f32)] * 2,
        in_specs=[pl.BlockSpec(memory_space=pltpu.HBM)] * 2,
        out_specs=[vmem()] * 2,
        scratch_shapes=[pltpu.SemaphoreType.DMA((4,))],
        compiler_params=pltpu.CompilerParams(vmem_limit_bytes=1 << 20),
    )(*[pltpu.with_memory_space_constraint(x, pltpu.HBM) for x in (body_force, viscosity)])
    odd, even = swap(odd, even, "gz")
    load, height, conduct, left, right = call(
        surface_own,
        [(8, 128), (64, 256), (64, 256), (8, 128), (8, 128)],
        (topography, kappa),
    )
    planes, odd, even = call(
        assemble,
        [(PLANES, 8, 128), (2, 8, 128), (2, 8, 128)],
        (body_force, viscosity, load, odd, even, left, right),
    )
    odd, even = swap(odd, even, "gy")
    odd, even, from_left, from_right, height, conduct = call(
        prepare_rows,
        [(GX_ROWS, 128), (GX_ROWS, 128), (2, 8, 128), (2, 8, 128), (64, 256), (64, 256)],
        (planes, odd, even, height, conduct),
    )
    odd, even = swap(odd, even, "gx")
    group = lax.axis_size("gx") * lax.axis_size("gy")
    (inner,) = call(inner_rows, [(48, 128)], (height, conduct))
    image, sums, top, height = call(
        operate,
        [(3, 8, 8, 128), (group, 128), (2, 8, 128), (64, 128)],
        (planes, from_left, from_right, odd, even, height, conduct, inner),
        [
            pltpu.VMEM((PLANES, 16, 256), f32),
            pltpu.VMEM((3 * DEPTHS, 16, 256), f32),
            pltpu.VMEM((DEPTHS, 8, 128), f32),
        ],
    )
    sums = lax.all_to_all(sums.reshape(group, 1, 128), ("gx", "gy"), 0, 0)
    (parts,) = call(middle, [(lax.axis_size("gz"), 8, 128)], (sums.reshape(group, 128), top))
    parts = lax.all_to_all(parts, "gz", 0, 0)
    velocity, surface = call(
        finish, [(3, 8, 8, 128), (64, 128)], (parts, planes, image, height)
    )
    return velocity, surface


def solution(mesh):
    in_specs = (P(None, "gz", "gx", "gy"), P("gz", "gx", "gy"), P("gx", "gy"), P("gx", "gy"))
    out_specs = (P(None, "gz", "gx", "gy"), P("gx", ("gy", "gz")))
    return jax.shard_map(local, mesh=mesh, in_specs=in_specs, out_specs=out_specs, check_vma=False)
```

```python
import jax
import jax.numpy as jnp
from jax import lax
from jax.experimental import pallas as pl
from jax.experimental.pallas import tpu as pltpu
from jax.sharding import PartitionSpec as P

STEPS = 8
DRAG = 1.0
TIME_STEP = 1.0
LOAD_GAIN = 4.0
FACE, EDGE, CORNER = 0.5, 0.25, 0.5 / 3.0
TOTAL = 6 * FACE + 12 * EDGE + 8 * CORNER

DEPTHS = 12
PLANES = 4 * DEPTHS
PAIRS_ROW = 2 * PLANES
SURFACE_ROW = PAIRS_ROW + 8
GX_ROWS = SURFACE_ROW + 32

f32 = jnp.float32


def vmem():
    return pl.BlockSpec(memory_space=pltpu.VMEM)


def call(body, outs, ins, scratch=(), cost=20000, limit=8 << 20):
    return pl.pallas_call(
        body,
        out_shape=[jax.ShapeDtypeStruct(s, f32) for s in outs],
        in_specs=[vmem() for _ in ins],
        out_specs=[vmem() for _ in outs],
        scratch_shapes=list(scratch),
        compiler_params=pltpu.CompilerParams(vmem_limit_bytes=limit),
        cost_estimate=pl.CostEstimate(flops=cost * 1024, bytes_accessed=1 << 18, transcendentals=0),
    )(*ins)


def lanes(shape):
    return lax.broadcasted_iota(jnp.int32, shape, len(shape) - 1)


def rolled(x, amount, axis=1):
    amount = amount % x.shape[axis]
    return x if amount == 0 else pltpu.roll(x, amount, axis)


def surface_own(topo_ref, kappa_ref, load_ref, height_ref, conduct_ref, left_ref, right_ref):
    g = lax.axis_index("gz")
    last = lax.axis_size("gz") - 1
    lane = lanes((8, 128))
    pieces = []
    for v in range(8):
        piece = topo_ref[:, 128 * v : 128 * v + 128].reshape(8, 8, 128)
        pieces.append(jnp.sum(piece, axis=1))
    stacked = jnp.concatenate(pieces, axis=0)
    pick = (
        lax.broadcasted_iota(jnp.int32, (128, 128), 0) // 8 == lax.broadcasted_iota(jnp.int32, (128, 128), 1)
    ).astype(f32)
    sums = jnp.dot(stacked, pick, precision=lax.Precision.HIGHEST, preferred_element_type=f32)
    load = jnp.zeros((8, 128), f32)
    for v in range(8):
        load = load + rolled(sums[8 * v : 8 * v + 8], 16 * v)
    load_ref[...] = jnp.where(g == last, load * (-LOAD_GAIN / 64.0), 0.0)
    wide = lanes((64, 128))
    own = pl.ds(pl.multiple_of(g * 128, 128), 128)
    before = pl.ds(pl.multiple_of(jnp.maximum(g - 1, 0) * 128, 128), 128)
    after = pl.ds(pl.multiple_of(jnp.minimum(g + 1, last) * 128, 128), 128)
    for source, target in ((topo_ref, height_ref), (kappa_ref, conduct_ref)):
        target[:, 0:128] = source[:, own].astype(f32)
        side = jnp.where((wide < 8) & (g < last), source[:, after].astype(f32), 0.0)
        side = jnp.where((wide >= 120) & (g > 0), source[:, before].astype(f32), side)
        target[:, 128:256] = side
    width = topo_ref.shape[1]
    left = jnp.zeros((8, 128), f32)
    right = jnp.zeros((8, 128), f32)
    slot = 0
    for source in (topo_ref, kappa_ref):
        head = source[:, 0:128].astype(f32)
        tail = source[:, width - 128 : width].astype(f32)
        for r in range(8):
            mask = lane // 8 == slot
            left = jnp.where(mask, rolled(head[8 * r : 8 * r + 8], 8 * slot), left)
            right = jnp.where(mask, rolled(tail[8 * r : 8 * r + 8], 8 * slot - 120), right)
            slot += 1
    left_ref[...] = left
    right_ref[...] = right


def is_even(axis):
    return lax.rem(lax.axis_index(axis), 2) == 0


def fetch(force_ref, visc_ref, odd_ref, even_ref, sems):
    depth = visc_ref.shape[0]
    start = jnp.where(is_even("gz"), 0, depth - 2)
    moves = []
    for target, first in ((odd_ref, start), (even_ref, depth - 2 - start)):
        moves.append((force_ref.at[:, pl.ds(first, 2)], target.at[0:3]))
        moves.append((visc_ref.at[pl.ds(first, 2)], target.at[3]))
    copies = [pltpu.make_async_copy(source, target, sems.at[i]) for i, (source, target) in enumerate(moves)]
    for copy in copies:
        copy.start()
    for copy in copies:
        copy.wait()


def assemble(force_ref, visc_ref, load_ref, odd_ref, even_ref, sl_ref, sr_ref, planes_ref, odd_out, even_out):
    upward = is_even("gz")
    lane = lanes((8, 128))
    left = jnp.zeros((8, 128), f32)
    right = jnp.zeros((8, 128), f32)
    for field in range(4):
        for depth in range(DEPTHS):
            if depth < 2:
                plane = jnp.where(upward, odd_ref[field, depth], even_ref[field, depth])
            elif depth >= DEPTHS - 2:
                i = depth - (DEPTHS - 2)
                plane = jnp.where(upward, even_ref[field, i], odd_ref[field, i])
            elif field == 3:
                plane = visc_ref[depth - 2]
            else:
                plane = force_ref[field, depth - 2]
                if field == 2 and depth == DEPTHS - 3:
                    plane = plane + load_ref[...]
            p = field * DEPTHS + depth
            planes_ref[p] = plane
            mask = lane // 2 == p
            left = jnp.where(mask, rolled(plane, 2 * p), left)
            right = jnp.where(mask, rolled(plane, 2 * p - 126), right)
    rightward = is_even("gy")
    odd_out[0] = jnp.where(rightward, left, right)
    even_out[0] = jnp.where(rightward, right, left)
    odd_out[1] = jnp.where(rightward, sl_ref[...], sr_ref[...])
    even_out[1] = jnp.where(rightward, sr_ref[...], sl_ref[...])


def prepare_rows(planes_ref, odd_ref, even_ref, height_ref, conduct_ref, odd_out, even_out, rl_ref, rr_ref, height_out, conduct_out):
    rightward = is_even("gy")
    for i in range(2):
        rl_ref[i] = jnp.where(rightward, odd_ref[i], even_ref[i])
        rr_ref[i] = jnp.where(rightward, even_ref[i], odd_ref[i])
    downward = is_even("gx")

    def send(rows, low, high):
        odd_out[rows, :] = jnp.where(downward, low, high)
        even_out[rows, :] = jnp.where(downward, high, low)

    g = lax.axis_index("gz")
    last = lax.axis_size("gz") - 1
    lane = lanes((8, 128))
    for p in range(PLANES):
        send(slice(2 * p, 2 * p + 2), planes_ref[p, 0:2, :], planes_ref[p, 6:8, :])
    pad = jnp.zeros((4, 128), f32)
    send(
        slice(PAIRS_ROW, SURFACE_ROW),
        jnp.concatenate([rl_ref[0, 0:2, :], rr_ref[0, 0:2, :], pad], axis=0),
        jnp.concatenate([rl_ref[0, 6:8, :], rr_ref[0, 6:8, :], pad], axis=0),
    )
    slot = 0
    for index, (source, target) in enumerate(((height_ref, height_out), (conduct_ref, conduct_out))):
        base = SURFACE_ROW + 16 * index
        for r in range(8):
            rows = slice(8 * r, 8 * r + 8)
            main = source[rows, 0:128]
            side = source[rows, 128:256]
            side = jnp.where((g == 0) & (lane >= 120), rolled(rl_ref[1], 120 - 8 * slot), side)
            side = jnp.where((g == last) & (lane < 8), rolled(rr_ref[1], -8 * slot), side)
            target[rows, 0:128] = main
            target[rows, 128:256] = side
            if r == 0:
                first = (main, side)
            if r == 7:
                send(slice(base, base + 8), first[0], main)
                send(slice(base + 8, base + 16), first[1], side)
            slot += 1


def stencil(before, here, after):
    outer = before + after
    a = FACE * here + EDGE * outer
    b = EDGE * here + CORNER * outer
    both = a + rolled(b, 1, 0) + rolled(b, 15, 0)
    rows = rolled(a, 1, 0) + rolled(a, 15, 0)
    return FACE * outer + rows + rolled(both, 1, 1) + rolled(both, 255, 1)


def sided(odd_ref, even_ref, axis):
    first = is_even(axis)

    def before(rows):
        return jnp.where(first, odd_ref[rows, :], even_ref[rows, :])

    def after(rows):
        return jnp.where(first, even_ref[rows, :], odd_ref[rows, :])

    return before, after


def steps(h, k):
    rows = h.shape[0]
    inside = k > 0.0
    along = 0.5 * (k + rolled(k, 255, 1))
    across = 0.5 * (k + rolled(k, rows - 1, 0))
    for step in range(STEPS):
        s = rolled(h, 255, 1) - h
        q = along * s * lax.rsqrt(1.0 + s * s)
        t = rolled(h, rows - 1, 0) - h
        r = across * t * lax.rsqrt(1.0 + t * t)
        change = (q - rolled(q, 1, 1)) + (r - rolled(r, 1, 0))
        h = jnp.where(inside, h + TIME_STEP * change, 0.0)
    return h


def operate(
    planes_ref, rl_ref, rr_ref, odd_ref, even_ref, height_ref, conduct_ref, image_ref, sums_ref, top_ref, out_ref, x, w, diag
):
    lane = lanes((8, 128))
    row = lax.broadcasted_iota(jnp.int32, (8, 128), 0)
    pad = jnp.zeros((4, 128), f32)
    before, after = sided(odd_ref, even_ref, "gx")

    def around(start):
        rows = slice(start, start + 2)
        return jnp.concatenate([after(rows), pad, before(rows)], axis=0)

    def extended(source, base):
        def joined(side):
            return jnp.concatenate([side(slice(base, base + 8)), side(slice(base + 8, base + 16))], axis=1)

        return jnp.concatenate([source[...], joined(after), joined(before)], axis=0)

    stepped = steps(extended(height_ref, SURFACE_ROW), extended(conduct_ref, SURFACE_ROW + 16))
    out_ref[...] = stepped[0:64, 0:128]
    lower_l = around(PAIRS_ROW)
    lower_r = around(PAIRS_ROW + 2)
    for p in range(PLANES):
        x[p, 0:8, 0:128] = planes_ref[p]
        x[p, 8:16, 0:128] = around(2 * p)
        for start, l, r in ((0, rl_ref[0], rr_ref[0]), (8, lower_l, lower_r)):
            side = jnp.where(lane < 2, rolled(r, -2 * p), 0.0)
            side = jnp.where(lane >= 126, rolled(l, 126 - 2 * p), side)
            x[p, start : start + 8, 128:256] = side
    for depth in range(1, DEPTHS - 1):
        e = [x[3 * DEPTHS + depth + i] for i in (-1, 0, 1)]
        d = (DRAG + TOTAL * e[1]) + stencil(*e)
        diag[depth] = d[0:8, 0:128]
        inside = e[1] > 0.0
        for c in range(3):
            v = [x[c * DEPTHS + depth + i] for i in (-1, 0, 1)]
            ev = [e[i] * v[i] for i in range(3)]
            out = v[1] * d - e[1] * stencil(*v) - stencil(*ev)
            w[c * DEPTHS + depth] = jnp.where(inside, out, 0.0)
    m = [jnp.zeros((8, 128), f32) for _ in range(4)]
    for depth in range(2, DEPTHS - 2):
        e = x[3 * DEPTHS + depth, 0:8, 0:128]
        d = diag[depth]
        for c in range(3):
            p = c * DEPTHS + depth
            s = stencil(w[p - 1], w[p], w[p + 1])[0:8, 0:128]
            v = x[p, 0:8, 0:128]
            q = w[p, 0:8, 0:128]
            image_ref[c, depth - 2] = q
            m[0] = m[0] + v * v
            m[1] = m[1] + v * q
            m[2] = m[2] + q * q
            m[3] = m[3] + q * (q * d - 2.0 * (e * s))
    total = jnp.zeros((8, 128), f32)
    for k in range(4):
        total = jnp.where(lane == k, jnp.sum(m[k]), total)
    for i in range(sums_ref.shape[0] // 8):
        sums_ref[8 * i : 8 * i + 8, :] = total
    p = 2 * DEPTHS + DEPTHS - 3
    top_ref[0] = x[p, 0:8, 0:128]
    top_ref[1] = w[p, 0:8, 0:128]


def middle(sums_ref, top_ref, out_ref):
    lane = lanes((8, 128))
    part = jnp.sum(sums_ref[...], axis=0, keepdims=True)
    base = jnp.broadcast_to(rolled(part, 32), (8, 128))
    base = jnp.where((lane >= 32) & (lane < 36), base, 0.0)
    for j in range(out_ref.shape[0]):
        piece = jnp.where(lane < 16, rolled(top_ref[0], -16 * j), base)
        out_ref[j] = jnp.where(lane // 16 == 1, rolled(top_ref[1], 16 - 16 * j), piece)


def finish(parts_ref, planes_ref, image_ref, height_ref, velocity_ref, surface_ref):
    count = parts_ref.shape[0]
    lane = lanes((1, 128))
    total = parts_ref[0, 0:1, :]
    for j in range(1, count):
        total = total + parts_ref[j, 0:1, :]

    def moment(k):
        return jnp.sum(jnp.where(lane == 32 + k, total, 0.0), axis=1, keepdims=True)

    m0, m1, m2, m3 = (moment(k) for k in range(4))
    first = m0 / m1
    later = first * first * m2 - m0
    gain = 1.0 + later / m0
    second = later / (gain * gain * m1 - 2.0 * first * gain * m2 + first * first * m3)
    on_force = first + second * gain
    on_image = -(second * first)
    for c in range(3):
        for depth in range(8):
            velocity_ref[c, depth] = on_force * planes_ref[c * DEPTHS + depth + 2] + on_image * image_ref[c, depth]
    top = parts_ref[count - 1]
    rise = on_force * top + on_image * rolled(top, -16)
    spread = (
        lax.broadcasted_iota(jnp.int32, (128, 128), 1) // 8 == lax.broadcasted_iota(jnp.int32, (128, 128), 0)
    ).astype(f32)
    rise = jnp.where(lanes((8, 128)) < 16, rise, 0.0)
    wide = (STEPS * TIME_STEP) * jnp.dot(rise, spread, precision=lax.Precision.HIGHEST, preferred_element_type=f32)
    for r in range(8):
        rows = slice(8 * r, 8 * r + 8)
        surface_ref[rows, :] = height_ref[rows, :] + jnp.broadcast_to(wide[r : r + 1, :], (8, 128))


def swap(odd, even, axis):
    count = lax.axis_size(axis)

    def pairs(start):
        found = []
        for i in range(start, count - 1, 2):
            found += [(i, i + 1), (i + 1, i)]
        return found

    return lax.ppermute(odd, axis, pairs(1)), lax.ppermute(even, axis, pairs(0))


def local(body_force, viscosity, topography, kappa):
    odd, even = pl.pallas_call(
        fetch,
        out_shape=[jax.ShapeDtypeStruct((4, 2, 8, 128), f32)] * 2,
        in_specs=[pl.BlockSpec(memory_space=pltpu.HBM)] * 2,
        out_specs=[vmem()] * 2,
        scratch_shapes=[pltpu.SemaphoreType.DMA((4,))],
        compiler_params=pltpu.CompilerParams(vmem_limit_bytes=1 << 20),
    )(*[pltpu.with_memory_space_constraint(x, pltpu.HBM) for x in (body_force, viscosity)])
    odd, even = swap(odd, even, "gz")
    load, height, conduct, left, right = call(
        surface_own,
        [(8, 128), (64, 256), (64, 256), (8, 128), (8, 128)],
        (topography, kappa),
    )
    planes, odd, even = call(
        assemble,
        [(PLANES, 8, 128), (2, 8, 128), (2, 8, 128)],
        (body_force, viscosity, load, odd, even, left, right),
    )
    odd, even = swap(odd, even, "gy")
    odd, even, from_left, from_right, height, conduct = call(
        prepare_rows,
        [(GX_ROWS, 128), (GX_ROWS, 128), (2, 8, 128), (2, 8, 128), (64, 256), (64, 256)],
        (planes, odd, even, height, conduct),
    )
    odd, even = swap(odd, even, "gx")
    group = lax.axis_size("gx") * lax.axis_size("gy")
    image, sums, top, height = call(
        operate,
        [(3, 8, 8, 128), (group, 128), (2, 8, 128), (64, 128)],
        (planes, from_left, from_right, odd, even, height, conduct),
        [
            pltpu.VMEM((PLANES, 16, 256), f32),
            pltpu.VMEM((3 * DEPTHS, 16, 256), f32),
            pltpu.VMEM((DEPTHS, 8, 128), f32),
        ],
    )
    sums = lax.all_to_all(sums.reshape(group, 1, 128), ("gx", "gy"), 0, 0)
    (parts,) = call(middle, [(lax.axis_size("gz"), 8, 128)], (sums.reshape(group, 128), top))
    parts = lax.all_to_all(parts, "gz", 0, 0)
    velocity, surface = call(
        finish, [(3, 8, 8, 128), (64, 128)], (parts, planes, image, height)
    )
    return velocity, surface


def solution(mesh):
    in_specs = (P(None, "gz", "gx", "gy"), P("gz", "gx", "gy"), P("gx", "gy"), P("gx", "gy"))
    out_specs = (P(None, "gz", "gx", "gy"), P("gx", ("gy", "gz")))
    return jax.shard_map(local, mesh=mesh, in_specs=in_specs, out_specs=out_specs, check_vma=False)
```

```python
import jax
import jax.numpy as jnp
from jax import lax
from jax.experimental import pallas as pl
from jax.experimental.pallas import tpu as pltpu
from jax.sharding import PartitionSpec as P

STEPS = 8
DRAG = 1.0
TIME_STEP = 1.0
LOAD_GAIN = 4.0
FACE, EDGE, CORNER = 0.5, 0.25, 0.5 / 3.0
TOTAL = 6 * FACE + 12 * EDGE + 8 * CORNER

DEPTHS = 12
PLANES = 4 * DEPTHS
COLUMN_ROW = 8 * DEPTHS
SURFACE_ROW = COLUMN_ROW + 8
GX_ROWS = SURFACE_ROW + 32

f32 = jnp.float32


def vmem():
    return pl.BlockSpec(memory_space=pltpu.VMEM)


def call(body, outs, ins, scratch=(), cost=20000, limit=8 << 20):
    return pl.pallas_call(
        body,
        out_shape=[jax.ShapeDtypeStruct(s, f32) for s in outs],
        in_specs=[vmem() for _ in ins],
        out_specs=[vmem() for _ in outs],
        scratch_shapes=list(scratch),
        compiler_params=pltpu.CompilerParams(vmem_limit_bytes=limit),
        cost_estimate=pl.CostEstimate(flops=cost * 1024, bytes_accessed=1 << 18, transcendentals=0),
    )(*ins)


def lanes(shape):
    return lax.broadcasted_iota(jnp.int32, shape, len(shape) - 1)


def rolled(x, amount, axis=1):
    amount = amount % x.shape[axis]
    return x if amount == 0 else pltpu.roll(x, amount, axis)


def surface_own(topo_ref, kappa_ref, load_ref, height_ref, conduct_ref, left_ref, right_ref):
    g = lax.axis_index("gz")
    last = lax.axis_size("gz") - 1
    lane = lanes((8, 128))
    pieces = []
    for v in range(8):
        piece = topo_ref[:, 128 * v : 128 * v + 128].reshape(8, 8, 128)
        pieces.append(jnp.sum(piece, axis=1))
    stacked = jnp.concatenate(pieces, axis=0)
    pick = (
        lax.broadcasted_iota(jnp.int32, (128, 128), 0) // 8 == lax.broadcasted_iota(jnp.int32, (128, 128), 1)
    ).astype(f32)
    sums = jnp.dot(stacked, pick, precision=lax.Precision.HIGHEST, preferred_element_type=f32)
    load = jnp.zeros((8, 128), f32)
    for v in range(8):
        load = load + rolled(sums[8 * v : 8 * v + 8], 16 * v)
    load_ref[...] = jnp.where(g == last, load * (-LOAD_GAIN / 64.0), 0.0)
    wide = lanes((64, 128))
    own = pl.ds(pl.multiple_of(g * 128, 128), 128)
    before = pl.ds(pl.multiple_of(jnp.maximum(g - 1, 0) * 128, 128), 128)
    after = pl.ds(pl.multiple_of(jnp.minimum(g + 1, last) * 128, 128), 128)
    for source, target in ((topo_ref, height_ref), (kappa_ref, conduct_ref)):
        target[:, 0:128] = source[:, own].astype(f32)
        side = jnp.where((wide < 8) & (g < last), source[:, after].astype(f32), 0.0)
        side = jnp.where((wide >= 120) & (g > 0), source[:, before].astype(f32), side)
        target[:, 128:256] = side
    width = topo_ref.shape[1]
    left = jnp.zeros((8, 128), f32)
    right = jnp.zeros((8, 128), f32)
    slot = 0
    for source in (topo_ref, kappa_ref):
        head = source[:, 0:128].astype(f32)
        tail = source[:, width - 128 : width].astype(f32)
        for r in range(8):
            mask = lane // 8 == slot
            left = jnp.where(mask, rolled(head[8 * r : 8 * r + 8], 8 * slot), left)
            right = jnp.where(mask, rolled(tail[8 * r : 8 * r + 8], 8 * slot - 120), right)
            slot += 1
    left_ref[...] = left
    right_ref[...] = right


def is_even(axis):
    return lax.rem(lax.axis_index(axis), 2) == 0


def fetch(force_ref, visc_ref, odd_ref, even_ref, sems):
    depth = visc_ref.shape[0]
    start = jnp.where(is_even("gz"), 0, depth - 2)
    moves = []
    for target, first in ((odd_ref, start), (even_ref, depth - 2 - start)):
        moves.append((force_ref.at[:, pl.ds(first, 2)], target.at[0:3]))
        moves.append((visc_ref.at[pl.ds(first, 2)], target.at[3]))
    copies = [pltpu.make_async_copy(source, target, sems.at[i]) for i, (source, target) in enumerate(moves)]
    for copy in copies:
        copy.start()
    for copy in copies:
        copy.wait()


def assemble(force_ref, visc_ref, load_ref, odd_ref, even_ref, sl_ref, sr_ref, planes_ref, odd_out, even_out):
    upward = is_even("gz")
    lane = lanes((8, 128))
    left = jnp.zeros((8, 128), f32)
    right = jnp.zeros((8, 128), f32)
    for field in range(4):
        for depth in range(DEPTHS):
            if depth < 2:
                plane = jnp.where(upward, odd_ref[field, depth], even_ref[field, depth])
            elif depth >= DEPTHS - 2:
                i = depth - (DEPTHS - 2)
                plane = jnp.where(upward, even_ref[field, i], odd_ref[field, i])
            elif field == 3:
                plane = visc_ref[depth - 2]
            else:
                plane = force_ref[field, depth - 2]
                if field == 2 and depth == DEPTHS - 3:
                    plane = plane + load_ref[...]
            p = field * DEPTHS + depth
            planes_ref[p] = plane
            first = 8 * depth + 2 * field
            mask = lane // 2 == first // 2
            left = jnp.where(mask, rolled(plane, first), left)
            right = jnp.where(mask, rolled(plane, first - 126), right)
    rightward = is_even("gy")
    odd_out[0] = jnp.where(rightward, left, right)
    even_out[0] = jnp.where(rightward, right, left)
    odd_out[1] = jnp.where(rightward, sl_ref[...], sr_ref[...])
    even_out[1] = jnp.where(rightward, sr_ref[...], sl_ref[...])


def edge_rows(planes_ref, low_ref, high_ref):
    for depth in range(DEPTHS):
        for field in range(4):
            plane = planes_ref.at[field * DEPTHS + depth]
            near = 8 * depth + field
            low_ref[near : near + 1, :] = plane[0:1, :]
            low_ref[near + 4 : near + 5, :] = plane[1:2, :]
            high_ref[near : near + 1, :] = plane[7:8, :]
            high_ref[near + 4 : near + 5, :] = plane[6:7, :]


def prepare_rows(
    low_ref, high_ref, own_odd, own_even, odd_ref, even_ref, height_ref, conduct_ref,
    odd_out, even_out, column_ref, height_out, conduct_out,
):
    g = lax.axis_index("gz")
    last = lax.axis_size("gz") - 1
    lane = lanes((8, 128))
    rightward = is_even("gy")

    def chosen(first, second, i):
        return jnp.where(rightward, first[i], second[i])

    before, after = chosen(odd_ref, even_ref, 0), chosen(even_ref, odd_ref, 0)
    before_surface, after_surface = chosen(odd_ref, even_ref, 1), chosen(even_ref, odd_ref, 1)
    side = lax.rem(lane, 2) == 0
    levels = (
        jnp.where(side, chosen(own_odd, own_even, 0), chosen(own_even, own_odd, 0)),
        jnp.where(side, rolled(before, -1), rolled(after, 1)),
        jnp.where(side, before, after),
    )
    downward = is_even("gx")

    def send(rows, low, high):
        odd_out[rows, :] = jnp.where(downward, low, high)
        even_out[rows, :] = jnp.where(downward, high, low)

    for depth in range(DEPTHS):
        rows = slice(8 * depth, 8 * depth + 8)
        send(rows, low_ref[rows, :], high_ref[rows, :])
    pad = [jnp.zeros((2, 128), f32)]
    send(
        slice(COLUMN_ROW, SURFACE_ROW),
        jnp.concatenate([x[0:2] for x in levels] + pad, axis=0),
        jnp.concatenate([x[6:8] for x in levels] + pad, axis=0),
    )
    for i in range(3):
        column_ref[i] = levels[i]
    slot = 0
    for index, (source, target) in enumerate(((height_ref, height_out), (conduct_ref, conduct_out))):
        base = SURFACE_ROW + 16 * index
        for r in range(8):
            rows = slice(8 * r, 8 * r + 8)
            main = source[rows, 0:128]
            side = source[rows, 128:256]
            side = jnp.where((g == 0) & (lane >= 120), rolled(before_surface, 120 - 8 * slot), side)
            side = jnp.where((g == last) & (lane < 8), rolled(after_surface, -8 * slot), side)
            target[rows, 0:128] = main
            target[rows, 128:256] = side
            if r == 0:
                first = (main, side)
            if r == 7:
                send(slice(base, base + 8), first[0], main)
                send(slice(base + 8, base + 16), first[1], side)
            slot += 1


def weighted(before, here, after):
    outer = before + after
    return outer, FACE * here + EDGE * outer, EDGE * here + CORNER * outer


def pair(x):
    return rolled(x, 1, 0) + rolled(x, x.shape[0] - 1, 0)


def lane_pair(x, lane, first, last):
    return jnp.where(lane == 0, first, rolled(x, 1)) + jnp.where(lane == 127, last, rolled(x, 127))


def row_pair(x, row, edge, field):
    up = jnp.where(row == 0, rolled(edge, -field, 0), rolled(x, 1, 0))
    return up + jnp.where(row == 7, rolled(edge, 3 - field, 0), rolled(x, 7, 0))


def to_first(x, depth, field):
    return rolled(x, -(8 * depth + 2 * field))


def to_last(x, depth, field):
    return rolled(x, 126 - (8 * depth + 2 * field))


def spread_rows(x, row):
    field = lax.rem(row, 4)
    for f in range(3):
        x = jnp.where(field == f, rolled(x, f - 3, 0), x)
    return x


def spread_columns(x, lane):
    field = lax.rem(lane, 8) // 2
    for f in range(3):
        x = jnp.where(field == f, rolled(x, 2 * (f - 3)), x)
    return x


def column_sums(levels):
    parts = [weighted(rolled(x, 8), x, rolled(x, 120)) for x in levels]
    (_, ai, bi), (outer, an, bn), (_, af, bf) = parts
    beside = an + pair(bn)
    return FACE * outer + pair(an) + (ai + af) + pair(bi + bf), beside


def beside_rows(beside, depth, row):
    near = jnp.where(row < 4, jnp.broadcast_to(beside[15:16], (8, 128)), jnp.broadcast_to(beside[8:9], (8, 128)))
    field = lax.rem(row, 4)
    first, last = to_first(near, depth, 0), to_last(near, depth, 0)
    for f in range(1, 4):
        first = jnp.where(field == f, to_first(near, depth, f), first)
        last = jnp.where(field == f, to_last(near, depth, f), last)
    return first, last


def sided(odd_ref, even_ref, axis):
    first = is_even(axis)

    def before(rows):
        return jnp.where(first, odd_ref[rows, :], even_ref[rows, :])

    def after(rows):
        return jnp.where(first, even_ref[rows, :], odd_ref[rows, :])

    return before, after


def steps(h, k):
    rows = h.shape[0]
    inside = k > 0.0
    along = 0.5 * (k + rolled(k, 255, 1))
    across = 0.5 * (k + rolled(k, rows - 1, 0))
    for step in range(STEPS):
        s = rolled(h, 255, 1) - h
        q = along * s * lax.rsqrt(1.0 + s * s)
        t = rolled(h, rows - 1, 0) - h
        r = across * t * lax.rsqrt(1.0 + t * t)
        change = (q - rolled(q, 1, 1)) + (r - rolled(r, 1, 0))
        h = jnp.where(inside, h + TIME_STEP * change, 0.0)
    return h


def operate(
    planes_ref, low_ref, high_ref, column_ref, odd_ref, even_ref, height_ref, conduct_ref,
    image_ref, sums_ref, top_ref, out_ref,
):
    lane = lanes((8, 128))
    row = lax.broadcasted_iota(jnp.int32, (8, 128), 0)
    wide = lanes((16, 128))
    before, after = sided(odd_ref, even_ref, "gx")

    def extended(source, base):
        def joined(side):
            return jnp.concatenate([side(slice(base, base + 8)), side(slice(base + 8, base + 16))], axis=1)

        return jnp.concatenate([source[...], joined(after), joined(before)], axis=0)

    stepped = steps(extended(height_ref, SURFACE_ROW), extended(conduct_ref, SURFACE_ROW + 16))
    out_ref[...] = stepped[0:64, 0:128]
    columns = []
    for i in range(3):
        rows = slice(COLUMN_ROW + 2 * i, COLUMN_ROW + 2 * i + 2)
        columns.append(jnp.concatenate([column_ref[i], after(rows), jnp.zeros((4, 128), f32), before(rows)], axis=0))
    column_eta = [spread_columns(x, wide) for x in columns]
    column_sum, beside = column_sums(columns)
    column_sum_eta, beside_eta = column_sums([x * y for x, y in zip(columns, column_eta)])
    near_eta = column_eta[1]
    column_diag = DRAG + TOTAL * near_eta + spread_columns(column_sum, wide)
    column_image = columns[1] * column_diag - near_eta * column_sum - column_sum_eta
    column_image = jnp.where(near_eta > 0.0, column_image, 0.0)
    rows_of, rows_eta = [], []
    for depth in range(DEPTHS):
        rows = slice(8 * depth, 8 * depth + 8)
        b, a = before(rows), after(rows)
        found = (
            jnp.where(row < 4, low_ref[rows, :], rolled(high_ref[rows, :], 4, 0)),
            jnp.where(row < 4, b, rolled(a, 4, 0)),
            jnp.where(row < 4, rolled(b, 4, 0), a),
        )
        rows_of.append(found)
        rows_eta.append([spread_rows(x, row) for x in found])
    rows_product = [[x * y for x, y in zip(found, etas)] for found, etas in zip(rows_of, rows_eta)]

    def row_sums(levels, depth, beside_columns):
        parts = [weighted(levels[depth - 1][i], levels[depth][i], levels[depth + 1][i]) for i in range(3)]
        (_, ai, bi), (outer, an, bn), (_, af, bf) = parts
        first, last = beside_rows(beside_columns, depth, row)
        return FACE * outer + (ai + af) + lane_pair(an + (bi + bf), lane, first, last), an, bn

    def plane_sum(three, an, bn, beside_columns, depth, field):
        outer, a, b = weighted(*three)
        both = a + row_pair(b, row, bn, field)
        own = beside_columns[0:8]
        sides = lane_pair(both, lane, to_first(own, depth, field), to_last(own, depth, field))
        return FACE * outer + row_pair(a, row, an, field) + sides

    def plane(field, depth):
        return planes_ref[field * DEPTHS + depth]

    image, row_image, diagonal = {}, {}, {}
    for depth in range(1, DEPTHS - 1):
        row_sum, an, bn = row_sums(rows_of, depth, beside)
        row_sum_eta, an_eta, bn_eta = row_sums(rows_product, depth, beside_eta)
        near, eta = rows_of[depth][1], rows_eta[depth][1]
        diag = DRAG + TOTAL * eta + spread_rows(row_sum, row)
        row_image[depth] = jnp.where(eta > 0.0, near * diag - eta * row_sum - row_sum_eta, 0.0)
        e = [plane(3, depth + i) for i in (-1, 0, 1)]
        diag = DRAG + TOTAL * e[1] + plane_sum(e, an, bn, beside, depth, 3)
        diagonal[depth] = diag
        for c in range(3):
            v = [plane(c, depth + i) for i in (-1, 0, 1)]
            ev = [x * y for x, y in zip(e, v)]
            out = v[1] * diag - e[1] * plane_sum(v, an, bn, beside, depth, c)
            out = out - plane_sum(ev, an_eta, bn_eta, beside_eta, depth, c)
            image[c, depth] = jnp.where(e[1] > 0.0, out, 0.0)
    _, an, bn = weighted(rolled(column_image, 8), column_image, rolled(column_image, 120))
    beside = an + pair(bn)
    m = [jnp.zeros((8, 128), f32) for _ in range(4)]
    for depth in range(2, DEPTHS - 2):
        _, an, bn = weighted(row_image[depth - 1], row_image[depth], row_image[depth + 1])
        e = plane(3, depth)
        for c in range(3):
            s = plane_sum([image[c, depth + i] for i in (-1, 0, 1)], an, bn, beside, depth, c)
            v, q = plane(c, depth), image[c, depth]
            image_ref[c, depth - 2] = q
            m[0] = m[0] + v * v
            m[1] = m[1] + v * q
            m[2] = m[2] + q * q
            m[3] = m[3] + q * (q * diagonal[depth] - 2.0 * (e * s))
    total = jnp.zeros((8, 128), f32)
    for k in range(4):
        total = jnp.where(lane == k, jnp.sum(m[k]), total)
    for i in range(sums_ref.shape[0] // 8):
        sums_ref[8 * i : 8 * i + 8, :] = total
    top_ref[0] = plane(2, DEPTHS - 3)
    top_ref[1] = image[2, DEPTHS - 3]


def middle(sums_ref, top_ref, out_ref):
    lane = lanes((8, 128))
    part = jnp.sum(sums_ref[...], axis=0, keepdims=True)
    base = jnp.broadcast_to(rolled(part, 32), (8, 128))
    base = jnp.where((lane >= 32) & (lane < 36), base, 0.0)
    for j in range(out_ref.shape[0]):
        piece = jnp.where(lane < 16, rolled(top_ref[0], -16 * j), base)
        out_ref[j] = jnp.where(lane // 16 == 1, rolled(top_ref[1], 16 - 16 * j), piece)


def finish(parts_ref, planes_ref, image_ref, height_ref, velocity_ref, surface_ref):
    count = parts_ref.shape[0]
    lane = lanes((1, 128))
    total = parts_ref[0, 0:1, :]
    for j in range(1, count):
        total = total + parts_ref[j, 0:1, :]

    def moment(k):
        return jnp.sum(jnp.where(lane == 32 + k, total, 0.0), axis=1, keepdims=True)

    m0, m1, m2, m3 = (moment(k) for k in range(4))
    first = m0 / m1
    later = first * first * m2 - m0
    gain = 1.0 + later / m0
    second = later / (gain * gain * m1 - 2.0 * first * gain * m2 + first * first * m3)
    on_force = first + second * gain
    on_image = -(second * first)
    for c in range(3):
        for depth in range(8):
            velocity_ref[c, depth] = on_force * planes_ref[c * DEPTHS + depth + 2] + on_image * image_ref[c, depth]
    top = parts_ref[count - 1]
    rise = on_force * top + on_image * rolled(top, -16)
    spread = (
        lax.broadcasted_iota(jnp.int32, (128, 128), 1) // 8 == lax.broadcasted_iota(jnp.int32, (128, 128), 0)
    ).astype(f32)
    rise = jnp.where(lanes((8, 128)) < 16, rise, 0.0)
    wide = (STEPS * TIME_STEP) * jnp.dot(rise, spread, precision=lax.Precision.HIGHEST, preferred_element_type=f32)
    for r in range(8):
        rows = slice(8 * r, 8 * r + 8)
        surface_ref[rows, :] = height_ref[rows, :] + jnp.broadcast_to(wide[r : r + 1, :], (8, 128))


def swap(odd, even, axis):
    count = lax.axis_size(axis)

    def pairs(start):
        found = []
        for i in range(start, count - 1, 2):
            found += [(i, i + 1), (i + 1, i)]
        return found

    return lax.ppermute(odd, axis, pairs(1)), lax.ppermute(even, axis, pairs(0))


def local(body_force, viscosity, topography, kappa):
    odd, even = pl.pallas_call(
        fetch,
        out_shape=[jax.ShapeDtypeStruct((4, 2, 8, 128), f32)] * 2,
        in_specs=[pl.BlockSpec(memory_space=pltpu.HBM)] * 2,
        out_specs=[vmem()] * 2,
        scratch_shapes=[pltpu.SemaphoreType.DMA((4,))],
        compiler_params=pltpu.CompilerParams(vmem_limit_bytes=1 << 20),
    )(*[pltpu.with_memory_space_constraint(x, pltpu.HBM) for x in (body_force, viscosity)])
    odd, even = swap(odd, even, "gz")
    load, height, conduct, left, right = call(
        surface_own,
        [(8, 128), (64, 256), (64, 256), (8, 128), (8, 128)],
        (topography, kappa),
    )
    planes, odd, even = call(
        assemble,
        [(PLANES, 8, 128), (2, 8, 128), (2, 8, 128)],
        (body_force, viscosity, load, odd, even, left, right),
    )
    own = (odd, even)
    odd, even = swap(odd, even, "gy")
    low, high = call(edge_rows, [(COLUMN_ROW, 128)] * 2, (planes,))
    odd, even, columns, height, conduct = call(
        prepare_rows,
        [(GX_ROWS, 128), (GX_ROWS, 128), (3, 8, 128), (64, 256), (64, 256)],
        (low, high, *own, odd, even, height, conduct),
    )
    odd, even = swap(odd, even, "gx")
    group = lax.axis_size("gx") * lax.axis_size("gy")
    image, sums, top, height = call(
        operate,
        [(3, 8, 8, 128), (group, 128), (2, 8, 128), (64, 128)],
        (planes, low, high, columns, odd, even, height, conduct),
    )
    sums = lax.all_to_all(sums.reshape(group, 1, 128), ("gx", "gy"), 0, 0)
    (parts,) = call(middle, [(lax.axis_size("gz"), 8, 128)], (sums.reshape(group, 128), top))
    parts = lax.all_to_all(parts, "gz", 0, 0)
    velocity, surface = call(
        finish, [(3, 8, 8, 128), (64, 128)], (parts, planes, image, height)
    )
    return velocity, surface


def solution(mesh):
    in_specs = (P(None, "gz", "gx", "gy"), P("gz", "gx", "gy"), P("gx", "gy"), P("gx", "gy"))
    out_specs = (P(None, "gz", "gx", "gy"), P("gx", ("gy", "gz")))
    return jax.shard_map(local, mesh=mesh, in_specs=in_specs, out_specs=out_specs, check_vma=False)
```

```python
import jax
import jax.numpy as jnp
from jax import lax
from jax.experimental import pallas as pl
from jax.experimental.pallas import tpu as pltpu
from jax.sharding import PartitionSpec as P

STEPS = 8
DRAG = 1.0
TIME_STEP = 1.0
LOAD_GAIN = 4.0
FACE, EDGE, CORNER = 0.5, 0.25, 0.5 / 3.0
TOTAL = 6 * FACE + 12 * EDGE + 8 * CORNER

DEPTHS = 12
PLANES = 4 * DEPTHS
COLUMN_ROW = 8 * DEPTHS
SURFACE_ROW = COLUMN_ROW + 8
GX_ROWS = SURFACE_ROW + 32

f32 = jnp.float32


def vmem():
    return pl.BlockSpec(memory_space=pltpu.VMEM)


def call(body, outs, ins, scratch=(), cost=20000, limit=8 << 20):
    return pl.pallas_call(
        body,
        out_shape=[jax.ShapeDtypeStruct(s, f32) for s in outs],
        in_specs=[vmem() for _ in ins],
        out_specs=[vmem() for _ in outs],
        scratch_shapes=list(scratch),
        compiler_params=pltpu.CompilerParams(vmem_limit_bytes=limit),
        cost_estimate=pl.CostEstimate(flops=cost * 1024, bytes_accessed=1 << 18, transcendentals=0),
    )(*ins)


def lanes(shape):
    return lax.broadcasted_iota(jnp.int32, shape, len(shape) - 1)


def rolled(x, amount, axis=1):
    amount = amount % x.shape[axis]
    return x if amount == 0 else pltpu.roll(x, amount, axis)


def surface_own(topo_ref, kappa_ref, load_ref, height_ref, conduct_ref, left_ref, right_ref):
    g = lax.axis_index("gz")
    last = lax.axis_size("gz") - 1
    lane = lanes((8, 128))
    pieces = []
    for v in range(8):
        piece = topo_ref[:, 128 * v : 128 * v + 128].reshape(8, 8, 128)
        pieces.append(jnp.sum(piece, axis=1))
    stacked = jnp.concatenate(pieces, axis=0)
    pick = (
        lax.broadcasted_iota(jnp.int32, (128, 128), 0) // 8 == lax.broadcasted_iota(jnp.int32, (128, 128), 1)
    ).astype(f32)
    sums = jnp.dot(stacked, pick, precision=lax.Precision.HIGHEST, preferred_element_type=f32)
    load = jnp.zeros((8, 128), f32)
    for v in range(8):
        load = load + rolled(sums[8 * v : 8 * v + 8], 16 * v)
    load_ref[...] = jnp.where(g == last, load * (-LOAD_GAIN / 64.0), 0.0)
    wide = lanes((64, 128))
    own = pl.ds(pl.multiple_of(g * 128, 128), 128)
    before = pl.ds(pl.multiple_of(jnp.maximum(g - 1, 0) * 128, 128), 128)
    after = pl.ds(pl.multiple_of(jnp.minimum(g + 1, last) * 128, 128), 128)
    for source, target in ((topo_ref, height_ref), (kappa_ref, conduct_ref)):
        target[:, 0:128] = source[:, own].astype(f32)
        side = jnp.where((wide < 8) & (g < last), source[:, after].astype(f32), 0.0)
        side = jnp.where((wide >= 120) & (g > 0), source[:, before].astype(f32), side)
        target[:, 128:256] = side
    width = topo_ref.shape[1]
    left = jnp.zeros((8, 128), f32)
    right = jnp.zeros((8, 128), f32)
    slot = 0
    for source in (topo_ref, kappa_ref):
        head = source[:, 0:128].astype(f32)
        tail = source[:, width - 128 : width].astype(f32)
        for r in range(8):
            mask = lane // 8 == slot
            left = jnp.where(mask, rolled(head[8 * r : 8 * r + 8], 8 * slot), left)
            right = jnp.where(mask, rolled(tail[8 * r : 8 * r + 8], 8 * slot - 120), right)
            slot += 1
    left_ref[...] = left
    right_ref[...] = right


def is_even(axis):
    return lax.rem(lax.axis_index(axis), 2) == 0


def fetch(force_ref, visc_ref, odd_ref, even_ref, sems):
    depth = visc_ref.shape[0]
    start = jnp.where(is_even("gz"), 0, depth - 2)
    moves = []
    for target, first in ((odd_ref, start), (even_ref, depth - 2 - start)):
        moves.append((force_ref.at[:, pl.ds(first, 2)], target.at[0:3]))
        moves.append((visc_ref.at[pl.ds(first, 2)], target.at[3]))
    copies = [pltpu.make_async_copy(source, target, sems.at[i]) for i, (source, target) in enumerate(moves)]
    for copy in copies:
        copy.start()
    for copy in copies:
        copy.wait()


def packed(plane, depth, field, left, right, lane):
    first = 8 * depth + 2 * field
    mask = lane // 2 == first // 2
    left = jnp.where(mask, rolled(plane, first), left)
    return left, jnp.where(mask, rolled(plane, first - 126), right)


def own_planes(force_ref, visc_ref, load_ref, sl_ref, sr_ref, planes_ref, left_ref, right_ref):
    lane = lanes((8, 128))
    left = jnp.zeros((8, 128), f32)
    right = jnp.zeros((8, 128), f32)
    depths = visc_ref.shape[0]
    for field in range(4):
        for depth in range(depths):
            plane = visc_ref[depth] if field == 3 else force_ref[field, depth]
            if field == 2 and depth == depths - 1:
                plane = plane + load_ref[...]
            planes_ref[field, depth] = plane
            left, right = packed(plane, depth + 2, field, left, right, lane)
    left_ref[0] = left
    right_ref[0] = right
    left_ref[1] = sl_ref[...]
    right_ref[1] = sr_ref[...]


def assemble(own_ref, odd_ref, even_ref, left_ref, right_ref, planes_ref, odd_out, even_out):
    upward = is_even("gz")
    lane = lanes((8, 128))
    left, right = left_ref[0], right_ref[0]
    for field in range(4):
        for depth in range(DEPTHS):
            p = field * DEPTHS + depth
            if 2 <= depth < DEPTHS - 2:
                planes_ref[p] = own_ref[field, depth - 2]
                continue
            if depth < 2:
                plane = jnp.where(upward, odd_ref[field, depth], even_ref[field, depth])
            else:
                i = depth - (DEPTHS - 2)
                plane = jnp.where(upward, even_ref[field, i], odd_ref[field, i])
            planes_ref[p] = plane
            left, right = packed(plane, depth, field, left, right, lane)
    rightward = is_even("gy")
    odd_out[0] = jnp.where(rightward, left, right)
    even_out[0] = jnp.where(rightward, right, left)
    odd_out[1] = jnp.where(rightward, left_ref[1], right_ref[1])
    even_out[1] = jnp.where(rightward, right_ref[1], left_ref[1])


def edge_rows(planes_ref, low_ref, high_ref):
    for depth in range(DEPTHS):
        for field in range(4):
            plane = planes_ref.at[field * DEPTHS + depth]
            near = 8 * depth + field
            low_ref[near : near + 1, :] = plane[0:1, :]
            low_ref[near + 4 : near + 5, :] = plane[1:2, :]
            high_ref[near : near + 1, :] = plane[7:8, :]
            high_ref[near + 4 : near + 5, :] = plane[6:7, :]


def prepare_rows(
    low_ref, high_ref, own_odd, own_even, odd_ref, even_ref, height_ref, conduct_ref,
    odd_out, even_out, column_ref, height_out, conduct_out,
):
    g = lax.axis_index("gz")
    last = lax.axis_size("gz") - 1
    lane = lanes((8, 128))
    rightward = is_even("gy")

    def chosen(first, second, i):
        return jnp.where(rightward, first[i], second[i])

    before, after = chosen(odd_ref, even_ref, 0), chosen(even_ref, odd_ref, 0)
    before_surface, after_surface = chosen(odd_ref, even_ref, 1), chosen(even_ref, odd_ref, 1)
    side = lax.rem(lane, 2) == 0
    levels = (
        jnp.where(side, chosen(own_odd, own_even, 0), chosen(own_even, own_odd, 0)),
        jnp.where(side, rolled(before, -1), rolled(after, 1)),
        jnp.where(side, before, after),
    )
    downward = is_even("gx")

    def send(rows, low, high):
        odd_out[rows, :] = jnp.where(downward, low, high)
        even_out[rows, :] = jnp.where(downward, high, low)

    for depth in range(DEPTHS):
        rows = slice(8 * depth, 8 * depth + 8)
        send(rows, low_ref[rows, :], high_ref[rows, :])
    pad = [jnp.zeros((2, 128), f32)]
    send(
        slice(COLUMN_ROW, SURFACE_ROW),
        jnp.concatenate([x[0:2] for x in levels] + pad, axis=0),
        jnp.concatenate([x[6:8] for x in levels] + pad, axis=0),
    )
    for i in range(3):
        column_ref[i] = levels[i]
    slot = 0
    for index, (source, target) in enumerate(((height_ref, height_out), (conduct_ref, conduct_out))):
        base = SURFACE_ROW + 16 * index
        for r in range(8):
            rows = slice(8 * r, 8 * r + 8)
            main = source[rows, 0:128]
            side = source[rows, 128:256]
            side = jnp.where((g == 0) & (lane >= 120), rolled(before_surface, 120 - 8 * slot), side)
            side = jnp.where((g == last) & (lane < 8), rolled(after_surface, -8 * slot), side)
            target[rows, 0:128] = main
            target[rows, 128:256] = side
            if r == 0:
                first = (main, side)
            if r == 7:
                send(slice(base, base + 8), first[0], main)
                send(slice(base + 8, base + 16), first[1], side)
            slot += 1


def weighted(before, here, after):
    outer = before + after
    return outer, FACE * here + EDGE * outer, EDGE * here + CORNER * outer


def pair(x):
    return rolled(x, 1, 0) + rolled(x, x.shape[0] - 1, 0)


def lane_pair(x, lane, first, last):
    return jnp.where(lane == 0, first, rolled(x, 1)) + jnp.where(lane == 127, last, rolled(x, 127))


def row_pair(x, row, edge, field):
    up = jnp.where(row == 0, rolled(edge, -field, 0), rolled(x, 1, 0))
    return up + jnp.where(row == 7, rolled(edge, 3 - field, 0), rolled(x, 7, 0))


def to_first(x, depth, field):
    return rolled(x, -(8 * depth + 2 * field))


def to_last(x, depth, field):
    return rolled(x, 126 - (8 * depth + 2 * field))


def spread_rows(x, row):
    field = lax.rem(row, 4)
    for f in range(3):
        x = jnp.where(field == f, rolled(x, f - 3, 0), x)
    return x


def spread_columns(x, lane):
    field = lax.rem(lane, 8) // 2
    for f in range(3):
        x = jnp.where(field == f, rolled(x, 2 * (f - 3)), x)
    return x


def column_sums(levels):
    parts = [weighted(rolled(x, 8), x, rolled(x, 120)) for x in levels]
    (_, ai, bi), (outer, an, bn), (_, af, bf) = parts
    beside = an + pair(bn)
    return FACE * outer + pair(an) + (ai + af) + pair(bi + bf), beside


def beside_rows(beside, depth, row):
    near = jnp.where(row < 4, jnp.broadcast_to(beside[15:16], (8, 128)), jnp.broadcast_to(beside[8:9], (8, 128)))
    field = lax.rem(row, 4)
    first, last = to_first(near, depth, 0), to_last(near, depth, 0)
    for f in range(1, 4):
        first = jnp.where(field == f, to_first(near, depth, f), first)
        last = jnp.where(field == f, to_last(near, depth, f), last)
    return first, last


def sided(odd_ref, even_ref, axis):
    first = is_even(axis)

    def before(rows):
        return jnp.where(first, odd_ref[rows, :], even_ref[rows, :])

    def after(rows):
        return jnp.where(first, even_ref[rows, :], odd_ref[rows, :])

    return before, after


def flux(conduct, slope):
    return conduct * slope * lax.rsqrt(1.0 + slope * slope)


def steps(h, k):
    rows = h.shape[0]
    inside = k > 0.0
    along = 0.5 * (k + rolled(k, 255, 1))
    along_before = rolled(along, 1, 1)
    across = 0.5 * (k + rolled(k, rows - 1, 0))
    for step in range(STEPS):
        q = flux(along, rolled(h, 255, 1) - h) - flux(along_before, h - rolled(h, 1, 1))
        r = flux(across, rolled(h, rows - 1, 0) - h)
        h = jnp.where(inside, h + TIME_STEP * (q + (r - rolled(r, 1, 0))), 0.0)
    return h


def inner_rows(height_ref, conduct_ref, out_ref):
    out_ref[...] = steps(height_ref[...], conduct_ref[...])[8:56, 0:128]


def operate(
    planes_ref, low_ref, high_ref, column_ref, odd_ref, even_ref, height_ref, conduct_ref, inner_ref,
    image_ref, sums_ref, top_ref, out_ref,
):
    lane = lanes((8, 128))
    row = lax.broadcasted_iota(jnp.int32, (8, 128), 0)
    wide = lanes((16, 128))
    before, after = sided(odd_ref, even_ref, "gx")

    def banded(source, base):
        def joined(side):
            return jnp.concatenate([side(slice(base, base + 8)), side(slice(base + 8, base + 16))], axis=1)

        return jnp.concatenate([source[48:64, :], joined(after), joined(before), source[0:16, :]], axis=0)

    band = steps(banded(height_ref, SURFACE_ROW), banded(conduct_ref, SURFACE_ROW + 16))
    out_ref[0:8, :] = band[32:40, 0:128]
    out_ref[8:56, :] = inner_ref[...]
    out_ref[56:64, :] = band[8:16, 0:128]
    columns = []
    for i in range(3):
        rows = slice(COLUMN_ROW + 2 * i, COLUMN_ROW + 2 * i + 2)
        columns.append(jnp.concatenate([column_ref[i], after(rows), jnp.zeros((4, 128), f32), before(rows)], axis=0))
    column_eta = [spread_columns(x, wide) for x in columns]
    column_sum, beside = column_sums(columns)
    column_sum_eta, beside_eta = column_sums([x * y for x, y in zip(columns, column_eta)])
    near_eta = column_eta[1]
    column_diag = DRAG + TOTAL * near_eta + spread_columns(column_sum, wide)
    column_image = columns[1] * column_diag - near_eta * column_sum - column_sum_eta
    column_image = jnp.where(near_eta > 0.0, column_image, 0.0)
    rows_of, rows_eta = [], []
    for depth in range(DEPTHS):
        rows = slice(8 * depth, 8 * depth + 8)
        b, a = before(rows), after(rows)
        found = (
            jnp.where(row < 4, low_ref[rows, :], rolled(high_ref[rows, :], 4, 0)),
            jnp.where(row < 4, b, rolled(a, 4, 0)),
            jnp.where(row < 4, rolled(b, 4, 0), a),
        )
        rows_of.append(found)
        rows_eta.append([spread_rows(x, row) for x in found])
    rows_product = [[x * y for x, y in zip(found, etas)] for found, etas in zip(rows_of, rows_eta)]

    def row_sums(levels, depth, beside_columns):
        parts = [weighted(levels[depth - 1][i], levels[depth][i], levels[depth + 1][i]) for i in range(3)]
        (_, ai, bi), (outer, an, bn), (_, af, bf) = parts
        first, last = beside_rows(beside_columns, depth, row)
        return FACE * outer + (ai + af) + lane_pair(an + (bi + bf), lane, first, last), an, bn

    def plane_sum(three, an, bn, beside_columns, depth, field):
        outer, a, b = weighted(*three)
        both = a + row_pair(b, row, bn, field)
        own = beside_columns[0:8]
        sides = lane_pair(both, lane, to_first(own, depth, field), to_last(own, depth, field))
        return FACE * outer + row_pair(a, row, an, field) + sides

    def plane(field, depth):
        return planes_ref[field * DEPTHS + depth]

    image, row_image, diagonal = {}, {}, {}
    for depth in range(1, DEPTHS - 1):
        row_sum, an, bn = row_sums(rows_of, depth, beside)
        row_sum_eta, an_eta, bn_eta = row_sums(rows_product, depth, beside_eta)
        near, eta = rows_of[depth][1], rows_eta[depth][1]
        diag = DRAG + TOTAL * eta + spread_rows(row_sum, row)
        row_image[depth] = jnp.where(eta > 0.0, near * diag - eta * row_sum - row_sum_eta, 0.0)
        e = [plane(3, depth + i) for i in (-1, 0, 1)]
        diag = DRAG + TOTAL * e[1] + plane_sum(e, an, bn, beside, depth, 3)
        diagonal[depth] = diag
        for c in range(3):
            v = [plane(c, depth + i) for i in (-1, 0, 1)]
            ev = [x * y for x, y in zip(e, v)]
            out = v[1] * diag - e[1] * plane_sum(v, an, bn, beside, depth, c)
            out = out - plane_sum(ev, an_eta, bn_eta, beside_eta, depth, c)
            image[c, depth] = jnp.where(e[1] > 0.0, out, 0.0)
    _, an, bn = weighted(rolled(column_image, 8), column_image, rolled(column_image, 120))
    beside = an + pair(bn)
    m = [jnp.zeros((8, 128), f32) for _ in range(4)]
    for depth in range(2, DEPTHS - 2):
        _, an, bn = weighted(row_image[depth - 1], row_image[depth], row_image[depth + 1])
        e = plane(3, depth)
        for c in range(3):
            s = plane_sum([image[c, depth + i] for i in (-1, 0, 1)], an, bn, beside, depth, c)
            v, q = plane(c, depth), image[c, depth]
            image_ref[c, depth - 2] = q
            m[0] = m[0] + v * v
            m[1] = m[1] + v * q
            m[2] = m[2] + q * q
            m[3] = m[3] + q * (q * diagonal[depth] - 2.0 * (e * s))
    total = jnp.zeros((8, 128), f32)
    for k in range(4):
        part = m[k]
        for amount in (64, 32, 16):
            part = part + rolled(part, amount)
        total = jnp.where(lane // 16 == 2 + k, part, total)
    for amount in (4, 2, 1):
        total = total + rolled(total, amount, 0)
    for i in range(sums_ref.shape[0] // 8):
        sums_ref[8 * i : 8 * i + 8, :] = total
    top_ref[0] = plane(2, DEPTHS - 3)
    top_ref[1] = image[2, DEPTHS - 3]


def middle(sums_ref, top_ref, out_ref):
    lane = lanes((8, 128))
    part = jnp.sum(sums_ref[...], axis=0, keepdims=True)
    base = jnp.broadcast_to(part, (8, 128))
    for j in range(out_ref.shape[0]):
        piece = jnp.where(lane < 16, rolled(top_ref[0], -16 * j), base)
        out_ref[j] = jnp.where(lane // 16 == 1, rolled(top_ref[1], 16 - 16 * j), piece)


def finish(parts_ref, planes_ref, image_ref, height_ref, velocity_ref, surface_ref):
    count = parts_ref.shape[0]
    lane = lanes((1, 128))
    total = parts_ref[0, 0:1, :]
    for j in range(1, count):
        total = total + parts_ref[j, 0:1, :]

    def moment(k):
        return jnp.sum(jnp.where(lane // 16 == 2 + k, total, 0.0), axis=1, keepdims=True)

    m0, m1, m2, m3 = (moment(k) for k in range(4))
    first = m0 / m1
    later = first * first * m2 - m0
    gain = 1.0 + later / m0
    second = later / (gain * gain * m1 - 2.0 * first * gain * m2 + first * first * m3)
    on_force = first + second * gain
    on_image = -(second * first)
    for c in range(3):
        for depth in range(8):
            velocity_ref[c, depth] = on_force * planes_ref[c * DEPTHS + depth + 2] + on_image * image_ref[c, depth]
    top = parts_ref[count - 1]
    rise = on_force * top + on_image * rolled(top, -16)
    spread = (
        lax.broadcasted_iota(jnp.int32, (128, 128), 1) // 8 == lax.broadcasted_iota(jnp.int32, (128, 128), 0)
    ).astype(f32)
    rise = jnp.where(lanes((8, 128)) < 16, rise, 0.0)
    wide = (STEPS * TIME_STEP) * jnp.dot(rise, spread, precision=lax.Precision.HIGHEST, preferred_element_type=f32)
    for r in range(8):
        rows = slice(8 * r, 8 * r + 8)
        surface_ref[rows, :] = height_ref[rows, :] + jnp.broadcast_to(wide[r : r + 1, :], (8, 128))


def swap(odd, even, axis):
    count = lax.axis_size(axis)

    def pairs(start):
        found = []
        for i in range(start, count - 1, 2):
            found += [(i, i + 1), (i + 1, i)]
        return found

    return lax.ppermute(odd, axis, pairs(1)), lax.ppermute(even, axis, pairs(0))


def local(body_force, viscosity, topography, kappa):
    odd, even = pl.pallas_call(
        fetch,
        out_shape=[jax.ShapeDtypeStruct((4, 2, 8, 128), f32)] * 2,
        in_specs=[pl.BlockSpec(memory_space=pltpu.HBM)] * 2,
        out_specs=[vmem()] * 2,
        scratch_shapes=[pltpu.SemaphoreType.DMA((4,))],
        compiler_params=pltpu.CompilerParams(vmem_limit_bytes=1 << 20),
    )(*[pltpu.with_memory_space_constraint(x, pltpu.HBM) for x in (body_force, viscosity)])
    odd, even = swap(odd, even, "gz")
    load, height, conduct, left, right = call(
        surface_own,
        [(8, 128), (64, 256), (64, 256), (8, 128), (8, 128)],
        (topography, kappa),
    )
    planes, left, right = call(
        own_planes,
        [(4, 8, 8, 128), (2, 8, 128), (2, 8, 128)],
        (body_force, viscosity, load, left, right),
    )
    planes, odd, even = call(
        assemble,
        [(PLANES, 8, 128), (2, 8, 128), (2, 8, 128)],
        (planes, odd, even, left, right),
    )
    own = (odd, even)
    odd, even = swap(odd, even, "gy")
    low, high = call(edge_rows, [(COLUMN_ROW, 128)] * 2, (planes,))
    odd, even, columns, height, conduct = call(
        prepare_rows,
        [(GX_ROWS, 128), (GX_ROWS, 128), (3, 8, 128), (64, 256), (64, 256)],
        (low, high, *own, odd, even, height, conduct),
    )
    odd, even = swap(odd, even, "gx")
    (inner,) = call(inner_rows, [(48, 128)], (height, conduct))
    group = lax.axis_size("gx") * lax.axis_size("gy")
    image, sums, top, height = call(
        operate,
        [(3, 8, 8, 128), (group, 128), (2, 8, 128), (64, 128)],
        (planes, low, high, columns, odd, even, height, conduct, inner),
    )
    sums = lax.all_to_all(sums.reshape(group, 1, 128), ("gx", "gy"), 0, 0)
    (parts,) = call(middle, [(lax.axis_size("gz"), 8, 128)], (sums.reshape(group, 128), top))
    parts = lax.all_to_all(parts, "gz", 0, 0)
    velocity, surface = call(
        finish, [(3, 8, 8, 128), (64, 128)], (parts, planes, image, height)
    )
    return velocity, surface


def solution(mesh):
    in_specs = (P(None, "gz", "gx", "gy"), P("gz", "gx", "gy"), P("gx", "gy"), P("gx", "gy"))
    out_specs = (P(None, "gz", "gx", "gy"), P("gx", ("gy", "gz")))
    return jax.shard_map(local, mesh=mesh, in_specs=in_specs, out_specs=out_specs, check_vma=False)
```

```python
import jax
import jax.numpy as jnp
from jax import lax
from jax.experimental import pallas as pl
from jax.experimental.pallas import tpu as pltpu
from jax.sharding import PartitionSpec as P

STEPS = 8
DRAG = 1.0
TIME_STEP = 1.0
LOAD_GAIN = 4.0
FACE, EDGE, CORNER = 0.5, 0.25, 0.5 / 3.0
TOTAL = 6 * FACE + 12 * EDGE + 8 * CORNER

DEPTHS = 12
PLANES = 4 * DEPTHS
COLUMN_ROW = 8 * DEPTHS
SURFACE_ROW = COLUMN_ROW + 8
GX_ROWS = SURFACE_ROW + 32

f32 = jnp.float32


def vmem():
    return pl.BlockSpec(memory_space=pltpu.VMEM)


def call(body, outs, ins, scratch=(), cost=20000, limit=8 << 20):
    return pl.pallas_call(
        body,
        out_shape=[jax.ShapeDtypeStruct(s, f32) for s in outs],
        in_specs=[vmem() for _ in ins],
        out_specs=[vmem() for _ in outs],
        scratch_shapes=list(scratch),
        compiler_params=pltpu.CompilerParams(vmem_limit_bytes=limit),
        cost_estimate=pl.CostEstimate(flops=cost * 1024, bytes_accessed=1 << 18, transcendentals=0),
    )(*ins)


def lanes(shape):
    return lax.broadcasted_iota(jnp.int32, shape, len(shape) - 1)


def rolled(x, amount, axis=1):
    amount = amount % x.shape[axis]
    return x if amount == 0 else pltpu.roll(x, amount, axis)


def own_block(
    force_hbm, visc_hbm, topo_hbm, kappa_hbm, planes_ref, left_ref, right_ref, height_ref, conduct_ref,
    force_ref, visc_ref, topo_ref, kappa_ref, sems,
):
    moves = ((topo_hbm, topo_ref), (kappa_hbm, kappa_ref), (force_hbm, force_ref), (visc_hbm, visc_ref))
    copies = [pltpu.make_async_copy(source, target, sems.at[i]) for i, (source, target) in enumerate(moves)]
    for copy in copies:
        copy.start()
    for copy in copies:
        copy.wait()
    g = lax.axis_index("gz")
    last = lax.axis_size("gz") - 1
    lane = lanes((8, 128))
    pieces = []
    for v in range(8):
        piece = topo_ref[:, 128 * v : 128 * v + 128].reshape(8, 8, 128)
        pieces.append(jnp.sum(piece, axis=1))
    stacked = jnp.concatenate(pieces, axis=0)
    pick = (
        lax.broadcasted_iota(jnp.int32, (128, 128), 0) // 8 == lax.broadcasted_iota(jnp.int32, (128, 128), 1)
    ).astype(f32)
    sums = jnp.dot(stacked, pick, precision=lax.Precision.HIGHEST, preferred_element_type=f32)
    load = jnp.zeros((8, 128), f32)
    for v in range(8):
        load = load + rolled(sums[8 * v : 8 * v + 8], 16 * v)
    load = jnp.where(g == last, load * (-LOAD_GAIN / 64.0), 0.0)
    wide = lanes((64, 128))
    own = pl.ds(pl.multiple_of(g * 128, 128), 128)
    before = pl.ds(pl.multiple_of(jnp.maximum(g - 1, 0) * 128, 128), 128)
    after = pl.ds(pl.multiple_of(jnp.minimum(g + 1, last) * 128, 128), 128)
    for source, target in ((topo_ref, height_ref), (kappa_ref, conduct_ref)):
        target[:, 0:128] = source[:, own].astype(f32)
        side = jnp.where((wide < 8) & (g < last), source[:, after].astype(f32), 0.0)
        side = jnp.where((wide >= 120) & (g > 0), source[:, before].astype(f32), side)
        target[:, 128:256] = side
    width = topo_ref.shape[1]
    left = jnp.zeros((8, 128), f32)
    right = jnp.zeros((8, 128), f32)
    slot = 0
    for source in (topo_ref, kappa_ref):
        head = source[:, 0:128].astype(f32)
        tail = source[:, width - 128 : width].astype(f32)
        for r in range(8):
            mask = lane // 8 == slot
            left = jnp.where(mask, rolled(head[8 * r : 8 * r + 8], 8 * slot), left)
            right = jnp.where(mask, rolled(tail[8 * r : 8 * r + 8], 8 * slot - 120), right)
            slot += 1
    left_ref[1] = left
    right_ref[1] = right
    left = jnp.zeros((8, 128), f32)
    right = jnp.zeros((8, 128), f32)
    depths = visc_ref.shape[0]
    for field in range(4):
        for depth in range(depths):
            plane = visc_ref[depth] if field == 3 else force_ref[field, depth]
            if field == 2 and depth == depths - 1:
                plane = plane + load
            planes_ref[field, depth] = plane
            left, right = packed(plane, depth + 2, field, left, right, lane)
    left_ref[0] = left
    right_ref[0] = right


def is_even(axis):
    return lax.rem(lax.axis_index(axis), 2) == 0


def fetch(force_ref, visc_ref, odd_ref, even_ref, sems):
    depth = visc_ref.shape[0]
    start = jnp.where(is_even("gz"), 0, depth - 2)
    moves = []
    for target, first in ((odd_ref, start), (even_ref, depth - 2 - start)):
        moves.append((force_ref.at[:, pl.ds(first, 2)], target.at[0:3]))
        moves.append((visc_ref.at[pl.ds(first, 2)], target.at[3]))
    copies = [pltpu.make_async_copy(source, target, sems.at[i]) for i, (source, target) in enumerate(moves)]
    for copy in copies:
        copy.start()
    for copy in copies:
        copy.wait()


def packed(plane, depth, field, left, right, lane):
    first = 8 * depth + 2 * field
    mask = lane // 2 == first // 2
    left = jnp.where(mask, rolled(plane, first), left)
    return left, jnp.where(mask, rolled(plane, first - 126), right)


def assemble(own_ref, odd_ref, even_ref, left_ref, right_ref, planes_ref, odd_out, even_out):
    upward = is_even("gz")
    lane = lanes((8, 128))
    left, right = left_ref[0], right_ref[0]
    for field in range(4):
        for depth in range(DEPTHS):
            p = field * DEPTHS + depth
            if 2 <= depth < DEPTHS - 2:
                planes_ref[p] = own_ref[field, depth - 2]
                continue
            if depth < 2:
                plane = jnp.where(upward, odd_ref[field, depth], even_ref[field, depth])
            else:
                i = depth - (DEPTHS - 2)
                plane = jnp.where(upward, even_ref[field, i], odd_ref[field, i])
            planes_ref[p] = plane
            left, right = packed(plane, depth, field, left, right, lane)
    rightward = is_even("gy")
    odd_out[0] = jnp.where(rightward, left, right)
    even_out[0] = jnp.where(rightward, right, left)
    odd_out[1] = jnp.where(rightward, left_ref[1], right_ref[1])
    even_out[1] = jnp.where(rightward, right_ref[1], left_ref[1])


def edge_rows(planes_ref, low_ref, high_ref):
    for depth in range(DEPTHS):
        for field in range(4):
            plane = planes_ref.at[field * DEPTHS + depth]
            near = 8 * depth + field
            low_ref[near : near + 1, :] = plane[0:1, :]
            low_ref[near + 4 : near + 5, :] = plane[1:2, :]
            high_ref[near : near + 1, :] = plane[7:8, :]
            high_ref[near + 4 : near + 5, :] = plane[6:7, :]


def prepare_rows(
    low_ref, high_ref, own_odd, own_even, odd_ref, even_ref, height_ref, conduct_ref,
    odd_out, even_out, column_ref, height_out, conduct_out,
):
    g = lax.axis_index("gz")
    last = lax.axis_size("gz") - 1
    lane = lanes((8, 128))
    rightward = is_even("gy")

    def chosen(first, second, i):
        return jnp.where(rightward, first[i], second[i])

    before, after = chosen(odd_ref, even_ref, 0), chosen(even_ref, odd_ref, 0)
    before_surface, after_surface = chosen(odd_ref, even_ref, 1), chosen(even_ref, odd_ref, 1)
    side = lax.rem(lane, 2) == 0
    levels = (
        jnp.where(side, chosen(own_odd, own_even, 0), chosen(own_even, own_odd, 0)),
        jnp.where(side, rolled(before, -1), rolled(after, 1)),
        jnp.where(side, before, after),
    )
    downward = is_even("gx")

    def send(rows, low, high):
        odd_out[rows, :] = jnp.where(downward, low, high)
        even_out[rows, :] = jnp.where(downward, high, low)

    for depth in range(DEPTHS):
        rows = slice(8 * depth, 8 * depth + 8)
        send(rows, low_ref[rows, :], high_ref[rows, :])
    pad = [jnp.zeros((2, 128), f32)]
    send(
        slice(COLUMN_ROW, SURFACE_ROW),
        jnp.concatenate([x[0:2] for x in levels] + pad, axis=0),
        jnp.concatenate([x[6:8] for x in levels] + pad, axis=0),
    )
    for i in range(3):
        column_ref[i] = levels[i]
    slot = 0
    for index, (source, target) in enumerate(((height_ref, height_out), (conduct_ref, conduct_out))):
        base = SURFACE_ROW + 16 * index
        for r in range(8):
            rows = slice(8 * r, 8 * r + 8)
            main = source[rows, 0:128]
            side = source[rows, 128:256]
            side = jnp.where((g == 0) & (lane >= 120), rolled(before_surface, 120 - 8 * slot), side)
            side = jnp.where((g == last) & (lane < 8), rolled(after_surface, -8 * slot), side)
            target[rows, 0:128] = main
            target[rows, 128:256] = side
            if r == 0:
                first = (main, side)
            if r == 7:
                send(slice(base, base + 8), first[0], main)
                send(slice(base + 8, base + 16), first[1], side)
            slot += 1


def weighted(before, here, after):
    outer = before + after
    return outer, FACE * here + EDGE * outer, EDGE * here + CORNER * outer


def pair(x):
    return rolled(x, 1, 0) + rolled(x, x.shape[0] - 1, 0)


def lane_pair(x, lane, first, last):
    return jnp.where(lane == 0, first, rolled(x, 1)) + jnp.where(lane == 127, last, rolled(x, 127))


def row_pair(x, row, edge, field):
    up = jnp.where(row == 0, rolled(edge, -field, 0), rolled(x, 1, 0))
    return up + jnp.where(row == 7, rolled(edge, 3 - field, 0), rolled(x, 7, 0))


def to_first(x, depth, field):
    return rolled(x, -(8 * depth + 2 * field))


def to_last(x, depth, field):
    return rolled(x, 126 - (8 * depth + 2 * field))


def spread_rows(x, row):
    field = lax.rem(row, 4)
    for f in range(3):
        x = jnp.where(field == f, rolled(x, f - 3, 0), x)
    return x


def spread_columns(x, lane):
    field = lax.rem(lane, 8) // 2
    for f in range(3):
        x = jnp.where(field == f, rolled(x, 2 * (f - 3)), x)
    return x


def column_sums(levels):
    parts = [weighted(rolled(x, 8), x, rolled(x, 120)) for x in levels]
    (_, ai, bi), (outer, an, bn), (_, af, bf) = parts
    beside = an + pair(bn)
    return FACE * outer + pair(an) + (ai + af) + pair(bi + bf), beside


def beside_rows(beside, depth, row):
    near = jnp.where(row < 4, jnp.broadcast_to(beside[15:16], (8, 128)), jnp.broadcast_to(beside[8:9], (8, 128)))
    field = lax.rem(row, 4)
    first, last = to_first(near, depth, 0), to_last(near, depth, 0)
    for f in range(1, 4):
        first = jnp.where(field == f, to_first(near, depth, f), first)
        last = jnp.where(field == f, to_last(near, depth, f), last)
    return first, last


def sided(odd_ref, even_ref, axis):
    first = is_even(axis)

    def before(rows):
        return jnp.where(first, odd_ref[rows, :], even_ref[rows, :])

    def after(rows):
        return jnp.where(first, even_ref[rows, :], odd_ref[rows, :])

    return before, after


def flux(conduct, slope):
    return conduct * slope * lax.rsqrt(1.0 + slope * slope)


def steps(h, k):
    rows = h.shape[0]
    inside = k > 0.0
    along = 0.5 * (k + rolled(k, 255, 1))
    along_before = rolled(along, 1, 1)
    across = 0.5 * (k + rolled(k, rows - 1, 0))
    for step in range(STEPS):
        q = flux(along, rolled(h, 255, 1) - h) - flux(along_before, h - rolled(h, 1, 1))
        r = flux(across, rolled(h, rows - 1, 0) - h)
        h = jnp.where(inside, h + TIME_STEP * (q + (r - rolled(r, 1, 0))), 0.0)
    return h


def inner_rows(height_ref, conduct_ref, out_ref):
    out_ref[...] = steps(height_ref[...], conduct_ref[...])[8:56, 0:128]


def operate(
    planes_ref, low_ref, high_ref, column_ref, odd_ref, even_ref, height_ref, conduct_ref, inner_ref,
    image_ref, sums_ref, top_ref, out_ref,
):
    lane = lanes((8, 128))
    row = lax.broadcasted_iota(jnp.int32, (8, 128), 0)
    wide = lanes((16, 128))
    before, after = sided(odd_ref, even_ref, "gx")

    def banded(source, base):
        def joined(side):
            return jnp.concatenate([side(slice(base, base + 8)), side(slice(base + 8, base + 16))], axis=1)

        return jnp.concatenate([source[48:64, :], joined(after), joined(before), source[0:16, :]], axis=0)

    band = steps(banded(height_ref, SURFACE_ROW), banded(conduct_ref, SURFACE_ROW + 16))
    out_ref[0:8, :] = band[32:40, 0:128]
    out_ref[8:56, :] = inner_ref[...]
    out_ref[56:64, :] = band[8:16, 0:128]
    columns = []
    for i in range(3):
        rows = slice(COLUMN_ROW + 2 * i, COLUMN_ROW + 2 * i + 2)
        columns.append(jnp.concatenate([column_ref[i], after(rows), jnp.zeros((4, 128), f32), before(rows)], axis=0))
    column_eta = [spread_columns(x, wide) for x in columns]
    column_sum, beside = column_sums(columns)
    column_sum_eta, beside_eta = column_sums([x * y for x, y in zip(columns, column_eta)])
    near_eta = column_eta[1]
    column_diag = DRAG + TOTAL * near_eta + spread_columns(column_sum, wide)
    column_image = columns[1] * column_diag - near_eta * column_sum - column_sum_eta
    column_image = jnp.where(near_eta > 0.0, column_image, 0.0)
    rows_of, rows_eta = [], []
    for depth in range(DEPTHS):
        rows = slice(8 * depth, 8 * depth + 8)
        b, a = before(rows), after(rows)
        found = (
            jnp.where(row < 4, low_ref[rows, :], rolled(high_ref[rows, :], 4, 0)),
            jnp.where(row < 4, b, rolled(a, 4, 0)),
            jnp.where(row < 4, rolled(b, 4, 0), a),
        )
        rows_of.append(found)
        rows_eta.append([spread_rows(x, row) for x in found])
    rows_product = [[x * y for x, y in zip(found, etas)] for found, etas in zip(rows_of, rows_eta)]

    def row_sums(levels, depth, beside_columns):
        parts = [weighted(levels[depth - 1][i], levels[depth][i], levels[depth + 1][i]) for i in range(3)]
        (_, ai, bi), (outer, an, bn), (_, af, bf) = parts
        first, last = beside_rows(beside_columns, depth, row)
        return FACE * outer + (ai + af) + lane_pair(an + (bi + bf), lane, first, last), an, bn

    def plane_sum(three, an, bn, beside_columns, depth, field):
        outer, a, b = weighted(*three)
        both = a + row_pair(b, row, bn, field)
        own = beside_columns[0:8]
        sides = lane_pair(both, lane, to_first(own, depth, field), to_last(own, depth, field))
        return FACE * outer + row_pair(a, row, an, field) + sides

    def plane(field, depth):
        return planes_ref[field * DEPTHS + depth]

    image, row_image, diagonal = {}, {}, {}
    for depth in range(1, DEPTHS - 1):
        row_sum, an, bn = row_sums(rows_of, depth, beside)
        row_sum_eta, an_eta, bn_eta = row_sums(rows_product, depth, beside_eta)
        near, eta = rows_of[depth][1], rows_eta[depth][1]
        diag = DRAG + TOTAL * eta + spread_rows(row_sum, row)
        row_image[depth] = jnp.where(eta > 0.0, near * diag - eta * row_sum - row_sum_eta, 0.0)
        e = [plane(3, depth + i) for i in (-1, 0, 1)]
        diag = DRAG + TOTAL * e[1] + plane_sum(e, an, bn, beside, depth, 3)
        diagonal[depth] = diag
        for c in range(3):
            v = [plane(c, depth + i) for i in (-1, 0, 1)]
            ev = [x * y for x, y in zip(e, v)]
            out = v[1] * diag - e[1] * plane_sum(v, an, bn, beside, depth, c)
            out = out - plane_sum(ev, an_eta, bn_eta, beside_eta, depth, c)
            image[c, depth] = jnp.where(e[1] > 0.0, out, 0.0)
    _, an, bn = weighted(rolled(column_image, 8), column_image, rolled(column_image, 120))
    beside = an + pair(bn)
    m = [jnp.zeros((8, 128), f32) for _ in range(4)]
    for depth in range(2, DEPTHS - 2):
        _, an, bn = weighted(row_image[depth - 1], row_image[depth], row_image[depth + 1])
        e = plane(3, depth)
        for c in range(3):
            s = plane_sum([image[c, depth + i] for i in (-1, 0, 1)], an, bn, beside, depth, c)
            v, q = plane(c, depth), image[c, depth]
            image_ref[c, depth - 2] = q
            m[0] = m[0] + v * v
            m[1] = m[1] + v * q
            m[2] = m[2] + q * q
            m[3] = m[3] + q * (q * diagonal[depth] - 2.0 * (e * s))
    total = jnp.zeros((8, 128), f32)
    for k in range(4):
        part = m[k]
        for amount in (64, 32, 16):
            part = part + rolled(part, amount)
        total = jnp.where(lane // 16 == 2 + k, part, total)
    for amount in (4, 2, 1):
        total = total + rolled(total, amount, 0)
    for i in range(sums_ref.shape[0] // 8):
        sums_ref[8 * i : 8 * i + 8, :] = total
    top_ref[0] = plane(2, DEPTHS - 3)
    top_ref[1] = image[2, DEPTHS - 3]


def middle(sums_ref, top_ref, out_ref):
    lane = lanes((8, 128))
    part = jnp.sum(sums_ref[...], axis=0, keepdims=True)
    base = jnp.broadcast_to(part, (8, 128))
    for j in range(out_ref.shape[0]):
        piece = jnp.where(lane < 16, rolled(top_ref[0], -16 * j), base)
        out_ref[j] = jnp.where(lane // 16 == 1, rolled(top_ref[1], 16 - 16 * j), piece)


def finish(parts_ref, planes_ref, image_ref, height_ref, velocity_ref, surface_ref):
    count = parts_ref.shape[0]
    lane = lanes((1, 128))
    total = parts_ref[0, 0:1, :]
    for j in range(1, count):
        total = total + parts_ref[j, 0:1, :]

    def moment(k):
        return jnp.sum(jnp.where(lane // 16 == 2 + k, total, 0.0), axis=1, keepdims=True)

    m0, m1, m2, m3 = (moment(k) for k in range(4))
    first = m0 / m1
    later = first * first * m2 - m0
    gain = 1.0 + later / m0
    second = later / (gain * gain * m1 - 2.0 * first * gain * m2 + first * first * m3)
    on_force = first + second * gain
    on_image = -(second * first)
    for c in range(3):
        for depth in range(8):
            velocity_ref[c, depth] = on_force * planes_ref[c * DEPTHS + depth + 2] + on_image * image_ref[c, depth]
    top = parts_ref[count - 1]
    rise = on_force * top + on_image * rolled(top, -16)
    spread = (
        lax.broadcasted_iota(jnp.int32, (128, 128), 1) // 8 == lax.broadcasted_iota(jnp.int32, (128, 128), 0)
    ).astype(f32)
    rise = jnp.where(lanes((8, 128)) < 16, rise, 0.0)
    wide = (STEPS * TIME_STEP) * jnp.dot(rise, spread, precision=lax.Precision.HIGHEST, preferred_element_type=f32)
    for r in range(8):
        rows = slice(8 * r, 8 * r + 8)
        surface_ref[rows, :] = height_ref[rows, :] + jnp.broadcast_to(wide[r : r + 1, :], (8, 128))


def swap(odd, even, axis):
    count = lax.axis_size(axis)

    def pairs(start):
        found = []
        for i in range(start, count - 1, 2):
            found += [(i, i + 1), (i + 1, i)]
        return found

    return lax.ppermute(odd, axis, pairs(1)), lax.ppermute(even, axis, pairs(0))


def local(body_force, viscosity, topography, kappa):
    inputs = [
        pltpu.with_memory_space_constraint(x, pltpu.HBM) for x in (body_force, viscosity, topography, kappa)
    ]
    odd, even = pl.pallas_call(
        fetch,
        out_shape=[jax.ShapeDtypeStruct((4, 2, 8, 128), f32)] * 2,
        in_specs=[pl.BlockSpec(memory_space=pltpu.HBM)] * 2,
        out_specs=[vmem()] * 2,
        scratch_shapes=[pltpu.SemaphoreType.DMA((4,))],
        compiler_params=pltpu.CompilerParams(vmem_limit_bytes=1 << 20),
    )(*inputs[:2])
    odd, even = swap(odd, even, "gz")
    planes, left, right, height, conduct = pl.pallas_call(
        own_block,
        out_shape=[
            jax.ShapeDtypeStruct(shape, f32)
            for shape in ((4, 8, 8, 128), (2, 8, 128), (2, 8, 128), (64, 256), (64, 256))
        ],
        in_specs=[pl.BlockSpec(memory_space=pltpu.HBM)] * 4,
        out_specs=[vmem()] * 5,
        scratch_shapes=[pltpu.VMEM(x.shape, x.dtype) for x in inputs] + [pltpu.SemaphoreType.DMA((4,))],
        compiler_params=pltpu.CompilerParams(vmem_limit_bytes=8 << 20),
        cost_estimate=pl.CostEstimate(flops=20000 * 1024, bytes_accessed=1 << 18, transcendentals=0),
    )(*inputs)
    planes, odd, even = call(
        assemble,
        [(PLANES, 8, 128), (2, 8, 128), (2, 8, 128)],
        (planes, odd, even, left, right),
    )
    own = (odd, even)
    odd, even = swap(odd, even, "gy")
    low, high = call(edge_rows, [(COLUMN_ROW, 128)] * 2, (planes,))
    odd, even, columns, height, conduct = call(
        prepare_rows,
        [(GX_ROWS, 128), (GX_ROWS, 128), (3, 8, 128), (64, 256), (64, 256)],
        (low, high, *own, odd, even, height, conduct),
    )
    odd, even = swap(odd, even, "gx")
    (inner,) = call(inner_rows, [(48, 128)], (height, conduct))
    group = lax.axis_size("gx") * lax.axis_size("gy")
    image, sums, top, height = call(
        operate,
        [(3, 8, 8, 128), (group, 128), (2, 8, 128), (64, 128)],
        (planes, low, high, columns, odd, even, height, conduct, inner),
    )
    sums = lax.all_to_all(sums.reshape(group, 1, 128), ("gx", "gy"), 0, 0)
    (parts,) = call(middle, [(lax.axis_size("gz"), 8, 128)], (sums.reshape(group, 128), top))
    parts = lax.all_to_all(parts, "gz", 0, 0)
    velocity, surface = call(
        finish, [(3, 8, 8, 128), (64, 128)], (parts, planes, image, height)
    )
    return velocity, surface


def solution(mesh):
    in_specs = (P(None, "gz", "gx", "gy"), P("gz", "gx", "gy"), P("gx", "gy"), P("gx", "gy"))
    out_specs = (P(None, "gz", "gx", "gy"), P("gx", ("gy", "gz")))
    return jax.shard_map(local, mesh=mesh, in_specs=in_specs, out_specs=out_specs, check_vma=False)
```

```python
import jax
import jax.numpy as jnp
from jax import lax
from jax.experimental import pallas as pl
from jax.experimental.pallas import tpu as pltpu
from jax.sharding import PartitionSpec as P

STEPS = 8
DRAG = 1.0
TIME_STEP = 1.0
LOAD_GAIN = 4.0
FACE, EDGE, CORNER = 0.5, 0.25, 0.5 / 3.0
TOTAL = 6 * FACE + 12 * EDGE + 8 * CORNER

DEPTHS = 12
PLANES = 4 * DEPTHS
COLUMN_ROW = 8 * DEPTHS
SURFACE_ROW = COLUMN_ROW + 8
GX_ROWS = SURFACE_ROW + 32

f32 = jnp.float32


def vmem():
    return pl.BlockSpec(memory_space=pltpu.VMEM)


def call(body, outs, ins, scratch=(), cost=20000, limit=8 << 20):
    return pl.pallas_call(
        body,
        out_shape=[jax.ShapeDtypeStruct(s, f32) for s in outs],
        in_specs=[vmem() for _ in ins],
        out_specs=[vmem() for _ in outs],
        scratch_shapes=list(scratch),
        compiler_params=pltpu.CompilerParams(vmem_limit_bytes=limit),
        cost_estimate=pl.CostEstimate(flops=cost * 1024, bytes_accessed=1 << 18, transcendentals=0),
    )(*ins)


def lanes(shape):
    return lax.broadcasted_iota(jnp.int32, shape, len(shape) - 1)


def rolled(x, amount, axis=1):
    amount = amount % x.shape[axis]
    return x if amount == 0 else pltpu.roll(x, amount, axis)


def own_block(
    force_hbm, visc_hbm, topo_hbm, kappa_hbm, planes_ref, left_ref, right_ref, height_ref, conduct_ref,
    force_ref, visc_ref, topo_ref, kappa_ref, sems,
):
    moves = ((topo_hbm, topo_ref), (kappa_hbm, kappa_ref), (force_hbm, force_ref), (visc_hbm, visc_ref))
    copies = [pltpu.make_async_copy(source, target, sems.at[i]) for i, (source, target) in enumerate(moves)]
    for copy in copies:
        copy.start()
    for copy in copies:
        copy.wait()
    g = lax.axis_index("gz")
    last = lax.axis_size("gz") - 1
    lane = lanes((8, 128))
    pieces = []
    for v in range(8):
        piece = topo_ref[:, 128 * v : 128 * v + 128].reshape(8, 8, 128)
        pieces.append(jnp.sum(piece, axis=1))
    stacked = jnp.concatenate(pieces, axis=0)
    pick = (
        lax.broadcasted_iota(jnp.int32, (128, 128), 0) // 8 == lax.broadcasted_iota(jnp.int32, (128, 128), 1)
    ).astype(f32)
    sums = jnp.dot(stacked, pick, precision=lax.Precision.HIGHEST, preferred_element_type=f32)
    load = jnp.zeros((8, 128), f32)
    for v in range(8):
        load = load + rolled(sums[8 * v : 8 * v + 8], 16 * v)
    load = jnp.where(g == last, load * (-LOAD_GAIN / 64.0), 0.0)
    wide = lanes((64, 128))
    own = pl.ds(pl.multiple_of(g * 128, 128), 128)
    before = pl.ds(pl.multiple_of(jnp.maximum(g - 1, 0) * 128, 128), 128)
    after = pl.ds(pl.multiple_of(jnp.minimum(g + 1, last) * 128, 128), 128)
    for source, target in ((topo_ref, height_ref), (kappa_ref, conduct_ref)):
        target[:, 0:128] = source[:, own].astype(f32)
        side = jnp.where((wide < 8) & (g < last), source[:, after].astype(f32), 0.0)
        side = jnp.where((wide >= 120) & (g > 0), source[:, before].astype(f32), side)
        target[:, 128:256] = side
    width = topo_ref.shape[1]
    left = jnp.zeros((8, 128), f32)
    right = jnp.zeros((8, 128), f32)
    slot = 0
    for source in (topo_ref, kappa_ref):
        head = source[:, 0:128].astype(f32)
        tail = source[:, width - 128 : width].astype(f32)
        for r in range(8):
            mask = lane // 8 == slot
            left = jnp.where(mask, rolled(head[8 * r : 8 * r + 8], 8 * slot), left)
            right = jnp.where(mask, rolled(tail[8 * r : 8 * r + 8], 8 * slot - 120), right)
            slot += 1
    left_ref[1] = left
    right_ref[1] = right
    left = jnp.zeros((8, 128), f32)
    right = jnp.zeros((8, 128), f32)
    depths = visc_ref.shape[0]
    for field in range(4):
        for depth in range(depths):
            plane = visc_ref[depth] if field == 3 else force_ref[field, depth]
            if field == 2 and depth == depths - 1:
                plane = plane + load
            planes_ref[field, depth] = plane
            left, right = packed(plane, depth + 2, field, left, right, lane)
    left_ref[0] = left
    right_ref[0] = right


def is_even(axis):
    return lax.rem(lax.axis_index(axis), 2) == 0


def fetch(force_ref, visc_ref, odd_ref, even_ref, sems):
    depth = visc_ref.shape[0]
    start = jnp.where(is_even("gz"), 0, depth - 2)
    moves = []
    for target, first in ((odd_ref, start), (even_ref, depth - 2 - start)):
        moves.append((force_ref.at[:, pl.ds(first, 2)], target.at[0:3]))
        moves.append((visc_ref.at[pl.ds(first, 2)], target.at[3]))
    copies = [pltpu.make_async_copy(source, target, sems.at[i]) for i, (source, target) in enumerate(moves)]
    for copy in copies:
        copy.start()
    for copy in copies:
        copy.wait()


def packed(plane, depth, field, left, right, lane):
    first = 8 * depth + 2 * field
    mask = lane // 2 == first // 2
    left = jnp.where(mask, rolled(plane, first), left)
    return left, jnp.where(mask, rolled(plane, first - 126), right)


def assemble(own_ref, odd_ref, even_ref, left_ref, right_ref, planes_ref, odd_out, even_out):
    upward = is_even("gz")
    lane = lanes((8, 128))
    left, right = left_ref[0], right_ref[0]
    for field in range(4):
        for depth in range(DEPTHS):
            p = field * DEPTHS + depth
            if 2 <= depth < DEPTHS - 2:
                planes_ref[p] = own_ref[field, depth - 2]
                continue
            if depth < 2:
                plane = jnp.where(upward, odd_ref[field, depth], even_ref[field, depth])
            else:
                i = depth - (DEPTHS - 2)
                plane = jnp.where(upward, even_ref[field, i], odd_ref[field, i])
            planes_ref[p] = plane
            left, right = packed(plane, depth, field, left, right, lane)
    rightward = is_even("gy")
    odd_out[0] = jnp.where(rightward, left, right)
    even_out[0] = jnp.where(rightward, right, left)
    odd_out[1] = jnp.where(rightward, left_ref[1], right_ref[1])
    even_out[1] = jnp.where(rightward, right_ref[1], left_ref[1])


def edge_rows(planes_ref, low_ref, high_ref):
    for depth in range(DEPTHS):
        for field in range(4):
            plane = planes_ref.at[field * DEPTHS + depth]
            near = 8 * depth + field
            low_ref[near : near + 1, :] = plane[0:1, :]
            low_ref[near + 4 : near + 5, :] = plane[1:2, :]
            high_ref[near : near + 1, :] = plane[7:8, :]
            high_ref[near + 4 : near + 5, :] = plane[6:7, :]


def prepare_rows(
    low_ref, high_ref, own_odd, own_even, odd_ref, even_ref, height_ref, conduct_ref,
    odd_out, even_out, column_ref, height_out, conduct_out,
):
    g = lax.axis_index("gz")
    last = lax.axis_size("gz") - 1
    lane = lanes((8, 128))
    rightward = is_even("gy")

    def chosen(first, second, i):
        return jnp.where(rightward, first[i], second[i])

    before, after = chosen(odd_ref, even_ref, 0), chosen(even_ref, odd_ref, 0)
    before_surface, after_surface = chosen(odd_ref, even_ref, 1), chosen(even_ref, odd_ref, 1)
    side = lax.rem(lane, 2) == 0
    levels = (
        jnp.where(side, chosen(own_odd, own_even, 0), chosen(own_even, own_odd, 0)),
        jnp.where(side, rolled(before, -1), rolled(after, 1)),
        jnp.where(side, before, after),
    )
    downward = is_even("gx")

    def send(rows, low, high):
        odd_out[rows, :] = jnp.where(downward, low, high)
        even_out[rows, :] = jnp.where(downward, high, low)

    for depth in range(DEPTHS):
        rows = slice(8 * depth, 8 * depth + 8)
        send(rows, low_ref[rows, :], high_ref[rows, :])
    pad = [jnp.zeros((2, 128), f32)]
    send(
        slice(COLUMN_ROW, SURFACE_ROW),
        jnp.concatenate([x[0:2] for x in levels] + pad, axis=0),
        jnp.concatenate([x[6:8] for x in levels] + pad, axis=0),
    )
    for i in range(3):
        column_ref[i] = levels[i]
    slot = 0
    for index, (source, target) in enumerate(((height_ref, height_out), (conduct_ref, conduct_out))):
        base = SURFACE_ROW + 16 * index
        for r in range(8):
            rows = slice(8 * r, 8 * r + 8)
            main = source[rows, 0:128]
            side = source[rows, 128:256]
            side = jnp.where((g == 0) & (lane >= 120), rolled(before_surface, 120 - 8 * slot), side)
            side = jnp.where((g == last) & (lane < 8), rolled(after_surface, -8 * slot), side)
            target[rows, 0:128] = main
            target[rows, 128:256] = side
            if r == 0:
                first = (main, side)
            if r == 7:
                send(slice(base, base + 8), first[0], main)
                send(slice(base + 8, base + 16), first[1], side)
            slot += 1


def weighted(before, here, after):
    outer = before + after
    return outer, FACE * here + EDGE * outer, EDGE * here + CORNER * outer


def pair(x):
    return rolled(x, 1, 0) + rolled(x, x.shape[0] - 1, 0)


def lane_pair(x, lane, first, last):
    return jnp.where(lane == 0, first, rolled(x, 1)) + jnp.where(lane == 127, last, rolled(x, 127))


def row_pair(x, row, edge, field):
    up = jnp.where(row == 0, rolled(edge, -field, 0), rolled(x, 1, 0))
    return up + jnp.where(row == 7, rolled(edge, 3 - field, 0), rolled(x, 7, 0))


def to_first(x, depth, field):
    return rolled(x, -(8 * depth + 2 * field))


def to_last(x, depth, field):
    return rolled(x, 126 - (8 * depth + 2 * field))


def spread_rows(x, row):
    field = lax.rem(row, 4)
    for f in range(3):
        x = jnp.where(field == f, rolled(x, f - 3, 0), x)
    return x


def spread_columns(x, lane):
    field = lax.rem(lane, 8) // 2
    for f in range(3):
        x = jnp.where(field == f, rolled(x, 2 * (f - 3)), x)
    return x


def column_sums(levels):
    parts = [weighted(rolled(x, 8), x, rolled(x, 120)) for x in levels]
    (_, ai, bi), (outer, an, bn), (_, af, bf) = parts
    beside = an + pair(bn)
    return FACE * outer + pair(an) + (ai + af) + pair(bi + bf), beside


def beside_rows(beside, depth, row):
    near = jnp.where(row < 4, jnp.broadcast_to(beside[15:16], (8, 128)), jnp.broadcast_to(beside[8:9], (8, 128)))
    field = lax.rem(row, 4)
    first, last = to_first(near, depth, 0), to_last(near, depth, 0)
    for f in range(1, 4):
        first = jnp.where(field == f, to_first(near, depth, f), first)
        last = jnp.where(field == f, to_last(near, depth, f), last)
    return first, last


def sided(odd_ref, even_ref, axis):
    first = is_even(axis)

    def before(rows):
        return jnp.where(first, odd_ref[rows, :], even_ref[rows, :])

    def after(rows):
        return jnp.where(first, even_ref[rows, :], odd_ref[rows, :])

    return before, after


def flux(conduct, slope):
    return conduct * slope * lax.rsqrt(1.0 + slope * slope)


def steps(h, k):
    rows = h.shape[0]
    inside = k > 0.0
    along = 0.5 * (k + rolled(k, 255, 1))
    along_before = rolled(along, 1, 1)
    across = 0.5 * (k + rolled(k, rows - 1, 0))
    for step in range(STEPS):
        q = flux(along, rolled(h, 255, 1) - h) - flux(along_before, h - rolled(h, 1, 1))
        r = flux(across, rolled(h, rows - 1, 0) - h)
        h = jnp.where(inside, h + TIME_STEP * (q + (r - rolled(r, 1, 0))), 0.0)
    return h


def inner_rows(height_ref, conduct_ref, out_ref):
    out_ref[...] = steps(height_ref[...], conduct_ref[...])[8:56, 0:128]


def operate(
    planes_ref, low_ref, high_ref, column_ref, odd_ref, even_ref, height_ref, conduct_ref, inner_ref,
    image_ref, sums_ref, top_ref, out_ref,
):
    lane = lanes((8, 128))
    row = lax.broadcasted_iota(jnp.int32, (8, 128), 0)
    wide = lanes((16, 128))
    before, after = sided(odd_ref, even_ref, "gx")

    def banded(source, base):
        def joined(side):
            return jnp.concatenate([side(slice(base, base + 8)), side(slice(base + 8, base + 16))], axis=1)

        return jnp.concatenate([source[48:64, :], joined(after), joined(before), source[0:16, :]], axis=0)

    band = steps(banded(height_ref, SURFACE_ROW), banded(conduct_ref, SURFACE_ROW + 16))
    out_ref[0:8, :] = band[32:40, 0:128]
    out_ref[8:56, :] = inner_ref[...]
    out_ref[56:64, :] = band[8:16, 0:128]
    columns = []
    for i in range(3):
        rows = slice(COLUMN_ROW + 2 * i, COLUMN_ROW + 2 * i + 2)
        columns.append(jnp.concatenate([column_ref[i], after(rows), jnp.zeros((4, 128), f32), before(rows)], axis=0))
    column_eta = [spread_columns(x, wide) for x in columns]
    column_sum, beside = column_sums(columns)
    column_sum_eta, beside_eta = column_sums([x * y for x, y in zip(columns, column_eta)])
    near_eta = column_eta[1]
    column_diag = DRAG + TOTAL * near_eta + spread_columns(column_sum, wide)
    column_image = columns[1] * column_diag - near_eta * column_sum - column_sum_eta
    column_image = jnp.where(near_eta > 0.0, column_image, 0.0)
    rows_of, rows_eta = [], []
    for depth in range(DEPTHS):
        rows = slice(8 * depth, 8 * depth + 8)
        b, a = before(rows), after(rows)
        found = (
            jnp.where(row < 4, low_ref[rows, :], rolled(high_ref[rows, :], 4, 0)),
            jnp.where(row < 4, b, rolled(a, 4, 0)),
            jnp.where(row < 4, rolled(b, 4, 0), a),
        )
        rows_of.append(found)
        rows_eta.append([spread_rows(x, row) for x in found])
    rows_product = [[x * y for x, y in zip(found, etas)] for found, etas in zip(rows_of, rows_eta)]

    def row_sums(levels, depth, beside_columns):
        parts = [weighted(levels[depth - 1][i], levels[depth][i], levels[depth + 1][i]) for i in range(3)]
        (_, ai, bi), (outer, an, bn), (_, af, bf) = parts
        first, last = beside_rows(beside_columns, depth, row)
        return FACE * outer + (ai + af) + lane_pair(an + (bi + bf), lane, first, last), an, bn

    def plane_sum(three, an, bn, beside_columns, depth, field):
        outer, a, b = weighted(*three)
        both = a + row_pair(b, row, bn, field)
        own = beside_columns[0:8]
        sides = lane_pair(both, lane, to_first(own, depth, field), to_last(own, depth, field))
        return FACE * outer + row_pair(a, row, an, field) + sides

    def plane(field, depth):
        return planes_ref[field * DEPTHS + depth]

    image, row_image, diagonal = {}, {}, {}
    for depth in range(1, DEPTHS - 1):
        row_sum, an, bn = row_sums(rows_of, depth, beside)
        row_sum_eta, an_eta, bn_eta = row_sums(rows_product, depth, beside_eta)
        near, eta = rows_of[depth][1], rows_eta[depth][1]
        diag = DRAG + TOTAL * eta + spread_rows(row_sum, row)
        row_image[depth] = jnp.where(eta > 0.0, near * diag - eta * row_sum - row_sum_eta, 0.0)
        e = [plane(3, depth + i) for i in (-1, 0, 1)]
        diag = DRAG + TOTAL * e[1] + plane_sum(e, an, bn, beside, depth, 3)
        diagonal[depth] = diag
        for c in range(3):
            v = [plane(c, depth + i) for i in (-1, 0, 1)]
            ev = [x * y for x, y in zip(e, v)]
            out = v[1] * diag - e[1] * plane_sum(v, an, bn, beside, depth, c)
            out = out - plane_sum(ev, an_eta, bn_eta, beside_eta, depth, c)
            image[c, depth] = jnp.where(e[1] > 0.0, out, 0.0)
    _, an, bn = weighted(rolled(column_image, 8), column_image, rolled(column_image, 120))
    beside = an + pair(bn)
    m = [jnp.zeros((8, 128), f32) for _ in range(4)]
    for depth in range(2, DEPTHS - 2):
        _, an, bn = weighted(row_image[depth - 1], row_image[depth], row_image[depth + 1])
        e = plane(3, depth)
        for c in range(3):
            s = plane_sum([image[c, depth + i] for i in (-1, 0, 1)], an, bn, beside, depth, c)
            v, q = plane(c, depth), image[c, depth]
            image_ref[c, depth - 2] = q
            m[0] = m[0] + v * v
            m[1] = m[1] + v * q
            m[2] = m[2] + q * q
            m[3] = m[3] + q * (q * diagonal[depth] - 2.0 * (e * s))
    total = jnp.zeros((8, 128), f32)
    for k in range(4):
        part = m[k]
        for amount in (64, 32, 16):
            part = part + rolled(part, amount)
        total = jnp.where(lane // 16 == 2 + k, part, total)
    for amount in (4, 2, 1):
        total = total + rolled(total, amount, 0)
    for i in range(sums_ref.shape[0] // 8):
        sums_ref[8 * i : 8 * i + 8, :] = total
    top_ref[0] = plane(2, DEPTHS - 3)
    top_ref[1] = image[2, DEPTHS - 3]


def middle(sums_ref, top_ref, out_ref):
    lane = lanes((8, 128))
    part = jnp.sum(sums_ref[...], axis=0, keepdims=True)
    base = jnp.broadcast_to(part, (8, 128))
    for j in range(out_ref.shape[0]):
        piece = jnp.where(lane < 16, rolled(top_ref[0], -16 * j), base)
        out_ref[j] = jnp.where(lane // 16 == 1, rolled(top_ref[1], 16 - 16 * j), piece)


def finish(parts_ref, planes_ref, image_ref, height_ref, velocity_hbm, surface_hbm, velocity_ref, surface_ref, sems):
    count = parts_ref.shape[0]
    lane = lanes((1, 128))
    top = parts_ref[count - 1]
    top = jnp.where(lanes((16, 128)) < 16, jnp.concatenate([top, rolled(top, -16)], axis=0), 0.0)
    spread = (
        lax.broadcasted_iota(jnp.int32, (128, 128), 1) // 8 == lax.broadcasted_iota(jnp.int32, (128, 128), 0)
    ).astype(f32)
    wide = jnp.dot(top, spread, precision=lax.Precision.HIGHEST, preferred_element_type=f32)
    total = parts_ref[0, 0:1, :]
    for j in range(1, count):
        total = total + parts_ref[j, 0:1, :]

    def moment(k):
        return jnp.sum(jnp.where(lane // 16 == 2 + k, total, 0.0), axis=1, keepdims=True)

    m0, m1, m2, m3 = (moment(k) for k in range(4))
    first = m0 / m1
    later = first * first * m2 - m0
    gain = 1.0 + later / m0
    second = later / (gain * gain * m1 - 2.0 * first * gain * m2 + first * first * m3)
    on_force = first + second * gain
    on_image = -(second * first)
    for c in range(3):
        for depth in range(8):
            velocity_ref[c, depth] = on_force * planes_ref[c * DEPTHS + depth + 2] + on_image * image_ref[c, depth]
    velocity_copy = pltpu.make_async_copy(velocity_ref, velocity_hbm, sems.at[0])
    velocity_copy.start()
    rise = (STEPS * TIME_STEP) * (on_force * wide[0:8] + on_image * wide[8:16])
    for r in range(8):
        rows = slice(8 * r, 8 * r + 8)
        surface_ref[rows, :] = height_ref[rows, :] + jnp.broadcast_to(rise[r : r + 1, :], (8, 128))
    surface_copy = pltpu.make_async_copy(surface_ref, surface_hbm, sems.at[1])
    surface_copy.start()
    velocity_copy.wait()
    surface_copy.wait()


def swap(odd, even, axis):
    count = lax.axis_size(axis)

    def pairs(start):
        found = []
        for i in range(start, count - 1, 2):
            found += [(i, i + 1), (i + 1, i)]
        return found

    return lax.ppermute(odd, axis, pairs(1)), lax.ppermute(even, axis, pairs(0))


def local(body_force, viscosity, topography, kappa):
    inputs = [
        pltpu.with_memory_space_constraint(x, pltpu.HBM) for x in (body_force, viscosity, topography, kappa)
    ]
    odd, even = pl.pallas_call(
        fetch,
        out_shape=[jax.ShapeDtypeStruct((4, 2, 8, 128), f32)] * 2,
        in_specs=[pl.BlockSpec(memory_space=pltpu.HBM)] * 2,
        out_specs=[vmem()] * 2,
        scratch_shapes=[pltpu.SemaphoreType.DMA((4,))],
        compiler_params=pltpu.CompilerParams(vmem_limit_bytes=1 << 20),
    )(*inputs[:2])
    odd, even = swap(odd, even, "gz")
    planes, left, right, height, conduct = pl.pallas_call(
        own_block,
        out_shape=[
            jax.ShapeDtypeStruct(shape, f32)
            for shape in ((4, 8, 8, 128), (2, 8, 128), (2, 8, 128), (64, 256), (64, 256))
        ],
        in_specs=[pl.BlockSpec(memory_space=pltpu.HBM)] * 4,
        out_specs=[vmem()] * 5,
        scratch_shapes=[pltpu.VMEM(x.shape, x.dtype) for x in inputs] + [pltpu.SemaphoreType.DMA((4,))],
        compiler_params=pltpu.CompilerParams(vmem_limit_bytes=8 << 20),
        cost_estimate=pl.CostEstimate(flops=20000 * 1024, bytes_accessed=1 << 18, transcendentals=0),
    )(*inputs)
    planes, odd, even = call(
        assemble,
        [(PLANES, 8, 128), (2, 8, 128), (2, 8, 128)],
        (planes, odd, even, left, right),
    )
    own = (odd, even)
    odd, even = swap(odd, even, "gy")
    low, high = call(edge_rows, [(COLUMN_ROW, 128)] * 2, (planes,))
    odd, even, columns, height, conduct = call(
        prepare_rows,
        [(GX_ROWS, 128), (GX_ROWS, 128), (3, 8, 128), (64, 256), (64, 256)],
        (low, high, *own, odd, even, height, conduct),
    )
    odd, even = swap(odd, even, "gx")
    (inner,) = call(inner_rows, [(48, 128)], (height, conduct))
    group = lax.axis_size("gx") * lax.axis_size("gy")
    image, sums, top, height = call(
        operate,
        [(3, 8, 8, 128), (group, 128), (2, 8, 128), (64, 128)],
        (planes, low, high, columns, odd, even, height, conduct, inner),
    )
    sums = lax.all_to_all(sums.reshape(group, 1, 128), ("gx", "gy"), 0, 0)
    (parts,) = call(middle, [(lax.axis_size("gz"), 8, 128)], (sums.reshape(group, 128), top))
    parts = lax.all_to_all(parts, "gz", 0, 0)
    shapes = ((3, 8, 8, 128), (64, 128))
    velocity, surface = pl.pallas_call(
        finish,
        out_shape=[jax.ShapeDtypeStruct(shape, f32) for shape in shapes],
        in_specs=[vmem()] * 4,
        out_specs=[pl.BlockSpec(memory_space=pltpu.HBM)] * 2,
        scratch_shapes=[pltpu.VMEM(shape, f32) for shape in shapes] + [pltpu.SemaphoreType.DMA((2,))],
        compiler_params=pltpu.CompilerParams(vmem_limit_bytes=8 << 20),
    )(parts, planes, image, height)
    return velocity, surface


def solution(mesh):
    in_specs = (P(None, "gz", "gx", "gy"), P("gz", "gx", "gy"), P("gx", "gy"), P("gx", "gy"))
    out_specs = (P(None, "gz", "gx", "gy"), P("gx", ("gy", "gz")))
    return jax.shard_map(local, mesh=mesh, in_specs=in_specs, out_specs=out_specs, check_vma=False)
```

```python
import jax
import jax.numpy as jnp
from jax import lax
from jax.experimental import pallas as pl
from jax.experimental.pallas import tpu as pltpu
from jax.sharding import PartitionSpec as P

STEPS = 8
DRAG = 1.0
TIME_STEP = 1.0
LOAD_GAIN = 4.0
FACE, EDGE, CORNER = 0.5, 0.25, 0.5 / 3.0
TOTAL = 6 * FACE + 12 * EDGE + 8 * CORNER

DEPTHS = 12
PLANES = 4 * DEPTHS
COLUMN_ROW = 8 * DEPTHS
SURFACE_ROW = COLUMN_ROW + 8
GX_ROWS = SURFACE_ROW + 32

f32 = jnp.float32


def vmem():
    return pl.BlockSpec(memory_space=pltpu.VMEM)


def call(body, outs, ins, scratch=(), cost=20000, limit=8 << 20):
    return pl.pallas_call(
        body,
        out_shape=[jax.ShapeDtypeStruct(s, f32) for s in outs],
        in_specs=[vmem() for _ in ins],
        out_specs=[vmem() for _ in outs],
        scratch_shapes=list(scratch),
        compiler_params=pltpu.CompilerParams(vmem_limit_bytes=limit),
        cost_estimate=pl.CostEstimate(flops=cost * 1024, bytes_accessed=1 << 18, transcendentals=0),
    )(*ins)


def lanes(shape):
    return lax.broadcasted_iota(jnp.int32, shape, len(shape) - 1)


def rolled(x, amount, axis=1):
    amount = amount % x.shape[axis]
    return x if amount == 0 else pltpu.roll(x, amount, axis)


def own_block(
    force_hbm, visc_hbm, topo_hbm, kappa_hbm, planes_ref, left_ref, right_ref, height_ref, conduct_ref,
    force_ref, visc_ref, topo_ref, kappa_ref, sems,
):
    moves = ((topo_hbm, topo_ref), (kappa_hbm, kappa_ref), (force_hbm, force_ref), (visc_hbm, visc_ref))
    copies = [pltpu.make_async_copy(source, target, sems.at[i]) for i, (source, target) in enumerate(moves)]
    for copy in copies:
        copy.start()
    for copy in copies:
        copy.wait()
    g = lax.axis_index("gz")
    last = lax.axis_size("gz") - 1
    lane = lanes((8, 128))
    pieces = []
    for v in range(8):
        piece = topo_ref[:, 128 * v : 128 * v + 128].reshape(8, 8, 128)
        pieces.append(jnp.sum(piece, axis=1))
    stacked = jnp.concatenate(pieces, axis=0)
    pick = (
        lax.broadcasted_iota(jnp.int32, (128, 128), 0) // 8 == lax.broadcasted_iota(jnp.int32, (128, 128), 1)
    ).astype(f32)
    sums = jnp.dot(stacked, pick, precision=lax.Precision.HIGHEST, preferred_element_type=f32)
    load = jnp.zeros((8, 128), f32)
    for v in range(8):
        load = load + rolled(sums[8 * v : 8 * v + 8], 16 * v)
    load = jnp.where(g == last, load * (-LOAD_GAIN / 64.0), 0.0)
    wide = lanes((64, 128))
    own = pl.ds(pl.multiple_of(g * 128, 128), 128)
    before = pl.ds(pl.multiple_of(jnp.maximum(g - 1, 0) * 128, 128), 128)
    after = pl.ds(pl.multiple_of(jnp.minimum(g + 1, last) * 128, 128), 128)
    for source, target in ((topo_ref, height_ref), (kappa_ref, conduct_ref)):
        target[:, 0:128] = source[:, own].astype(f32)
        side = jnp.where((wide < 8) & (g < last), source[:, after].astype(f32), 0.0)
        side = jnp.where((wide >= 120) & (g > 0), source[:, before].astype(f32), side)
        target[:, 128:256] = side
    width = topo_ref.shape[1]
    left = jnp.zeros((8, 128), f32)
    right = jnp.zeros((8, 128), f32)
    slot = 0
    for source in (topo_ref, kappa_ref):
        head = source[:, 0:128].astype(f32)
        tail = source[:, width - 128 : width].astype(f32)
        for r in range(8):
            mask = lane // 8 == slot
            left = jnp.where(mask, rolled(head[8 * r : 8 * r + 8], 8 * slot), left)
            right = jnp.where(mask, rolled(tail[8 * r : 8 * r + 8], 8 * slot - 120), right)
            slot += 1
    left_ref[1] = left
    right_ref[1] = right
    left = jnp.zeros((8, 128), f32)
    right = jnp.zeros((8, 128), f32)
    depths = visc_ref.shape[0]
    for field in range(4):
        for depth in range(depths):
            plane = visc_ref[depth] if field == 3 else force_ref[field, depth]
            if field == 2 and depth == depths - 1:
                plane = plane + load
            planes_ref[field, depth] = plane
            left, right = packed(plane, depth + 2, field, left, right, lane)
    left_ref[0] = left
    right_ref[0] = right


def is_even(axis):
    return lax.rem(lax.axis_index(axis), 2) == 0


def fetch(force_ref, visc_ref, odd_ref, even_ref, sems):
    depth = visc_ref.shape[0]
    start = jnp.where(is_even("gz"), 0, depth - 2)
    moves = []
    for target, first in ((odd_ref, start), (even_ref, depth - 2 - start)):
        moves.append((force_ref.at[:, pl.ds(first, 2)], target.at[0:3]))
        moves.append((visc_ref.at[pl.ds(first, 2)], target.at[3]))
    copies = [pltpu.make_async_copy(source, target, sems.at[i]) for i, (source, target) in enumerate(moves)]
    for copy in copies:
        copy.start()
    for copy in copies:
        copy.wait()


def packed(plane, depth, field, left, right, lane):
    first = 8 * depth + 2 * field
    mask = lane // 2 == first // 2
    left = jnp.where(mask, rolled(plane, first), left)
    return left, jnp.where(mask, rolled(plane, first - 126), right)


def assemble(own_ref, odd_ref, even_ref, left_ref, right_ref, planes_ref, odd_out, even_out):
    upward = is_even("gz")
    lane = lanes((8, 128))
    left, right = left_ref[0], right_ref[0]
    for field in range(4):
        for depth in range(DEPTHS):
            p = field * DEPTHS + depth
            if 2 <= depth < DEPTHS - 2:
                planes_ref[p] = own_ref[field, depth - 2]
                continue
            if depth < 2:
                plane = jnp.where(upward, odd_ref[field, depth], even_ref[field, depth])
            else:
                i = depth - (DEPTHS - 2)
                plane = jnp.where(upward, even_ref[field, i], odd_ref[field, i])
            planes_ref[p] = plane
            left, right = packed(plane, depth, field, left, right, lane)
    rightward = is_even("gy")
    odd_out[0] = jnp.where(rightward, left, right)
    even_out[0] = jnp.where(rightward, right, left)
    odd_out[1] = jnp.where(rightward, left_ref[1], right_ref[1])
    even_out[1] = jnp.where(rightward, right_ref[1], left_ref[1])


def edge_rows(planes_ref, low_ref, high_ref):
    for depth in range(DEPTHS):
        for field in range(4):
            plane = planes_ref.at[field * DEPTHS + depth]
            near = 8 * depth + field
            low_ref[near : near + 1, :] = plane[0:1, :]
            low_ref[near + 4 : near + 5, :] = plane[1:2, :]
            high_ref[near : near + 1, :] = plane[7:8, :]
            high_ref[near + 4 : near + 5, :] = plane[6:7, :]


def prepare_rows(
    low_ref, high_ref, own_odd, own_even, odd_ref, even_ref, height_ref, conduct_ref,
    odd_out, even_out, column_ref, height_out, conduct_out,
):
    g = lax.axis_index("gz")
    last = lax.axis_size("gz") - 1
    lane = lanes((8, 128))
    rightward = is_even("gy")

    def chosen(first, second, i):
        return jnp.where(rightward, first[i], second[i])

    before, after = chosen(odd_ref, even_ref, 0), chosen(even_ref, odd_ref, 0)
    before_surface, after_surface = chosen(odd_ref, even_ref, 1), chosen(even_ref, odd_ref, 1)
    side = lax.rem(lane, 2) == 0
    levels = (
        jnp.where(side, chosen(own_odd, own_even, 0), chosen(own_even, own_odd, 0)),
        jnp.where(side, rolled(before, -1), rolled(after, 1)),
        jnp.where(side, before, after),
    )
    downward = is_even("gx")

    def send(rows, low, high):
        odd_out[rows, :] = jnp.where(downward, low, high)
        even_out[rows, :] = jnp.where(downward, high, low)

    for depth in range(DEPTHS):
        rows = slice(8 * depth, 8 * depth + 8)
        send(rows, low_ref[rows, :], high_ref[rows, :])
    pad = [jnp.zeros((2, 128), f32)]
    send(
        slice(COLUMN_ROW, SURFACE_ROW),
        jnp.concatenate([x[0:2] for x in levels] + pad, axis=0),
        jnp.concatenate([x[6:8] for x in levels] + pad, axis=0),
    )
    for i in range(3):
        column_ref[i] = levels[i]
    slot = 0
    for index, (source, target) in enumerate(((height_ref, height_out), (conduct_ref, conduct_out))):
        base = SURFACE_ROW + 16 * index
        for r in range(8):
            rows = slice(8 * r, 8 * r + 8)
            main = source[rows, 0:128]
            side = source[rows, 128:256]
            side = jnp.where((g == 0) & (lane >= 120), rolled(before_surface, 120 - 8 * slot), side)
            side = jnp.where((g == last) & (lane < 8), rolled(after_surface, -8 * slot), side)
            target[rows, 0:128] = main
            target[rows, 128:256] = side
            if r == 0:
                first = (main, side)
            if r == 7:
                send(slice(base, base + 8), first[0], main)
                send(slice(base + 8, base + 16), first[1], side)
            slot += 1


def weighted(before, here, after):
    outer = before + after
    return outer, FACE * here + EDGE * outer, EDGE * here + CORNER * outer


def pair(x):
    return rolled(x, 1, 0) + rolled(x, x.shape[0] - 1, 0)


def lane_pair(x, lane, first, last):
    return jnp.where(lane == 0, first, rolled(x, 1)) + jnp.where(lane == 127, last, rolled(x, 127))


def row_pair(x, row, edge, field):
    up = jnp.where(row == 0, rolled(edge, -field, 0), rolled(x, 1, 0))
    return up + jnp.where(row == 7, rolled(edge, 3 - field, 0), rolled(x, 7, 0))


def to_first(x, depth, field):
    return rolled(x, -(8 * depth + 2 * field))


def to_last(x, depth, field):
    return rolled(x, 126 - (8 * depth + 2 * field))


def spread_rows(x, row):
    field = lax.rem(row, 4)
    for f in range(3):
        x = jnp.where(field == f, rolled(x, f - 3, 0), x)
    return x


def spread_columns(x, lane):
    field = lax.rem(lane, 8) // 2
    for f in range(3):
        x = jnp.where(field == f, rolled(x, 2 * (f - 3)), x)
    return x


def column_sums(levels):
    parts = [weighted(rolled(x, 8), x, rolled(x, 120)) for x in levels]
    (_, ai, bi), (outer, an, bn), (_, af, bf) = parts
    beside = an + pair(bn)
    return FACE * outer + pair(an) + (ai + af) + pair(bi + bf), beside


def beside_rows(beside, depth, row):
    near = jnp.where(row < 4, jnp.broadcast_to(beside[15:16], (8, 128)), jnp.broadcast_to(beside[8:9], (8, 128)))
    field = lax.rem(row, 4)
    first, last = to_first(near, depth, 0), to_last(near, depth, 0)
    for f in range(1, 4):
        first = jnp.where(field == f, to_first(near, depth, f), first)
        last = jnp.where(field == f, to_last(near, depth, f), last)
    return first, last


def sided(odd_ref, even_ref, axis):
    first = is_even(axis)

    def before(rows):
        return jnp.where(first, odd_ref[rows, :], even_ref[rows, :])

    def after(rows):
        return jnp.where(first, even_ref[rows, :], odd_ref[rows, :])

    return before, after


def flux(conduct, slope):
    return conduct * slope * lax.rsqrt(1.0 + slope * slope)


def steps(h, k):
    rows = h.shape[0]
    inside = k > 0.0
    along = 0.5 * (k + rolled(k, 255, 1))
    along_before = rolled(along, 1, 1)
    across = 0.5 * (k + rolled(k, rows - 1, 0))
    for step in range(STEPS):
        q = flux(along, rolled(h, 255, 1) - h) - flux(along_before, h - rolled(h, 1, 1))
        r = flux(across, rolled(h, rows - 1, 0) - h)
        h = jnp.where(inside, h + TIME_STEP * (q + (r - rolled(r, 1, 0))), 0.0)
    return h


def inner_rows(height_ref, conduct_ref, out_ref):
    out_ref[...] = steps(height_ref[...], conduct_ref[...])[8:56, 0:128]


def operate(
    planes_ref, low_ref, high_ref, column_ref, odd_ref, even_ref, height_ref, conduct_ref, inner_ref,
    image_ref, parts_ref, out_ref,
):
    lane = lanes((8, 128))
    row = lax.broadcasted_iota(jnp.int32, (8, 128), 0)
    wide = lanes((16, 128))
    before, after = sided(odd_ref, even_ref, "gx")

    def banded(source, base):
        def joined(side):
            return jnp.concatenate([side(slice(base, base + 8)), side(slice(base + 8, base + 16))], axis=1)

        return jnp.concatenate([source[48:64, :], joined(after), joined(before), source[0:16, :]], axis=0)

    band = steps(banded(height_ref, SURFACE_ROW), banded(conduct_ref, SURFACE_ROW + 16))
    out_ref[0:8, :] = band[32:40, 0:128]
    out_ref[8:56, :] = inner_ref[...]
    out_ref[56:64, :] = band[8:16, 0:128]
    columns = []
    for i in range(3):
        rows = slice(COLUMN_ROW + 2 * i, COLUMN_ROW + 2 * i + 2)
        columns.append(jnp.concatenate([column_ref[i], after(rows), jnp.zeros((4, 128), f32), before(rows)], axis=0))
    column_eta = [spread_columns(x, wide) for x in columns]
    column_sum, beside = column_sums(columns)
    column_sum_eta, beside_eta = column_sums([x * y for x, y in zip(columns, column_eta)])
    near_eta = column_eta[1]
    column_diag = DRAG + TOTAL * near_eta + spread_columns(column_sum, wide)
    column_image = columns[1] * column_diag - near_eta * column_sum - column_sum_eta
    column_image = jnp.where(near_eta > 0.0, column_image, 0.0)
    rows_of, rows_eta = [], []
    for depth in range(DEPTHS):
        rows = slice(8 * depth, 8 * depth + 8)
        b, a = before(rows), after(rows)
        found = (
            jnp.where(row < 4, low_ref[rows, :], rolled(high_ref[rows, :], 4, 0)),
            jnp.where(row < 4, b, rolled(a, 4, 0)),
            jnp.where(row < 4, rolled(b, 4, 0), a),
        )
        rows_of.append(found)
        rows_eta.append([spread_rows(x, row) for x in found])
    rows_product = [[x * y for x, y in zip(found, etas)] for found, etas in zip(rows_of, rows_eta)]

    def row_sums(levels, depth, beside_columns):
        parts = [weighted(levels[depth - 1][i], levels[depth][i], levels[depth + 1][i]) for i in range(3)]
        (_, ai, bi), (outer, an, bn), (_, af, bf) = parts
        first, last = beside_rows(beside_columns, depth, row)
        return FACE * outer + (ai + af) + lane_pair(an + (bi + bf), lane, first, last), an, bn

    def plane_sum(three, an, bn, beside_columns, depth, field):
        outer, a, b = weighted(*three)
        both = a + row_pair(b, row, bn, field)
        own = beside_columns[0:8]
        sides = lane_pair(both, lane, to_first(own, depth, field), to_last(own, depth, field))
        return FACE * outer + row_pair(a, row, an, field) + sides

    def plane(field, depth):
        return planes_ref[field * DEPTHS + depth]

    image, row_image, diagonal = {}, {}, {}
    for depth in range(1, DEPTHS - 1):
        row_sum, an, bn = row_sums(rows_of, depth, beside)
        row_sum_eta, an_eta, bn_eta = row_sums(rows_product, depth, beside_eta)
        near, eta = rows_of[depth][1], rows_eta[depth][1]
        diag = DRAG + TOTAL * eta + spread_rows(row_sum, row)
        row_image[depth] = jnp.where(eta > 0.0, near * diag - eta * row_sum - row_sum_eta, 0.0)
        e = [plane(3, depth + i) for i in (-1, 0, 1)]
        diag = DRAG + TOTAL * e[1] + plane_sum(e, an, bn, beside, depth, 3)
        diagonal[depth] = diag
        for c in range(3):
            v = [plane(c, depth + i) for i in (-1, 0, 1)]
            ev = [x * y for x, y in zip(e, v)]
            out = v[1] * diag - e[1] * plane_sum(v, an, bn, beside, depth, c)
            out = out - plane_sum(ev, an_eta, bn_eta, beside_eta, depth, c)
            image[c, depth] = jnp.where(e[1] > 0.0, out, 0.0)
    _, an, bn = weighted(rolled(column_image, 8), column_image, rolled(column_image, 120))
    beside = an + pair(bn)
    m = [jnp.zeros((8, 128), f32) for _ in range(4)]
    for depth in range(2, DEPTHS - 2):
        _, an, bn = weighted(row_image[depth - 1], row_image[depth], row_image[depth + 1])
        e = plane(3, depth)
        for c in range(3):
            s = plane_sum([image[c, depth + i] for i in (-1, 0, 1)], an, bn, beside, depth, c)
            v, q = plane(c, depth), image[c, depth]
            image_ref[c, depth - 2] = q
            m[0] = m[0] + v * v
            m[1] = m[1] + v * q
            m[2] = m[2] + q * q
            m[3] = m[3] + q * (q * diagonal[depth] - 2.0 * (e * s))
    total = jnp.zeros((8, 128), f32)
    for k in range(4):
        part = m[k]
        for amount in (64, 32, 16):
            part = part + rolled(part, amount)
        total = jnp.where(lane // 16 == 2 + k, part, total)
    for amount in (4, 2, 1):
        total = total + rolled(total, amount, 0)
    top = (plane(2, DEPTHS - 3), image[2, DEPTHS - 3])
    for j in range(parts_ref.shape[0]):
        piece = jnp.where(lane < 16, rolled(top[0], -16 * j), total)
        parts_ref[j] = jnp.where(lane // 16 == 1, rolled(top[1], 16 - 16 * j), piece)


def middle(parts_ref, sums_ref):
    total = parts_ref[0]
    for j in range(1, parts_ref.shape[0]):
        total = total + parts_ref[j]
    for i in range(sums_ref.shape[0] // 8):
        sums_ref[8 * i : 8 * i + 8, :] = total


def finish(sums_ref, parts_ref, planes_ref, image_ref, height_ref, velocity_hbm, surface_hbm, velocity_ref, surface_ref, sems):
    count = parts_ref.shape[0]
    lane = lanes((1, 128))
    top = parts_ref[count - 1]
    top = jnp.where(lanes((16, 128)) < 16, jnp.concatenate([top, rolled(top, -16)], axis=0), 0.0)
    spread = (
        lax.broadcasted_iota(jnp.int32, (128, 128), 1) // 8 == lax.broadcasted_iota(jnp.int32, (128, 128), 0)
    ).astype(f32)
    wide = jnp.dot(top, spread, precision=lax.Precision.HIGHEST, preferred_element_type=f32)
    total = jnp.sum(sums_ref[...], axis=0, keepdims=True)

    def moment(k):
        return jnp.sum(jnp.where(lane // 16 == 2 + k, total, 0.0), axis=1, keepdims=True)

    m0, m1, m2, m3 = (moment(k) for k in range(4))
    first = m0 / m1
    later = first * first * m2 - m0
    gain = 1.0 + later / m0
    second = later / (gain * gain * m1 - 2.0 * first * gain * m2 + first * first * m3)
    on_force = first + second * gain
    on_image = -(second * first)
    for c in range(3):
        for depth in range(8):
            velocity_ref[c, depth] = on_force * planes_ref[c * DEPTHS + depth + 2] + on_image * image_ref[c, depth]
    velocity_copy = pltpu.make_async_copy(velocity_ref, velocity_hbm, sems.at[0])
    velocity_copy.start()
    rise = (STEPS * TIME_STEP) * (on_force * wide[0:8] + on_image * wide[8:16])
    for r in range(8):
        rows = slice(8 * r, 8 * r + 8)
        surface_ref[rows, :] = height_ref[rows, :] + jnp.broadcast_to(rise[r : r + 1, :], (8, 128))
    surface_copy = pltpu.make_async_copy(surface_ref, surface_hbm, sems.at[1])
    surface_copy.start()
    velocity_copy.wait()
    surface_copy.wait()


def swap(odd, even, axis):
    count = lax.axis_size(axis)

    def pairs(start):
        found = []
        for i in range(start, count - 1, 2):
            found += [(i, i + 1), (i + 1, i)]
        return found

    return lax.ppermute(odd, axis, pairs(1)), lax.ppermute(even, axis, pairs(0))


def local(body_force, viscosity, topography, kappa):
    inputs = [
        pltpu.with_memory_space_constraint(x, pltpu.HBM) for x in (body_force, viscosity, topography, kappa)
    ]
    odd, even = pl.pallas_call(
        fetch,
        out_shape=[jax.ShapeDtypeStruct((4, 2, 8, 128), f32)] * 2,
        in_specs=[pl.BlockSpec(memory_space=pltpu.HBM)] * 2,
        out_specs=[vmem()] * 2,
        scratch_shapes=[pltpu.SemaphoreType.DMA((4,))],
        compiler_params=pltpu.CompilerParams(vmem_limit_bytes=1 << 20),
    )(*inputs[:2])
    odd, even = swap(odd, even, "gz")
    planes, left, right, height, conduct = pl.pallas_call(
        own_block,
        out_shape=[
            jax.ShapeDtypeStruct(shape, f32)
            for shape in ((4, 8, 8, 128), (2, 8, 128), (2, 8, 128), (64, 256), (64, 256))
        ],
        in_specs=[pl.BlockSpec(memory_space=pltpu.HBM)] * 4,
        out_specs=[vmem()] * 5,
        scratch_shapes=[pltpu.VMEM(x.shape, x.dtype) for x in inputs] + [pltpu.SemaphoreType.DMA((4,))],
        compiler_params=pltpu.CompilerParams(vmem_limit_bytes=8 << 20),
        cost_estimate=pl.CostEstimate(flops=20000 * 1024, bytes_accessed=1 << 18, transcendentals=0),
    )(*inputs)
    planes, odd, even = call(
        assemble,
        [(PLANES, 8, 128), (2, 8, 128), (2, 8, 128)],
        (planes, odd, even, left, right),
    )
    own = (odd, even)
    odd, even = swap(odd, even, "gy")
    low, high = call(edge_rows, [(COLUMN_ROW, 128)] * 2, (planes,))
    odd, even, columns, height, conduct = call(
        prepare_rows,
        [(GX_ROWS, 128), (GX_ROWS, 128), (3, 8, 128), (64, 256), (64, 256)],
        (low, high, *own, odd, even, height, conduct),
    )
    odd, even = swap(odd, even, "gx")
    (inner,) = call(inner_rows, [(48, 128)], (height, conduct))
    group = lax.axis_size("gx") * lax.axis_size("gy")
    image, parts, height = call(
        operate,
        [(3, 8, 8, 128), (lax.axis_size("gz"), 8, 128), (64, 128)],
        (planes, low, high, columns, odd, even, height, conduct, inner),
    )
    parts = lax.all_to_all(parts, "gz", 0, 0)
    (sums,) = call(middle, [(group, 128)], (parts,))
    sums = lax.all_to_all(sums.reshape(group, 1, 128), ("gx", "gy"), 0, 0).reshape(group, 128)
    shapes = ((3, 8, 8, 128), (64, 128))
    velocity, surface = pl.pallas_call(
        finish,
        out_shape=[jax.ShapeDtypeStruct(shape, f32) for shape in shapes],
        in_specs=[vmem()] * 5,
        out_specs=[pl.BlockSpec(memory_space=pltpu.HBM)] * 2,
        scratch_shapes=[pltpu.VMEM(shape, f32) for shape in shapes] + [pltpu.SemaphoreType.DMA((2,))],
        compiler_params=pltpu.CompilerParams(vmem_limit_bytes=8 << 20),
    )(sums, parts, planes, image, height)
    return velocity, surface


def solution(mesh):
    in_specs = (P(None, "gz", "gx", "gy"), P("gz", "gx", "gy"), P("gx", "gy"), P("gx", "gy"))
    out_specs = (P(None, "gz", "gx", "gy"), P("gx", ("gy", "gz")))
    return jax.shard_map(local, mesh=mesh, in_specs=in_specs, out_specs=out_specs, check_vma=False)
```

```python
import jax
import jax.numpy as jnp
from jax import lax
from jax.experimental import pallas as pl
from jax.experimental.pallas import tpu as pltpu
from jax.sharding import PartitionSpec as P

STEPS = 8
DRAG = 1.0
TIME_STEP = 1.0
LOAD_GAIN = 4.0
FACE, EDGE, CORNER = 0.5, 0.25, 0.5 / 3.0
TOTAL = 6 * FACE + 12 * EDGE + 8 * CORNER

DEPTHS = 12
PLANES = 4 * DEPTHS
COLUMN_ROW = 8 * DEPTHS
SURFACE_ROW = COLUMN_ROW + 8
GX_ROWS = SURFACE_ROW + 32

f32 = jnp.float32


def vmem():
    return pl.BlockSpec(memory_space=pltpu.VMEM)


def call(body, outs, ins, scratch=(), cost=20000, limit=8 << 20):
    return pl.pallas_call(
        body,
        out_shape=[jax.ShapeDtypeStruct(s, f32) for s in outs],
        in_specs=[vmem() for _ in ins],
        out_specs=[vmem() for _ in outs],
        scratch_shapes=list(scratch),
        compiler_params=pltpu.CompilerParams(vmem_limit_bytes=limit),
        cost_estimate=pl.CostEstimate(flops=cost * 1024, bytes_accessed=1 << 18, transcendentals=0),
    )(*ins)


def lanes(shape):
    return lax.broadcasted_iota(jnp.int32, shape, len(shape) - 1)


def rolled(x, amount, axis=1):
    amount = amount % x.shape[axis]
    return x if amount == 0 else pltpu.roll(x, amount, axis)


def own_block(
    force_hbm, visc_hbm, topo_hbm, kappa_hbm, planes_ref, left_ref, right_ref, height_ref, conduct_ref,
    force_ref, visc_ref, topo_ref, kappa_ref, sems,
):
    moves = ((topo_hbm, topo_ref), (kappa_hbm, kappa_ref), (force_hbm, force_ref), (visc_hbm, visc_ref))
    copies = [pltpu.make_async_copy(source, target, sems.at[i]) for i, (source, target) in enumerate(moves)]
    for copy in copies:
        copy.start()
    for copy in copies:
        copy.wait()
    g = lax.axis_index("gz")
    last = lax.axis_size("gz") - 1
    lane = lanes((8, 128))
    pieces = []
    for v in range(8):
        piece = topo_ref[:, 128 * v : 128 * v + 128].reshape(8, 8, 128)
        pieces.append(jnp.sum(piece, axis=1))
    stacked = jnp.concatenate(pieces, axis=0)
    pick = (
        lax.broadcasted_iota(jnp.int32, (128, 128), 0) // 8 == lax.broadcasted_iota(jnp.int32, (128, 128), 1)
    ).astype(f32)
    sums = jnp.dot(stacked, pick, precision=lax.Precision.HIGHEST, preferred_element_type=f32)
    load = jnp.zeros((8, 128), f32)
    for v in range(8):
        load = load + rolled(sums[8 * v : 8 * v + 8], 16 * v)
    load = jnp.where(g == last, load * (-LOAD_GAIN / 64.0), 0.0)
    wide = lanes((64, 128))
    own = pl.ds(pl.multiple_of(g * 128, 128), 128)
    before = pl.ds(pl.multiple_of(jnp.maximum(g - 1, 0) * 128, 128), 128)
    after = pl.ds(pl.multiple_of(jnp.minimum(g + 1, last) * 128, 128), 128)
    for source, target in ((topo_ref, height_ref), (kappa_ref, conduct_ref)):
        target[:, 0:128] = source[:, own].astype(f32)
        side = jnp.where((wide < 8) & (g < last), source[:, after].astype(f32), 0.0)
        side = jnp.where((wide >= 120) & (g > 0), source[:, before].astype(f32), side)
        target[:, 128:256] = side
    width = topo_ref.shape[1]
    left = jnp.zeros((8, 128), f32)
    right = jnp.zeros((8, 128), f32)
    slot = 0
    for source in (topo_ref, kappa_ref):
        head = source[:, 0:128].astype(f32)
        tail = source[:, width - 128 : width].astype(f32)
        for r in range(8):
            mask = lane // 8 == slot
            left = jnp.where(mask, rolled(head[8 * r : 8 * r + 8], 8 * slot), left)
            right = jnp.where(mask, rolled(tail[8 * r : 8 * r + 8], 8 * slot - 120), right)
            slot += 1
    left_ref[1] = left
    right_ref[1] = right
    left = jnp.zeros((8, 128), f32)
    right = jnp.zeros((8, 128), f32)
    depths = visc_ref.shape[0]
    for field in range(4):
        for depth in range(depths):
            plane = visc_ref[depth] if field == 3 else force_ref[field, depth]
            if field == 2 and depth == depths - 1:
                plane = plane + load
            planes_ref[field, depth] = plane
            left, right = packed(plane, depth + 2, field, left, right, lane)
    left_ref[0] = left
    right_ref[0] = right


def is_even(axis):
    return lax.rem(lax.axis_index(axis), 2) == 0


def fetch(force_ref, visc_ref, odd_ref, even_ref, sems):
    depth = visc_ref.shape[0]
    start = jnp.where(is_even("gz"), 0, depth - 2)
    moves = []
    for target, first in ((odd_ref, start), (even_ref, depth - 2 - start)):
        moves.append((force_ref.at[:, pl.ds(first, 2)], target.at[0:3]))
        moves.append((visc_ref.at[pl.ds(first, 2)], target.at[3]))
    copies = [pltpu.make_async_copy(source, target, sems.at[i]) for i, (source, target) in enumerate(moves)]
    for copy in copies:
        copy.start()
    for copy in copies:
        copy.wait()


def packed(plane, depth, field, left, right, lane):
    first = 8 * depth + 2 * field
    mask = lane // 2 == first // 2
    left = jnp.where(mask, rolled(plane, first), left)
    return left, jnp.where(mask, rolled(plane, first - 126), right)


def assemble(own_ref, odd_ref, even_ref, left_ref, right_ref, planes_ref, odd_out, even_out):
    upward = is_even("gz")
    lane = lanes((8, 128))
    left, right = left_ref[0], right_ref[0]
    for field in range(4):
        for depth in range(DEPTHS):
            p = field * DEPTHS + depth
            if 2 <= depth < DEPTHS - 2:
                planes_ref[p] = own_ref[field, depth - 2]
                continue
            if depth < 2:
                plane = jnp.where(upward, odd_ref[field, depth], even_ref[field, depth])
            else:
                i = depth - (DEPTHS - 2)
                plane = jnp.where(upward, even_ref[field, i], odd_ref[field, i])
            planes_ref[p] = plane
            left, right = packed(plane, depth, field, left, right, lane)
    rightward = is_even("gy")
    odd_out[0] = jnp.where(rightward, left, right)
    even_out[0] = jnp.where(rightward, right, left)
    odd_out[1] = jnp.where(rightward, left_ref[1], right_ref[1])
    even_out[1] = jnp.where(rightward, right_ref[1], left_ref[1])


def edge_rows(planes_ref, low_ref, high_ref):
    for depth in range(DEPTHS):
        for field in range(4):
            plane = planes_ref.at[field * DEPTHS + depth]
            near = 8 * depth + field
            low_ref[near : near + 1, :] = plane[0:1, :]
            low_ref[near + 4 : near + 5, :] = plane[1:2, :]
            high_ref[near : near + 1, :] = plane[7:8, :]
            high_ref[near + 4 : near + 5, :] = plane[6:7, :]


def prepare_rows(
    low_ref, high_ref, own_odd, own_even, odd_ref, even_ref, height_ref, conduct_ref,
    even_out, odd_out, column_ref, height_out, conduct_out,
):
    g = lax.axis_index("gz")
    last = lax.axis_size("gz") - 1
    lane = lanes((8, 128))
    rightward = is_even("gy")

    def chosen(first, second, i):
        return jnp.where(rightward, first[i], second[i])

    before, after = chosen(odd_ref, even_ref, 0), chosen(even_ref, odd_ref, 0)
    before_surface, after_surface = chosen(odd_ref, even_ref, 1), chosen(even_ref, odd_ref, 1)
    side = lax.rem(lane, 2) == 0
    levels = (
        jnp.where(side, chosen(own_odd, own_even, 0), chosen(own_even, own_odd, 0)),
        jnp.where(side, rolled(before, -1), rolled(after, 1)),
        jnp.where(side, before, after),
    )
    downward = is_even("gx")

    def send(rows, low, high):
        odd_out[rows, :] = jnp.where(downward, low, high)
        even_out[rows, :] = jnp.where(downward, high, low)

    for depth in range(DEPTHS):
        rows = slice(8 * depth, 8 * depth + 8)
        send(rows, low_ref[rows, :], high_ref[rows, :])
    pad = [jnp.zeros((2, 128), f32)]
    send(
        slice(COLUMN_ROW, SURFACE_ROW),
        jnp.concatenate([x[0:2] for x in levels] + pad, axis=0),
        jnp.concatenate([x[6:8] for x in levels] + pad, axis=0),
    )
    for i in range(3):
        column_ref[i] = levels[i]
    slot = 0
    for index, (source, target) in enumerate(((height_ref, height_out), (conduct_ref, conduct_out))):
        base = SURFACE_ROW + 16 * index
        for r in range(8):
            rows = slice(8 * r, 8 * r + 8)
            main = source[rows, 0:128]
            side = source[rows, 128:256]
            side = jnp.where((g == 0) & (lane >= 120), rolled(before_surface, 120 - 8 * slot), side)
            side = jnp.where((g == last) & (lane < 8), rolled(after_surface, -8 * slot), side)
            target[rows, 0:128] = main
            target[rows, 128:256] = side
            if r == 0:
                first = (main, side)
            if r == 7:
                send(slice(base, base + 8), first[0], main)
                send(slice(base + 8, base + 16), first[1], side)
            slot += 1


def weighted(before, here, after):
    outer = before + after
    return outer, FACE * here + EDGE * outer, EDGE * here + CORNER * outer


def pair(x):
    return rolled(x, 1, 0) + rolled(x, x.shape[0] - 1, 0)


def lane_pair(x, lane, first, last):
    return jnp.where(lane == 0, first, rolled(x, 1)) + jnp.where(lane == 127, last, rolled(x, 127))


def row_pair(x, row, edge, field):
    up = jnp.where(row == 0, rolled(edge, -field, 0), rolled(x, 1, 0))
    return up + jnp.where(row == 7, rolled(edge, 3 - field, 0), rolled(x, 7, 0))


def to_first(x, depth, field):
    return rolled(x, -(8 * depth + 2 * field))


def to_last(x, depth, field):
    return rolled(x, 126 - (8 * depth + 2 * field))


def spread_rows(x, row):
    field = lax.rem(row, 4)
    for f in range(3):
        x = jnp.where(field == f, rolled(x, f - 3, 0), x)
    return x


def spread_columns(x, lane):
    field = lax.rem(lane, 8) // 2
    for f in range(3):
        x = jnp.where(field == f, rolled(x, 2 * (f - 3)), x)
    return x


def column_sums(levels):
    parts = [weighted(rolled(x, 8), x, rolled(x, 120)) for x in levels]
    (_, ai, bi), (outer, an, bn), (_, af, bf) = parts
    beside = an + pair(bn)
    return FACE * outer + pair(an) + (ai + af) + pair(bi + bf), beside


def beside_rows(beside, depth, row):
    near = jnp.where(row < 4, jnp.broadcast_to(beside[15:16], (8, 128)), jnp.broadcast_to(beside[8:9], (8, 128)))
    field = lax.rem(row, 4)
    first, last = to_first(near, depth, 0), to_last(near, depth, 0)
    for f in range(1, 4):
        first = jnp.where(field == f, to_first(near, depth, f), first)
        last = jnp.where(field == f, to_last(near, depth, f), last)
    return first, last


def sided(odd_ref, even_ref, axis):
    first = is_even(axis)

    def before(rows):
        return jnp.where(first, odd_ref[rows, :], even_ref[rows, :])

    def after(rows):
        return jnp.where(first, even_ref[rows, :], odd_ref[rows, :])

    return before, after


def flux(conduct, slope):
    return conduct * slope * lax.rsqrt(1.0 + slope * slope)


def steps(h, k):
    rows = h.shape[0]
    inside = k > 0.0
    along = 0.5 * (k + rolled(k, 255, 1))
    along_before = rolled(along, 1, 1)
    across = 0.5 * (k + rolled(k, rows - 1, 0))
    for step in range(STEPS):
        q = flux(along, rolled(h, 255, 1) - h) - flux(along_before, h - rolled(h, 1, 1))
        r = flux(across, rolled(h, rows - 1, 0) - h)
        h = jnp.where(inside, h + TIME_STEP * (q + (r - rolled(r, 1, 0))), 0.0)
    return h


def inner_rows(height_ref, conduct_ref, out_ref):
    out_ref[...] = steps(height_ref[...], conduct_ref[...])[8:56, 0:128]


def operate(
    planes_ref, low_ref, high_ref, column_ref, even_ref, odd_ref, height_ref, conduct_ref, inner_ref,
    image_ref, sums_ref, top_ref, out_ref,
):
    lane = lanes((8, 128))
    row = lax.broadcasted_iota(jnp.int32, (8, 128), 0)
    wide = lanes((16, 128))
    before, after = sided(odd_ref, even_ref, "gx")

    def banded(source, base):
        def joined(side):
            return jnp.concatenate([side(slice(base, base + 8)), side(slice(base + 8, base + 16))], axis=1)

        return jnp.concatenate([source[48:64, :], joined(after), joined(before), source[0:16, :]], axis=0)

    band = steps(banded(height_ref, SURFACE_ROW), banded(conduct_ref, SURFACE_ROW + 16))
    out_ref[0:8, :] = band[32:40, 0:128]
    out_ref[8:56, :] = inner_ref[...]
    out_ref[56:64, :] = band[8:16, 0:128]
    columns = []
    for i in range(3):
        rows = slice(COLUMN_ROW + 2 * i, COLUMN_ROW + 2 * i + 2)
        columns.append(jnp.concatenate([column_ref[i], after(rows), jnp.zeros((4, 128), f32), before(rows)], axis=0))
    column_eta = [spread_columns(x, wide) for x in columns]
    column_sum, beside = column_sums(columns)
    column_sum_eta, beside_eta = column_sums([x * y for x, y in zip(columns, column_eta)])
    near_eta = column_eta[1]
    column_diag = DRAG + TOTAL * near_eta + spread_columns(column_sum, wide)
    column_image = columns[1] * column_diag - near_eta * column_sum - column_sum_eta
    column_image = jnp.where(near_eta > 0.0, column_image, 0.0)
    rows_of, rows_eta = [], []
    for depth in range(DEPTHS):
        rows = slice(8 * depth, 8 * depth + 8)
        b, a = before(rows), after(rows)
        found = (
            jnp.where(row < 4, low_ref[rows, :], rolled(high_ref[rows, :], 4, 0)),
            jnp.where(row < 4, b, rolled(a, 4, 0)),
            jnp.where(row < 4, rolled(b, 4, 0), a),
        )
        rows_of.append(found)
        rows_eta.append([spread_rows(x, row) for x in found])
    rows_product = [[x * y for x, y in zip(found, etas)] for found, etas in zip(rows_of, rows_eta)]

    def row_sums(levels, depth, beside_columns):
        parts = [weighted(levels[depth - 1][i], levels[depth][i], levels[depth + 1][i]) for i in range(3)]
        (_, ai, bi), (outer, an, bn), (_, af, bf) = parts
        first, last = beside_rows(beside_columns, depth, row)
        return FACE * outer + (ai + af) + lane_pair(an + (bi + bf), lane, first, last), an, bn

    def plane_sum(three, an, bn, beside_columns, depth, field):
        outer, a, b = weighted(*three)
        both = a + row_pair(b, row, bn, field)
        own = beside_columns[0:8]
        sides = lane_pair(both, lane, to_first(own, depth, field), to_last(own, depth, field))
        return FACE * outer + row_pair(a, row, an, field) + sides

    def plane(field, depth):
        return planes_ref[field * DEPTHS + depth]

    image, row_image, diagonal = {}, {}, {}
    for depth in range(1, DEPTHS - 1):
        row_sum, an, bn = row_sums(rows_of, depth, beside)
        row_sum_eta, an_eta, bn_eta = row_sums(rows_product, depth, beside_eta)
        near, eta = rows_of[depth][1], rows_eta[depth][1]
        diag = DRAG + TOTAL * eta + spread_rows(row_sum, row)
        row_image[depth] = jnp.where(eta > 0.0, near * diag - eta * row_sum - row_sum_eta, 0.0)
        e = [plane(3, depth + i) for i in (-1, 0, 1)]
        diag = DRAG + TOTAL * e[1] + plane_sum(e, an, bn, beside, depth, 3)
        diagonal[depth] = diag
        for c in range(3):
            v = [plane(c, depth + i) for i in (-1, 0, 1)]
            ev = [x * y for x, y in zip(e, v)]
            out = v[1] * diag - e[1] * plane_sum(v, an, bn, beside, depth, c)
            out = out - plane_sum(ev, an_eta, bn_eta, beside_eta, depth, c)
            image[c, depth] = jnp.where(e[1] > 0.0, out, 0.0)
    _, an, bn = weighted(rolled(column_image, 8), column_image, rolled(column_image, 120))
    beside = an + pair(bn)
    m = [jnp.zeros((8, 128), f32) for _ in range(4)]
    for depth in range(2, DEPTHS - 2):
        _, an, bn = weighted(row_image[depth - 1], row_image[depth], row_image[depth + 1])
        e = plane(3, depth)
        for c in range(3):
            s = plane_sum([image[c, depth + i] for i in (-1, 0, 1)], an, bn, beside, depth, c)
            v, q = plane(c, depth), image[c, depth]
            image_ref[c, depth - 2] = q
            m[0] = m[0] + v * v
            m[1] = m[1] + v * q
            m[2] = m[2] + q * q
            m[3] = m[3] + q * (q * diagonal[depth] - 2.0 * (e * s))
    total = jnp.zeros((8, 128), f32)
    for k in range(4):
        part = m[k]
        for amount in (64, 32, 16):
            part = part + rolled(part, amount)
        total = jnp.where(lane // 16 == 2 + k, part, total)
    for amount in (4, 2, 1):
        total = total + rolled(total, amount, 0)
    for i in range(sums_ref.shape[0] // 8):
        sums_ref[8 * i : 8 * i + 8, :] = total
    top_ref[0] = plane(2, DEPTHS - 3)
    top_ref[1] = image[2, DEPTHS - 3]


def middle(sums_ref, top_ref, out_ref):
    lane = lanes((8, 128))
    part = jnp.sum(sums_ref[...], axis=0, keepdims=True)
    base = jnp.broadcast_to(part, (8, 128))
    for j in range(out_ref.shape[0]):
        piece = jnp.where(lane < 16, rolled(top_ref[0], -16 * j), base)
        out_ref[j] = jnp.where(lane // 16 == 1, rolled(top_ref[1], 16 - 16 * j), piece)


def finish(parts_ref, planes_ref, image_ref, height_ref, velocity_hbm, surface_hbm, velocity_ref, surface_ref, sems):
    count = parts_ref.shape[0]
    lane = lanes((1, 128))
    top = parts_ref[count - 1]
    top = jnp.where(lanes((16, 128)) < 16, jnp.concatenate([top, rolled(top, -16)], axis=0), 0.0)
    spread = (
        lax.broadcasted_iota(jnp.int32, (128, 128), 1) // 8 == lax.broadcasted_iota(jnp.int32, (128, 128), 0)
    ).astype(f32)
    wide = jnp.dot(top, spread, precision=lax.Precision.HIGHEST, preferred_element_type=f32)
    total = parts_ref[0, 0:1, :]
    for j in range(1, count):
        total = total + parts_ref[j, 0:1, :]

    def moment(k):
        return jnp.sum(jnp.where(lane // 16 == 2 + k, total, 0.0), axis=1, keepdims=True)

    m0, m1, m2, m3 = (moment(k) for k in range(4))
    first = m0 / m1
    later = first * first * m2 - m0
    gain = 1.0 + later / m0
    second = later / (gain * gain * m1 - 2.0 * first * gain * m2 + first * first * m3)
    on_force = first + second * gain
    on_image = -(second * first)
    for c in range(3):
        for depth in range(8):
            velocity_ref[c, depth] = on_force * planes_ref[c * DEPTHS + depth + 2] + on_image * image_ref[c, depth]
    velocity_copy = pltpu.make_async_copy(velocity_ref, velocity_hbm, sems.at[0])
    velocity_copy.start()
    rise = (STEPS * TIME_STEP) * (on_force * wide[0:8] + on_image * wide[8:16])
    for r in range(8):
        rows = slice(8 * r, 8 * r + 8)
        surface_ref[rows, :] = height_ref[rows, :] + jnp.broadcast_to(rise[r : r + 1, :], (8, 128))
    surface_copy = pltpu.make_async_copy(surface_ref, surface_hbm, sems.at[1])
    surface_copy.start()
    velocity_copy.wait()
    surface_copy.wait()


def swap(odd, even, axis, even_first=False):
    count = lax.axis_size(axis)

    def pairs(start):
        found = []
        for i in range(start, count - 1, 2):
            found += [(i, i + 1), (i + 1, i)]
        return found

    if even_first:
        even = lax.ppermute(even, axis, pairs(0))
        return lax.ppermute(odd, axis, pairs(1)), even
    return lax.ppermute(odd, axis, pairs(1)), lax.ppermute(even, axis, pairs(0))


def local(body_force, viscosity, topography, kappa):
    inputs = [
        pltpu.with_memory_space_constraint(x, pltpu.HBM) for x in (body_force, viscosity, topography, kappa)
    ]
    odd, even = pl.pallas_call(
        fetch,
        out_shape=[jax.ShapeDtypeStruct((4, 2, 8, 128), f32)] * 2,
        in_specs=[pl.BlockSpec(memory_space=pltpu.HBM)] * 2,
        out_specs=[vmem()] * 2,
        scratch_shapes=[pltpu.SemaphoreType.DMA((4,))],
        compiler_params=pltpu.CompilerParams(vmem_limit_bytes=1 << 20),
    )(*inputs[:2])
    odd, even = swap(odd, even, "gz")
    planes, left, right, height, conduct = pl.pallas_call(
        own_block,
        out_shape=[
            jax.ShapeDtypeStruct(shape, f32)
            for shape in ((4, 8, 8, 128), (2, 8, 128), (2, 8, 128), (64, 256), (64, 256))
        ],
        in_specs=[pl.BlockSpec(memory_space=pltpu.HBM)] * 4,
        out_specs=[vmem()] * 5,
        scratch_shapes=[pltpu.VMEM(x.shape, x.dtype) for x in inputs] + [pltpu.SemaphoreType.DMA((4,))],
        compiler_params=pltpu.CompilerParams(vmem_limit_bytes=8 << 20),
        cost_estimate=pl.CostEstimate(flops=20000 * 1024, bytes_accessed=1 << 18, transcendentals=0),
    )(*inputs)
    planes, odd, even = call(
        assemble,
        [(PLANES, 8, 128), (2, 8, 128), (2, 8, 128)],
        (planes, odd, even, left, right),
    )
    own = (odd, even)
    odd, even = swap(odd, even, "gy")
    low, high = call(edge_rows, [(COLUMN_ROW, 128)] * 2, (planes,))
    even, odd, columns, height, conduct = call(
        prepare_rows,
        [(GX_ROWS, 128), (GX_ROWS, 128), (3, 8, 128), (64, 256), (64, 256)],
        (low, high, *own, odd, even, height, conduct),
    )
    odd, even = swap(odd, even, "gx", even_first=True)
    (inner,) = call(inner_rows, [(48, 128)], (height, conduct))
    group = lax.axis_size("gx") * lax.axis_size("gy")
    image, sums, top, height = call(
        operate,
        [(3, 8, 8, 128), (group, 128), (2, 8, 128), (64, 128)],
        (planes, low, high, columns, even, odd, height, conduct, inner),
    )
    sums = lax.all_to_all(sums.reshape(group, 1, 128), ("gx", "gy"), 0, 0)
    (parts,) = call(middle, [(lax.axis_size("gz"), 8, 128)], (sums.reshape(group, 128), top))
    parts = lax.all_to_all(parts, "gz", 0, 0)
    shapes = ((3, 8, 8, 128), (64, 128))
    velocity, surface = pl.pallas_call(
        finish,
        out_shape=[jax.ShapeDtypeStruct(shape, f32) for shape in shapes],
        in_specs=[vmem()] * 4,
        out_specs=[pl.BlockSpec(memory_space=pltpu.HBM)] * 2,
        scratch_shapes=[pltpu.VMEM(shape, f32) for shape in shapes] + [pltpu.SemaphoreType.DMA((2,))],
        compiler_params=pltpu.CompilerParams(vmem_limit_bytes=8 << 20),
    )(parts, planes, image, height)
    return velocity, surface


def solution(mesh):
    in_specs = (P(None, "gz", "gx", "gy"), P("gz", "gx", "gy"), P("gx", "gy"), P("gx", "gy"))
    out_specs = (P(None, "gz", "gx", "gy"), P("gx", ("gy", "gz")))
    return jax.shard_map(local, mesh=mesh, in_specs=in_specs, out_specs=out_specs, check_vma=False)
```

```python
import jax
import jax.numpy as jnp
from jax import lax
from jax.experimental import pallas as pl
from jax.experimental.pallas import tpu as pltpu
from jax.sharding import PartitionSpec as P

STEPS = 8
DRAG = 1.0
TIME_STEP = 1.0
LOAD_GAIN = 4.0
FACE, EDGE, CORNER = 0.5, 0.25, 0.5 / 3.0
TOTAL = 6 * FACE + 12 * EDGE + 8 * CORNER

DEPTHS = 12
PLANES = 4 * DEPTHS
COLUMN_ROW = 8 * DEPTHS
SURFACE_ROW = COLUMN_ROW + 8
GX_ROWS = SURFACE_ROW + 32

f32 = jnp.float32


def vmem():
    return pl.BlockSpec(memory_space=pltpu.VMEM)


def call(body, outs, ins, scratch=(), cost=20000, limit=8 << 20):
    return pl.pallas_call(
        body,
        out_shape=[jax.ShapeDtypeStruct(s, f32) for s in outs],
        in_specs=[vmem() for _ in ins],
        out_specs=[vmem() for _ in outs],
        scratch_shapes=list(scratch),
        compiler_params=pltpu.CompilerParams(vmem_limit_bytes=limit),
        cost_estimate=pl.CostEstimate(flops=cost * 1024, bytes_accessed=1 << 18, transcendentals=0),
    )(*ins)


def lanes(shape):
    return lax.broadcasted_iota(jnp.int32, shape, len(shape) - 1)


def rolled(x, amount, axis=1):
    amount = amount % x.shape[axis]
    return x if amount == 0 else pltpu.roll(x, amount, axis)


def own_block(
    force_hbm, visc_hbm, topo_hbm, kappa_hbm, planes_ref, left_ref, right_ref, height_ref, conduct_ref,
    force_ref, visc_ref, topo_ref, kappa_ref, sems,
):
    moves = ((topo_hbm, topo_ref), (kappa_hbm, kappa_ref), (force_hbm, force_ref), (visc_hbm, visc_ref))
    copies = [pltpu.make_async_copy(source, target, sems.at[i]) for i, (source, target) in enumerate(moves)]
    for copy in copies:
        copy.start()
    for copy in copies:
        copy.wait()
    g = lax.axis_index("gz")
    last = lax.axis_size("gz") - 1
    lane = lanes((8, 128))
    pieces = []
    for v in range(8):
        piece = topo_ref[:, 128 * v : 128 * v + 128].reshape(8, 8, 128)
        pieces.append(jnp.sum(piece, axis=1))
    stacked = jnp.concatenate(pieces, axis=0)
    pick = (
        lax.broadcasted_iota(jnp.int32, (128, 128), 0) // 8 == lax.broadcasted_iota(jnp.int32, (128, 128), 1)
    ).astype(f32)
    sums = jnp.dot(stacked, pick, precision=lax.Precision.HIGHEST, preferred_element_type=f32)
    load = jnp.zeros((8, 128), f32)
    for v in range(8):
        load = load + rolled(sums[8 * v : 8 * v + 8], 16 * v)
    load = jnp.where(g == last, load * (-LOAD_GAIN / 64.0), 0.0)
    wide = lanes((64, 128))
    own = pl.ds(pl.multiple_of(g * 128, 128), 128)
    before = pl.ds(pl.multiple_of(jnp.maximum(g - 1, 0) * 128, 128), 128)
    after = pl.ds(pl.multiple_of(jnp.minimum(g + 1, last) * 128, 128), 128)
    for source, target in ((topo_ref, height_ref), (kappa_ref, conduct_ref)):
        target[:, 0:128] = source[:, own].astype(f32)
        side = jnp.where((wide < 8) & (g < last), source[:, after].astype(f32), 0.0)
        side = jnp.where((wide >= 120) & (g > 0), source[:, before].astype(f32), side)
        target[:, 128:256] = side
    width = topo_ref.shape[1]
    left = jnp.zeros((8, 128), f32)
    right = jnp.zeros((8, 128), f32)
    slot = 0
    for source in (topo_ref, kappa_ref):
        head = source[:, 0:128].astype(f32)
        tail = source[:, width - 128 : width].astype(f32)
        for r in range(8):
            mask = lane // 8 == slot
            left = jnp.where(mask, rolled(head[8 * r : 8 * r + 8], 8 * slot), left)
            right = jnp.where(mask, rolled(tail[8 * r : 8 * r + 8], 8 * slot - 120), right)
            slot += 1
    left_ref[1] = left
    right_ref[1] = right
    left = jnp.zeros((8, 128), f32)
    right = jnp.zeros((8, 128), f32)
    depths = visc_ref.shape[0]
    for field in range(4):
        for depth in range(depths):
            plane = visc_ref[depth] if field == 3 else force_ref[field, depth]
            if field == 2 and depth == depths - 1:
                plane = plane + load
            planes_ref[field, depth] = plane
            left, right = packed(plane, depth + 2, field, left, right, lane)
    left_ref[0] = left
    right_ref[0] = right


def is_even(axis):
    return lax.rem(lax.axis_index(axis), 2) == 0


def fetch(force_ref, visc_ref, odd_ref, even_ref, sems):
    depth = visc_ref.shape[0]
    start = jnp.where(is_even("gz"), 0, depth - 2)
    moves = []
    for target, first in ((odd_ref, start), (even_ref, depth - 2 - start)):
        moves.append((force_ref.at[:, pl.ds(first, 2)], target.at[0:3]))
        moves.append((visc_ref.at[pl.ds(first, 2)], target.at[3]))
    copies = [pltpu.make_async_copy(source, target, sems.at[i]) for i, (source, target) in enumerate(moves)]
    for copy in copies:
        copy.start()
    for copy in copies:
        copy.wait()


def packed(plane, depth, field, left, right, lane):
    first = 8 * depth + 2 * field
    mask = lane // 2 == first // 2
    left = jnp.where(mask, rolled(plane, first), left)
    return left, jnp.where(mask, rolled(plane, first - 126), right)


def assemble(own_ref, odd_ref, even_ref, left_ref, right_ref, planes_ref, odd_out, even_out):
    upward = is_even("gz")
    lane = lanes((8, 128))
    left, right = left_ref[0], right_ref[0]
    for field in range(4):
        for depth in range(DEPTHS):
            p = field * DEPTHS + depth
            if 2 <= depth < DEPTHS - 2:
                planes_ref[p] = own_ref[field, depth - 2]
                continue
            if depth < 2:
                plane = jnp.where(upward, odd_ref[field, depth], even_ref[field, depth])
            else:
                i = depth - (DEPTHS - 2)
                plane = jnp.where(upward, even_ref[field, i], odd_ref[field, i])
            planes_ref[p] = plane
            left, right = packed(plane, depth, field, left, right, lane)
    rightward = is_even("gy")
    odd_out[0] = jnp.where(rightward, left, right)
    even_out[0] = jnp.where(rightward, right, left)
    odd_out[1] = jnp.where(rightward, left_ref[1], right_ref[1])
    even_out[1] = jnp.where(rightward, right_ref[1], left_ref[1])


def edge_rows(planes_ref, low_ref, high_ref):
    for depth in range(DEPTHS):
        for field in range(4):
            plane = planes_ref.at[field * DEPTHS + depth]
            near = 8 * depth + field
            low_ref[near : near + 1, :] = plane[0:1, :]
            low_ref[near + 4 : near + 5, :] = plane[1:2, :]
            high_ref[near : near + 1, :] = plane[7:8, :]
            high_ref[near + 4 : near + 5, :] = plane[6:7, :]


def prepare_rows(
    low_ref, high_ref, own_odd, own_even, odd_ref, even_ref, height_ref, conduct_ref,
    odd_out, even_out, column_ref, height_out, conduct_out,
):
    g = lax.axis_index("gz")
    last = lax.axis_size("gz") - 1
    lane = lanes((8, 128))
    rightward = is_even("gy")

    def chosen(first, second, i):
        return jnp.where(rightward, first[i], second[i])

    before, after = chosen(odd_ref, even_ref, 0), chosen(even_ref, odd_ref, 0)
    before_surface, after_surface = chosen(odd_ref, even_ref, 1), chosen(even_ref, odd_ref, 1)
    side = lax.rem(lane, 2) == 0
    levels = (
        jnp.where(side, chosen(own_odd, own_even, 0), chosen(own_even, own_odd, 0)),
        jnp.where(side, rolled(before, -1), rolled(after, 1)),
        jnp.where(side, before, after),
    )
    downward = is_even("gx")

    def send(rows, low, high):
        odd_out[rows, :] = jnp.where(downward, low, high)
        even_out[rows, :] = jnp.where(downward, high, low)

    for depth in range(DEPTHS):
        rows = slice(8 * depth, 8 * depth + 8)
        send(rows, low_ref[rows, :], high_ref[rows, :])
    pad = [jnp.zeros((2, 128), f32)]
    send(
        slice(COLUMN_ROW, SURFACE_ROW),
        jnp.concatenate([x[0:2] for x in levels] + pad, axis=0),
        jnp.concatenate([x[6:8] for x in levels] + pad, axis=0),
    )
    for i in range(3):
        column_ref[i] = levels[i]
    slot = 0
    for index, (source, target) in enumerate(((height_ref, height_out), (conduct_ref, conduct_out))):
        base = SURFACE_ROW + 16 * index
        for r in range(8):
            rows = slice(8 * r, 8 * r + 8)
            main = source[rows, 0:128]
            side = source[rows, 128:256]
            side = jnp.where((g == 0) & (lane >= 120), rolled(before_surface, 120 - 8 * slot), side)
            side = jnp.where((g == last) & (lane < 8), rolled(after_surface, -8 * slot), side)
            target[rows, 0:128] = main
            target[rows, 128:256] = side
            if r == 0:
                first = (main, side)
            if r == 7:
                send(slice(base, base + 8), first[0], main)
                send(slice(base + 8, base + 16), first[1], side)
            slot += 1


def weighted(before, here, after):
    outer = before + after
    return outer, FACE * here + EDGE * outer, EDGE * here + CORNER * outer


def pair(x):
    return rolled(x, 1, 0) + rolled(x, x.shape[0] - 1, 0)


def lane_pair(x, lane, first, last):
    return jnp.where(lane == 0, first, rolled(x, 1)) + jnp.where(lane == 127, last, rolled(x, 127))


def row_pair(x, row, edge, field):
    up = jnp.where(row == 0, rolled(edge, -field, 0), rolled(x, 1, 0))
    return up + jnp.where(row == 7, rolled(edge, 3 - field, 0), rolled(x, 7, 0))


def to_first(x, depth, field):
    return rolled(x, -(8 * depth + 2 * field))


def to_last(x, depth, field):
    return rolled(x, 126 - (8 * depth + 2 * field))


def spread_rows(x, row):
    field = lax.rem(row, 4)
    for f in range(3):
        x = jnp.where(field == f, rolled(x, f - 3, 0), x)
    return x


def spread_columns(x, lane):
    field = lax.rem(lane, 8) // 2
    for f in range(3):
        x = jnp.where(field == f, rolled(x, 2 * (f - 3)), x)
    return x


def column_sums(levels):
    parts = [weighted(rolled(x, 8), x, rolled(x, 120)) for x in levels]
    (_, ai, bi), (outer, an, bn), (_, af, bf) = parts
    beside = an + pair(bn)
    return FACE * outer + pair(an) + (ai + af) + pair(bi + bf), beside


def beside_rows(beside, depth, row):
    near = jnp.where(row < 4, jnp.broadcast_to(beside[15:16], (8, 128)), jnp.broadcast_to(beside[8:9], (8, 128)))
    field = lax.rem(row, 4)
    first, last = to_first(near, depth, 0), to_last(near, depth, 0)
    for f in range(1, 4):
        first = jnp.where(field == f, to_first(near, depth, f), first)
        last = jnp.where(field == f, to_last(near, depth, f), last)
    return first, last


def sided(odd_ref, even_ref, axis):
    first = is_even(axis)

    def before(rows):
        return jnp.where(first, odd_ref[rows, :], even_ref[rows, :])

    def after(rows):
        return jnp.where(first, even_ref[rows, :], odd_ref[rows, :])

    return before, after


def flux(conduct, slope):
    return conduct * slope * lax.rsqrt(1.0 + slope * slope)


def steps(h, k):
    rows = h.shape[0]
    inside = k > 0.0
    along = 0.5 * (k + rolled(k, 255, 1))
    along_before = rolled(along, 1, 1)
    across = 0.5 * (k + rolled(k, rows - 1, 0))
    for step in range(STEPS):
        q = flux(along, rolled(h, 255, 1) - h) - flux(along_before, h - rolled(h, 1, 1))
        r = flux(across, rolled(h, rows - 1, 0) - h)
        h = jnp.where(inside, h + TIME_STEP * (q + (r - rolled(r, 1, 0))), 0.0)
    return h


def inner_rows(height_ref, conduct_ref, out_ref):
    out_ref[...] = steps(height_ref[...], conduct_ref[...])[8:56, 0:128]


def operate(
    planes_ref, low_ref, high_ref, column_ref, odd_ref, even_ref, height_ref, conduct_ref, inner_ref,
    image_ref, sums_ref, top_ref, out_ref,
):
    lane = lanes((8, 128))
    row = lax.broadcasted_iota(jnp.int32, (8, 128), 0)
    wide = lanes((16, 128))
    before, after = sided(odd_ref, even_ref, "gx")

    def banded(source, base):
        def joined(side):
            return jnp.concatenate([side(slice(base, base + 8)), side(slice(base + 8, base + 16))], axis=1)

        return jnp.concatenate([source[48:64, :], joined(after), joined(before), source[0:16, :]], axis=0)

    band = steps(banded(height_ref, SURFACE_ROW), banded(conduct_ref, SURFACE_ROW + 16))
    out_ref[0:8, :] = band[32:40, 0:128]
    out_ref[8:56, :] = inner_ref[...]
    out_ref[56:64, :] = band[8:16, 0:128]
    columns = []
    for i in range(3):
        rows = slice(COLUMN_ROW + 2 * i, COLUMN_ROW + 2 * i + 2)
        columns.append(jnp.concatenate([column_ref[i], after(rows), jnp.zeros((4, 128), f32), before(rows)], axis=0))
    column_eta = [spread_columns(x, wide) for x in columns]
    column_sum, beside = column_sums(columns)
    column_sum_eta, beside_eta = column_sums([x * y for x, y in zip(columns, column_eta)])
    near_eta = column_eta[1]
    column_diag = DRAG + TOTAL * near_eta + spread_columns(column_sum, wide)
    column_image = columns[1] * column_diag - near_eta * column_sum - column_sum_eta
    column_image = jnp.where(near_eta > 0.0, column_image, 0.0)
    rows_of, rows_eta = [], []
    for depth in range(DEPTHS):
        rows = slice(8 * depth, 8 * depth + 8)
        b, a = before(rows), after(rows)
        found = (
            jnp.where(row < 4, low_ref[rows, :], rolled(high_ref[rows, :], 4, 0)),
            jnp.where(row < 4, b, rolled(a, 4, 0)),
            jnp.where(row < 4, rolled(b, 4, 0), a),
        )
        rows_of.append(found)
        rows_eta.append([spread_rows(x, row) for x in found])
    rows_product = [[x * y for x, y in zip(found, etas)] for found, etas in zip(rows_of, rows_eta)]

    def row_sums(levels, depth, beside_columns):
        parts = [weighted(levels[depth - 1][i], levels[depth][i], levels[depth + 1][i]) for i in range(3)]
        (_, ai, bi), (outer, an, bn), (_, af, bf) = parts
        first, last = beside_rows(beside_columns, depth, row)
        return FACE * outer + (ai + af) + lane_pair(an + (bi + bf), lane, first, last), an, bn

    def plane_sum(three, an, bn, beside_columns, depth, field):
        outer, a, b = weighted(*three)
        both = a + row_pair(b, row, bn, field)
        own = beside_columns[0:8]
        sides = lane_pair(both, lane, to_first(own, depth, field), to_last(own, depth, field))
        return FACE * outer + row_pair(a, row, an, field) + sides

    def plane(field, depth):
        return planes_ref[field * DEPTHS + depth]

    image, row_image, diagonal = {}, {}, {}
    for depth in range(1, DEPTHS - 1):
        row_sum, an, bn = row_sums(rows_of, depth, beside)
        row_sum_eta, an_eta, bn_eta = row_sums(rows_product, depth, beside_eta)
        near, eta = rows_of[depth][1], rows_eta[depth][1]
        diag = DRAG + TOTAL * eta + spread_rows(row_sum, row)
        row_image[depth] = jnp.where(eta > 0.0, near * diag - eta * row_sum - row_sum_eta, 0.0)
        e = [plane(3, depth + i) for i in (-1, 0, 1)]
        diag = DRAG + TOTAL * e[1] + plane_sum(e, an, bn, beside, depth, 3)
        diagonal[depth] = diag
        for c in range(3):
            v = [plane(c, depth + i) for i in (-1, 0, 1)]
            ev = [x * y for x, y in zip(e, v)]
            out = v[1] * diag - e[1] * plane_sum(v, an, bn, beside, depth, c)
            out = out - plane_sum(ev, an_eta, bn_eta, beside_eta, depth, c)
            image[c, depth] = jnp.where(e[1] > 0.0, out, 0.0)
    _, an, bn = weighted(rolled(column_image, 8), column_image, rolled(column_image, 120))
    beside = an + pair(bn)
    m = [jnp.zeros((8, 128), f32) for _ in range(4)]
    for depth in range(2, DEPTHS - 2):
        _, an, bn = weighted(row_image[depth - 1], row_image[depth], row_image[depth + 1])
        e = plane(3, depth)
        for c in range(3):
            s = plane_sum([image[c, depth + i] for i in (-1, 0, 1)], an, bn, beside, depth, c)
            v, q = plane(c, depth), image[c, depth]
            image_ref[c, depth - 2] = q
            m[0] = m[0] + v * v
            m[1] = m[1] + v * q
            m[2] = m[2] + q * q
            m[3] = m[3] + q * (q * diagonal[depth] - 2.0 * (e * s))
    total = jnp.zeros((8, 128), f32)
    for k in range(4):
        part = m[k]
        for amount in (64, 32, 16):
            part = part + rolled(part, amount)
        total = jnp.where(lane // 16 == 2 + k, part, total)
    for amount in (4, 2, 1):
        total = total + rolled(total, amount, 0)
    for i in range(sums_ref.shape[0] // 8):
        sums_ref[8 * i : 8 * i + 8, :] = total
    top_ref[0] = plane(2, DEPTHS - 3)
    top_ref[1] = image[2, DEPTHS - 3]


def middle(sums_ref, top_ref, out_ref):
    lane = lanes((8, 128))
    row = lax.broadcasted_iota(jnp.int32, (8, 128), 0)
    part = jnp.sum(sums_ref[...], axis=0, keepdims=True)
    flat = []
    for i in range(2):
        found = top_ref[i]
        for k in range(1, 8):
            found = jnp.where(
                lane // 16 == lax.rem(row + k, 8), rolled(rolled(top_ref[i], -k, 0), 16 * k), found
            )
        flat.append(found)
    for j in range(out_ref.shape[0]):
        out_ref[j, 0:1, :] = flat[0][j : j + 1]
        out_ref[j, 1:2, :] = flat[1][j : j + 1]
        out_ref[j, 2:3, :] = part
        out_ref[j, 3:4, :] = part


def finish(parts_ref, planes_ref, image_ref, height_ref, velocity_hbm, surface_hbm, velocity_ref, surface_ref, sems):
    count = parts_ref.shape[0]
    lane = lanes((1, 128))
    row = lax.broadcasted_iota(jnp.int32, (8, 128), 0)
    found = []
    for i in range(2):
        flat = jnp.broadcast_to(parts_ref[count - 1, i : i + 1, :], (8, 128))
        cells = flat
        for r in range(1, 8):
            cells = jnp.where(row == r, rolled(flat, -16 * r), cells)
        found.append(cells)
    top = jnp.where(lanes((16, 128)) < 16, jnp.concatenate(found, axis=0), 0.0)
    spread = (
        lax.broadcasted_iota(jnp.int32, (128, 128), 1) // 8 == lax.broadcasted_iota(jnp.int32, (128, 128), 0)
    ).astype(f32)
    wide = jnp.dot(top, spread, precision=lax.Precision.HIGHEST, preferred_element_type=f32)
    total = parts_ref[0, 2:3, :]
    for j in range(1, count):
        total = total + parts_ref[j, 2:3, :]

    def moment(k):
        return jnp.sum(jnp.where(lane // 16 == 2 + k, total, 0.0), axis=1, keepdims=True)

    m0, m1, m2, m3 = (moment(k) for k in range(4))
    first = m0 / m1
    later = first * first * m2 - m0
    gain = 1.0 + later / m0
    second = later / (gain * gain * m1 - 2.0 * first * gain * m2 + first * first * m3)
    on_force = first + second * gain
    on_image = -(second * first)
    for c in range(3):
        for depth in range(8):
            velocity_ref[c, depth] = on_force * planes_ref[c * DEPTHS + depth + 2] + on_image * image_ref[c, depth]
    velocity_copy = pltpu.make_async_copy(velocity_ref, velocity_hbm, sems.at[0])
    velocity_copy.start()
    rise = (STEPS * TIME_STEP) * (on_force * wide[0:8] + on_image * wide[8:16])
    for r in range(8):
        rows = slice(8 * r, 8 * r + 8)
        surface_ref[rows, :] = height_ref[rows, :] + jnp.broadcast_to(rise[r : r + 1, :], (8, 128))
    surface_copy = pltpu.make_async_copy(surface_ref, surface_hbm, sems.at[1])
    surface_copy.start()
    velocity_copy.wait()
    surface_copy.wait()


def swap(odd, even, axis):
    count = lax.axis_size(axis)

    def pairs(start):
        found = []
        for i in range(start, count - 1, 2):
            found += [(i, i + 1), (i + 1, i)]
        return found

    return lax.ppermute(odd, axis, pairs(1)), lax.ppermute(even, axis, pairs(0))


def local(body_force, viscosity, topography, kappa):
    inputs = [
        pltpu.with_memory_space_constraint(x, pltpu.HBM) for x in (body_force, viscosity, topography, kappa)
    ]
    odd, even = pl.pallas_call(
        fetch,
        out_shape=[jax.ShapeDtypeStruct((4, 2, 8, 128), f32)] * 2,
        in_specs=[pl.BlockSpec(memory_space=pltpu.HBM)] * 2,
        out_specs=[vmem()] * 2,
        scratch_shapes=[pltpu.SemaphoreType.DMA((4,))],
        compiler_params=pltpu.CompilerParams(vmem_limit_bytes=1 << 20),
    )(*inputs[:2])
    odd, even = swap(odd, even, "gz")
    planes, left, right, height, conduct = pl.pallas_call(
        own_block,
        out_shape=[
            jax.ShapeDtypeStruct(shape, f32)
            for shape in ((4, 8, 8, 128), (2, 8, 128), (2, 8, 128), (64, 256), (64, 256))
        ],
        in_specs=[pl.BlockSpec(memory_space=pltpu.HBM)] * 4,
        out_specs=[vmem()] * 5,
        scratch_shapes=[pltpu.VMEM(x.shape, x.dtype) for x in inputs] + [pltpu.SemaphoreType.DMA((4,))],
        compiler_params=pltpu.CompilerParams(vmem_limit_bytes=8 << 20),
        cost_estimate=pl.CostEstimate(flops=20000 * 1024, bytes_accessed=1 << 18, transcendentals=0),
    )(*inputs)
    planes, odd, even = call(
        assemble,
        [(PLANES, 8, 128), (2, 8, 128), (2, 8, 128)],
        (planes, odd, even, left, right),
    )
    own = (odd, even)
    odd, even = swap(odd, even, "gy")
    low, high = call(edge_rows, [(COLUMN_ROW, 128)] * 2, (planes,))
    odd, even, columns, height, conduct = call(
        prepare_rows,
        [(GX_ROWS, 128), (GX_ROWS, 128), (3, 8, 128), (64, 256), (64, 256)],
        (low, high, *own, odd, even, height, conduct),
    )
    odd, even = swap(odd, even, "gx")
    (inner,) = call(inner_rows, [(48, 128)], (height, conduct))
    group = lax.axis_size("gx") * lax.axis_size("gy")
    image, sums, top, height = call(
        operate,
        [(3, 8, 8, 128), (group, 128), (2, 8, 128), (64, 128)],
        (planes, low, high, columns, odd, even, height, conduct, inner),
    )
    sums = lax.all_to_all(sums.reshape(group, 1, 128), ("gx", "gy"), 0, 0)
    (parts,) = call(middle, [(lax.axis_size("gz"), 4, 128)], (sums.reshape(group, 128), top))
    parts = lax.all_to_all(parts, "gz", 0, 0)
    shapes = ((3, 8, 8, 128), (64, 128))
    velocity, surface = pl.pallas_call(
        finish,
        out_shape=[jax.ShapeDtypeStruct(shape, f32) for shape in shapes],
        in_specs=[vmem()] * 4,
        out_specs=[pl.BlockSpec(memory_space=pltpu.HBM)] * 2,
        scratch_shapes=[pltpu.VMEM(shape, f32) for shape in shapes] + [pltpu.SemaphoreType.DMA((2,))],
        compiler_params=pltpu.CompilerParams(vmem_limit_bytes=8 << 20),
    )(parts, planes, image, height)
    return velocity, surface


def solution(mesh):
    in_specs = (P(None, "gz", "gx", "gy"), P("gz", "gx", "gy"), P("gx", "gy"), P("gx", "gy"))
    out_specs = (P(None, "gz", "gx", "gy"), P("gx", ("gy", "gz")))
    return jax.shard_map(local, mesh=mesh, in_specs=in_specs, out_specs=out_specs, check_vma=False)
```

```python
import jax
import jax.numpy as jnp
from jax import lax
from jax.experimental import pallas as pl
from jax.experimental.pallas import tpu as pltpu
from jax.sharding import PartitionSpec as P

STEPS = 8
DRAG = 1.0
TIME_STEP = 1.0
LOAD_GAIN = 4.0
FACE, EDGE, CORNER = 0.5, 0.25, 0.5 / 3.0
TOTAL = 6 * FACE + 12 * EDGE + 8 * CORNER

DEPTHS = 12
PLANES = 4 * DEPTHS
COLUMN_ROW = 8 * DEPTHS
SURFACE_ROW = COLUMN_ROW + 8
GX_ROWS = SURFACE_ROW + 16

f32 = jnp.float32


def vmem():
    return pl.BlockSpec(memory_space=pltpu.VMEM)


def call(body, outs, ins, scratch=(), cost=20000, limit=8 << 20):
    return pl.pallas_call(
        body,
        out_shape=[jax.ShapeDtypeStruct(s, f32) for s in outs],
        in_specs=[vmem() for _ in ins],
        out_specs=[vmem() for _ in outs],
        scratch_shapes=list(scratch),
        compiler_params=pltpu.CompilerParams(vmem_limit_bytes=limit),
        cost_estimate=pl.CostEstimate(flops=cost * 1024, bytes_accessed=1 << 18, transcendentals=0),
    )(*ins)


def lanes(shape):
    return lax.broadcasted_iota(jnp.int32, shape, len(shape) - 1)


def rolled(x, amount, axis=1):
    amount = amount % x.shape[axis]
    return x if amount == 0 else pltpu.roll(x, amount, axis)


def own_block(
    force_hbm, visc_hbm, topo_hbm, kappa_hbm, planes_ref, left_ref, right_ref, height_ref, conduct_ref,
    force_ref, visc_ref, topo_ref, kappa_ref, sems,
):
    moves = ((topo_hbm, topo_ref), (kappa_hbm, kappa_ref), (force_hbm, force_ref), (visc_hbm, visc_ref))
    copies = [pltpu.make_async_copy(source, target, sems.at[i]) for i, (source, target) in enumerate(moves)]
    for copy in copies:
        copy.start()
    for copy in copies:
        copy.wait()
    g = lax.axis_index("gz")
    last = lax.axis_size("gz") - 1
    lane = lanes((8, 128))
    pieces = []
    for v in range(8):
        piece = topo_ref[:, 128 * v : 128 * v + 128].reshape(8, 8, 128)
        pieces.append(jnp.sum(piece, axis=1))
    stacked = jnp.concatenate(pieces, axis=0)
    pick = (
        lax.broadcasted_iota(jnp.int32, (128, 128), 0) // 8 == lax.broadcasted_iota(jnp.int32, (128, 128), 1)
    ).astype(f32)
    sums = jnp.dot(stacked, pick, precision=lax.Precision.HIGHEST, preferred_element_type=f32)
    load = jnp.zeros((8, 128), f32)
    for v in range(8):
        load = load + rolled(sums[8 * v : 8 * v + 8], 16 * v)
    load = jnp.where(g == last, load * (-LOAD_GAIN / 64.0), 0.0)
    wide = lanes((64, 128))
    own = pl.ds(pl.multiple_of(g * 128, 128), 128)
    before = pl.ds(pl.multiple_of(jnp.maximum(g - 1, 0) * 128, 128), 128)
    after = pl.ds(pl.multiple_of(jnp.minimum(g + 1, last) * 128, 128), 128)
    for source, target in ((topo_ref, height_ref), (kappa_ref, conduct_ref)):
        target[:, 0:128] = source[:, own].astype(f32)
        side = jnp.where((wide < 8) & (g < last), source[:, after].astype(f32), 0.0)
        side = jnp.where((wide >= 120) & (g > 0), source[:, before].astype(f32), side)
        target[:, 128:256] = side
    width = topo_ref.shape[1]
    left = jnp.zeros((8, 128), f32)
    right = jnp.zeros((8, 128), f32)
    slot = 0
    for source in (topo_ref, kappa_ref):
        head = source[:, 0:128].astype(f32)
        tail = source[:, width - 128 : width].astype(f32)
        for r in range(8):
            mask = lane // 8 == slot
            left = jnp.where(mask, rolled(head[8 * r : 8 * r + 8], 8 * slot), left)
            right = jnp.where(mask, rolled(tail[8 * r : 8 * r + 8], 8 * slot - 120), right)
            slot += 1
    left_ref[1] = left
    right_ref[1] = right
    left = jnp.zeros((8, 128), f32)
    right = jnp.zeros((8, 128), f32)
    depths = visc_ref.shape[0]
    for field in range(4):
        for depth in range(depths):
            plane = visc_ref[depth] if field == 3 else force_ref[field, depth]
            if field == 2 and depth == depths - 1:
                plane = plane + load
            planes_ref[field, depth] = plane
            left, right = packed(plane, depth + 2, field, left, right, lane)
    left_ref[0] = left
    right_ref[0] = right


def is_even(axis):
    return lax.rem(lax.axis_index(axis), 2) == 0


def fetch(force_ref, visc_ref, odd_ref, even_ref, sems):
    depth = visc_ref.shape[0]
    start = jnp.where(is_even("gz"), 0, depth - 2)
    moves = []
    for target, first in ((odd_ref, start), (even_ref, depth - 2 - start)):
        moves.append((force_ref.at[:, pl.ds(first, 2)], target.at[0:3]))
        moves.append((visc_ref.at[pl.ds(first, 2)], target.at[3]))
    copies = [pltpu.make_async_copy(source, target, sems.at[i]) for i, (source, target) in enumerate(moves)]
    for copy in copies:
        copy.start()
    for copy in copies:
        copy.wait()


def packed(plane, depth, field, left, right, lane):
    first = 8 * depth + 2 * field
    mask = lane // 2 == first // 2
    left = jnp.where(mask, rolled(plane, first), left)
    return left, jnp.where(mask, rolled(plane, first - 126), right)


def assemble(own_ref, odd_ref, even_ref, left_ref, right_ref, planes_ref, odd_out, even_out):
    upward = is_even("gz")
    lane = lanes((8, 128))
    left, right = left_ref[0], right_ref[0]
    for field in range(4):
        for depth in range(DEPTHS):
            p = field * DEPTHS + depth
            if 2 <= depth < DEPTHS - 2:
                planes_ref[p] = own_ref[field, depth - 2]
                continue
            if depth < 2:
                plane = jnp.where(upward, odd_ref[field, depth], even_ref[field, depth])
            else:
                i = depth - (DEPTHS - 2)
                plane = jnp.where(upward, even_ref[field, i], odd_ref[field, i])
            planes_ref[p] = plane
            left, right = packed(plane, depth, field, left, right, lane)
    rightward = is_even("gy")
    odd_out[0] = jnp.where(rightward, left, right)
    even_out[0] = jnp.where(rightward, right, left)
    odd_out[1] = jnp.where(rightward, left_ref[1], right_ref[1])
    even_out[1] = jnp.where(rightward, right_ref[1], left_ref[1])


def edge_rows(planes_ref, low_ref, high_ref):
    for depth in range(DEPTHS):
        for field in range(4):
            plane = planes_ref.at[field * DEPTHS + depth]
            near = 8 * depth + field
            low_ref[near : near + 1, :] = plane[0:1, :]
            low_ref[near + 4 : near + 5, :] = plane[1:2, :]
            high_ref[near : near + 1, :] = plane[7:8, :]
            high_ref[near + 4 : near + 5, :] = plane[6:7, :]


def prepare_rows(
    low_ref, high_ref, own_odd, own_even, odd_ref, even_ref, height_ref, conduct_ref,
    odd_out, even_out, column_ref, height_out, conduct_out,
):
    g = lax.axis_index("gz")
    last = lax.axis_size("gz") - 1
    lane = lanes((8, 128))
    rightward = is_even("gy")

    def chosen(first, second, i):
        return jnp.where(rightward, first[i], second[i])

    before, after = chosen(odd_ref, even_ref, 0), chosen(even_ref, odd_ref, 0)
    before_surface, after_surface = chosen(odd_ref, even_ref, 1), chosen(even_ref, odd_ref, 1)
    side = lax.rem(lane, 2) == 0
    levels = (
        jnp.where(side, chosen(own_odd, own_even, 0), chosen(own_even, own_odd, 0)),
        jnp.where(side, rolled(before, -1), rolled(after, 1)),
        jnp.where(side, before, after),
    )
    downward = is_even("gx")

    def send(rows, low, high):
        odd_out[rows, :] = jnp.where(downward, low, high)
        even_out[rows, :] = jnp.where(downward, high, low)

    for depth in range(DEPTHS):
        rows = slice(8 * depth, 8 * depth + 8)
        send(rows, low_ref[rows, :], high_ref[rows, :])
    for i in range(3):
        column_ref[i] = levels[i]
    slot = 0
    low_sides, high_sides = [], []
    for index, (source, target) in enumerate(((height_ref, height_out), (conduct_ref, conduct_out))):
        base = SURFACE_ROW + 8 * index
        for r in range(8):
            rows = slice(8 * r, 8 * r + 8)
            main = source[rows, 0:128]
            side = source[rows, 128:256]
            side = jnp.where((g == 0) & (lane >= 120), rolled(before_surface, 120 - 8 * slot), side)
            side = jnp.where((g == last) & (lane < 8), rolled(after_surface, -8 * slot), side)
            target[rows, 0:128] = main
            target[rows, 128:256] = side
            if r == 0:
                first = main
                low_sides.append(side)
            if r == 7:
                send(slice(base, base + 8), first, main)
                high_sides.append(side)
            slot += 1
    pad = [jnp.zeros((2, 128), f32)]
    shared = []
    for sides, rows in ((low_sides, slice(0, 2)), (high_sides, slice(6, 8))):
        found = rolled(jnp.concatenate([x[rows] for x in levels] + pad, axis=0), 16)
        found = jnp.where((lane < 8) | (lane >= 120), sides[0], found)
        found = jnp.where(lane // 8 == 1, rolled(sides[1], 8), found)
        shared.append(jnp.where(lane // 8 == 14, rolled(sides[1], -8), found))
    send(slice(COLUMN_ROW, SURFACE_ROW), *shared)


def weighted(before, here, after):
    outer = before + after
    return outer, FACE * here + EDGE * outer, EDGE * here + CORNER * outer


def pair(x):
    return rolled(x, 1, 0) + rolled(x, x.shape[0] - 1, 0)


def lane_pair(x, lane, first, last):
    return jnp.where(lane == 0, first, rolled(x, 1)) + jnp.where(lane == 127, last, rolled(x, 127))


def row_pair(x, row, edge, field):
    up = jnp.where(row == 0, rolled(edge, -field, 0), rolled(x, 1, 0))
    return up + jnp.where(row == 7, rolled(edge, 3 - field, 0), rolled(x, 7, 0))


def to_first(x, depth, field):
    return rolled(x, -(8 * depth + 2 * field))


def to_last(x, depth, field):
    return rolled(x, 126 - (8 * depth + 2 * field))


def spread_rows(x, row):
    field = lax.rem(row, 4)
    for f in range(3):
        x = jnp.where(field == f, rolled(x, f - 3, 0), x)
    return x


def spread_columns(x, lane):
    field = lax.rem(lane, 8) // 2
    for f in range(3):
        x = jnp.where(field == f, rolled(x, 2 * (f - 3)), x)
    return x


def column_sums(levels):
    parts = [weighted(rolled(x, 8), x, rolled(x, 120)) for x in levels]
    (_, ai, bi), (outer, an, bn), (_, af, bf) = parts
    beside = an + pair(bn)
    return FACE * outer + pair(an) + (ai + af) + pair(bi + bf), beside


def beside_rows(beside, depth, row):
    near = jnp.where(row < 4, jnp.broadcast_to(beside[15:16], (8, 128)), jnp.broadcast_to(beside[8:9], (8, 128)))
    field = lax.rem(row, 4)
    first, last = to_first(near, depth, 0), to_last(near, depth, 0)
    for f in range(1, 4):
        first = jnp.where(field == f, to_first(near, depth, f), first)
        last = jnp.where(field == f, to_last(near, depth, f), last)
    return first, last


def sided(odd_ref, even_ref, axis):
    first = is_even(axis)

    def before(rows):
        return jnp.where(first, odd_ref[rows, :], even_ref[rows, :])

    def after(rows):
        return jnp.where(first, even_ref[rows, :], odd_ref[rows, :])

    return before, after


def flux(conduct, slope):
    return conduct * slope * lax.rsqrt(1.0 + slope * slope)


def steps(h, k):
    rows = h.shape[0]
    inside = k > 0.0
    along = 0.5 * (k + rolled(k, 255, 1))
    along_before = rolled(along, 1, 1)
    across = 0.5 * (k + rolled(k, rows - 1, 0))
    for step in range(STEPS):
        q = flux(along, rolled(h, 255, 1) - h) - flux(along_before, h - rolled(h, 1, 1))
        r = flux(across, rolled(h, rows - 1, 0) - h)
        h = jnp.where(inside, h + TIME_STEP * (q + (r - rolled(r, 1, 0))), 0.0)
    return h


def inner_rows(height_ref, conduct_ref, out_ref):
    out_ref[...] = steps(height_ref[...], conduct_ref[...])[8:56, 0:128]


def operate(
    planes_ref, low_ref, high_ref, column_ref, odd_ref, even_ref, height_ref, conduct_ref, inner_ref,
    image_ref, sums_ref, top_ref, out_ref,
):
    lane = lanes((8, 128))
    row = lax.broadcasted_iota(jnp.int32, (8, 128), 0)
    wide = lanes((16, 128))
    before, after = sided(odd_ref, even_ref, "gx")

    def parted(shared):
        edge = (lane < 8) | (lane >= 120)
        conduct = jnp.where(lane < 8, rolled(shared, -8), jnp.where(lane >= 120, rolled(shared, 8), 0.0))
        return jnp.where(edge, shared, 0.0), conduct, jnp.where(lane < 96, rolled(shared, -16), 0.0)

    shared_before = parted(before(slice(COLUMN_ROW, SURFACE_ROW)))
    shared_after = parted(after(slice(COLUMN_ROW, SURFACE_ROW)))

    def banded(source, index):
        rows = slice(SURFACE_ROW + 8 * index, SURFACE_ROW + 8 * index + 8)
        outer = [
            jnp.concatenate([side(rows), shared[index]], axis=1)
            for side, shared in ((after, shared_after), (before, shared_before))
        ]
        return jnp.concatenate([source[48:64, :], *outer, source[0:16, :]], axis=0)

    band = steps(banded(height_ref, 0), banded(conduct_ref, 1))
    out_ref[0:8, :] = band[32:40, 0:128]
    out_ref[8:56, :] = inner_ref[...]
    out_ref[56:64, :] = band[8:16, 0:128]
    columns = []
    for i in range(3):
        rows = slice(2 * i, 2 * i + 2)
        halo = [shared_after[2][rows], jnp.zeros((4, 128), f32), shared_before[2][rows]]
        columns.append(jnp.concatenate([column_ref[i], *halo], axis=0))
    column_eta = [spread_columns(x, wide) for x in columns]
    column_sum, beside = column_sums(columns)
    column_sum_eta, beside_eta = column_sums([x * y for x, y in zip(columns, column_eta)])
    near_eta = column_eta[1]
    column_diag = DRAG + TOTAL * near_eta + spread_columns(column_sum, wide)
    column_image = columns[1] * column_diag - near_eta * column_sum - column_sum_eta
    column_image = jnp.where(near_eta > 0.0, column_image, 0.0)
    rows_of, rows_eta = [], []
    for depth in range(DEPTHS):
        rows = slice(8 * depth, 8 * depth + 8)
        b, a = before(rows), after(rows)
        found = (
            jnp.where(row < 4, low_ref[rows, :], rolled(high_ref[rows, :], 4, 0)),
            jnp.where(row < 4, b, rolled(a, 4, 0)),
            jnp.where(row < 4, rolled(b, 4, 0), a),
        )
        rows_of.append(found)
        rows_eta.append([spread_rows(x, row) for x in found])
    rows_product = [[x * y for x, y in zip(found, etas)] for found, etas in zip(rows_of, rows_eta)]

    def row_sums(levels, depth, beside_columns):
        parts = [weighted(levels[depth - 1][i], levels[depth][i], levels[depth + 1][i]) for i in range(3)]
        (_, ai, bi), (outer, an, bn), (_, af, bf) = parts
        first, last = beside_rows(beside_columns, depth, row)
        return FACE * outer + (ai + af) + lane_pair(an + (bi + bf), lane, first, last), an, bn

    def plane_sum(three, an, bn, beside_columns, depth, field):
        outer, a, b = weighted(*three)
        both = a + row_pair(b, row, bn, field)
        own = beside_columns[0:8]
        sides = lane_pair(both, lane, to_first(own, depth, field), to_last(own, depth, field))
        return FACE * outer + row_pair(a, row, an, field) + sides

    def plane(field, depth):
        return planes_ref[field * DEPTHS + depth]

    image, row_image, diagonal = {}, {}, {}
    for depth in range(1, DEPTHS - 1):
        row_sum, an, bn = row_sums(rows_of, depth, beside)
        row_sum_eta, an_eta, bn_eta = row_sums(rows_product, depth, beside_eta)
        near, eta = rows_of[depth][1], rows_eta[depth][1]
        diag = DRAG + TOTAL * eta + spread_rows(row_sum, row)
        row_image[depth] = jnp.where(eta > 0.0, near * diag - eta * row_sum - row_sum_eta, 0.0)
        e = [plane(3, depth + i) for i in (-1, 0, 1)]
        diag = DRAG + TOTAL * e[1] + plane_sum(e, an, bn, beside, depth, 3)
        diagonal[depth] = diag
        for c in range(3):
            v = [plane(c, depth + i) for i in (-1, 0, 1)]
            ev = [x * y for x, y in zip(e, v)]
            out = v[1] * diag - e[1] * plane_sum(v, an, bn, beside, depth, c)
            out = out - plane_sum(ev, an_eta, bn_eta, beside_eta, depth, c)
            image[c, depth] = jnp.where(e[1] > 0.0, out, 0.0)
    _, an, bn = weighted(rolled(column_image, 8), column_image, rolled(column_image, 120))
    beside = an + pair(bn)
    m = [jnp.zeros((8, 128), f32) for _ in range(4)]
    for depth in range(2, DEPTHS - 2):
        _, an, bn = weighted(row_image[depth - 1], row_image[depth], row_image[depth + 1])
        e = plane(3, depth)
        for c in range(3):
            s = plane_sum([image[c, depth + i] for i in (-1, 0, 1)], an, bn, beside, depth, c)
            v, q = plane(c, depth), image[c, depth]
            image_ref[c, depth - 2] = q
            m[0] = m[0] + v * v
            m[1] = m[1] + v * q
            m[2] = m[2] + q * q
            m[3] = m[3] + q * (q * diagonal[depth] - 2.0 * (e * s))
    total = jnp.zeros((8, 128), f32)
    for k in range(4):
        part = m[k]
        for amount in (64, 32, 16):
            part = part + rolled(part, amount)
        total = jnp.where(lane // 16 == 2 + k, part, total)
    for amount in (4, 2, 1):
        total = total + rolled(total, amount, 0)
    for i in range(sums_ref.shape[0] // 8):
        sums_ref[8 * i : 8 * i + 8, :] = total
    top_ref[0] = plane(2, DEPTHS - 3)
    top_ref[1] = image[2, DEPTHS - 3]


def middle(sums_ref, top_ref, out_ref):
    lane = lanes((8, 128))
    row = lax.broadcasted_iota(jnp.int32, (8, 128), 0)
    part = jnp.sum(sums_ref[...], axis=0, keepdims=True)
    flat = []
    for i in range(2):
        found = top_ref[i]
        for k in range(1, 8):
            found = jnp.where(
                lane // 16 == lax.rem(row + k, 8), rolled(rolled(top_ref[i], -k, 0), 16 * k), found
            )
        flat.append(found)
    for j in range(out_ref.shape[0]):
        out_ref[j, 0:1, :] = flat[0][j : j + 1]
        out_ref[j, 1:2, :] = flat[1][j : j + 1]
        out_ref[j, 2:3, :] = part
        out_ref[j, 3:4, :] = part


def finish(parts_ref, planes_ref, image_ref, height_ref, velocity_hbm, surface_hbm, velocity_ref, surface_ref, sems):
    count = parts_ref.shape[0]
    lane = lanes((1, 128))
    row = lax.broadcasted_iota(jnp.int32, (8, 128), 0)
    found = []
    for i in range(2):
        flat = jnp.broadcast_to(parts_ref[count - 1, i : i + 1, :], (8, 128))
        cells = flat
        for r in range(1, 8):
            cells = jnp.where(row == r, rolled(flat, -16 * r), cells)
        found.append(cells)
    top = jnp.where(lanes((16, 128)) < 16, jnp.concatenate(found, axis=0), 0.0)
    spread = (
        lax.broadcasted_iota(jnp.int32, (128, 128), 1) // 8 == lax.broadcasted_iota(jnp.int32, (128, 128), 0)
    ).astype(f32)
    wide = jnp.dot(top, spread, precision=lax.Precision.HIGHEST, preferred_element_type=f32)
    total = parts_ref[0, 2:3, :]
    for j in range(1, count):
        total = total + parts_ref[j, 2:3, :]

    def moment(k):
        return jnp.sum(jnp.where(lane // 16 == 2 + k, total, 0.0), axis=1, keepdims=True)

    m0, m1, m2, m3 = (moment(k) for k in range(4))
    first = m0 / m1
    later = first * first * m2 - m0
    gain = 1.0 + later / m0
    second = later / (gain * gain * m1 - 2.0 * first * gain * m2 + first * first * m3)
    on_force = first + second * gain
    on_image = -(second * first)
    for c in range(3):
        for depth in range(8):
            velocity_ref[c, depth] = on_force * planes_ref[c * DEPTHS + depth + 2] + on_image * image_ref[c, depth]
    velocity_copy = pltpu.make_async_copy(velocity_ref, velocity_hbm, sems.at[0])
    velocity_copy.start()
    rise = (STEPS * TIME_STEP) * (on_force * wide[0:8] + on_image * wide[8:16])
    for r in range(8):
        rows = slice(8 * r, 8 * r + 8)
        surface_ref[rows, :] = height_ref[rows, :] + jnp.broadcast_to(rise[r : r + 1, :], (8, 128))
    surface_copy = pltpu.make_async_copy(surface_ref, surface_hbm, sems.at[1])
    surface_copy.start()
    velocity_copy.wait()
    surface_copy.wait()


def swap(odd, even, axis):
    count = lax.axis_size(axis)

    def pairs(start):
        found = []
        for i in range(start, count - 1, 2):
            found += [(i, i + 1), (i + 1, i)]
        return found

    return lax.ppermute(odd, axis, pairs(1)), lax.ppermute(even, axis, pairs(0))


def local(body_force, viscosity, topography, kappa):
    inputs = [
        pltpu.with_memory_space_constraint(x, pltpu.HBM) for x in (body_force, viscosity, topography, kappa)
    ]
    odd, even = pl.pallas_call(
        fetch,
        out_shape=[jax.ShapeDtypeStruct((4, 2, 8, 128), f32)] * 2,
        in_specs=[pl.BlockSpec(memory_space=pltpu.HBM)] * 2,
        out_specs=[vmem()] * 2,
        scratch_shapes=[pltpu.SemaphoreType.DMA((4,))],
        compiler_params=pltpu.CompilerParams(vmem_limit_bytes=1 << 20),
    )(*inputs[:2])
    odd, even = swap(odd, even, "gz")
    planes, left, right, height, conduct = pl.pallas_call(
        own_block,
        out_shape=[
            jax.ShapeDtypeStruct(shape, f32)
            for shape in ((4, 8, 8, 128), (2, 8, 128), (2, 8, 128), (64, 256), (64, 256))
        ],
        in_specs=[pl.BlockSpec(memory_space=pltpu.HBM)] * 4,
        out_specs=[vmem()] * 5,
        scratch_shapes=[pltpu.VMEM(x.shape, x.dtype) for x in inputs] + [pltpu.SemaphoreType.DMA((4,))],
        compiler_params=pltpu.CompilerParams(vmem_limit_bytes=8 << 20),
        cost_estimate=pl.CostEstimate(flops=20000 * 1024, bytes_accessed=1 << 18, transcendentals=0),
    )(*inputs)
    planes, odd, even = call(
        assemble,
        [(PLANES, 8, 128), (2, 8, 128), (2, 8, 128)],
        (planes, odd, even, left, right),
    )
    own = (odd, even)
    odd, even = swap(odd, even, "gy")
    low, high = call(edge_rows, [(COLUMN_ROW, 128)] * 2, (planes,))
    odd, even, columns, height, conduct = call(
        prepare_rows,
        [(GX_ROWS, 128), (GX_ROWS, 128), (3, 8, 128), (64, 256), (64, 256)],
        (low, high, *own, odd, even, height, conduct),
    )
    odd, even = swap(odd, even, "gx")
    (inner,) = call(inner_rows, [(48, 128)], (height, conduct))
    group = lax.axis_size("gx") * lax.axis_size("gy")
    image, sums, top, height = call(
        operate,
        [(3, 8, 8, 128), (group, 128), (2, 8, 128), (64, 128)],
        (planes, low, high, columns, odd, even, height, conduct, inner),
    )
    sums = lax.all_to_all(sums.reshape(group, 1, 128), ("gx", "gy"), 0, 0)
    (parts,) = call(middle, [(lax.axis_size("gz"), 4, 128)], (sums.reshape(group, 128), top))
    parts = lax.all_to_all(parts, "gz", 0, 0)
    shapes = ((3, 8, 8, 128), (64, 128))
    velocity, surface = pl.pallas_call(
        finish,
        out_shape=[jax.ShapeDtypeStruct(shape, f32) for shape in shapes],
        in_specs=[vmem()] * 4,
        out_specs=[pl.BlockSpec(memory_space=pltpu.HBM)] * 2,
        scratch_shapes=[pltpu.VMEM(shape, f32) for shape in shapes] + [pltpu.SemaphoreType.DMA((2,))],
        compiler_params=pltpu.CompilerParams(vmem_limit_bytes=8 << 20),
    )(parts, planes, image, height)
    return velocity, surface


def solution(mesh):
    in_specs = (P(None, "gz", "gx", "gy"), P("gz", "gx", "gy"), P("gx", "gy"), P("gx", "gy"))
    out_specs = (P(None, "gz", "gx", "gy"), P("gx", ("gy", "gz")))
    return jax.shard_map(local, mesh=mesh, in_specs=in_specs, out_specs=out_specs, check_vma=False)
```

```python
import jax
import jax.numpy as jnp
from jax import lax
from jax.experimental import pallas as pl
from jax.experimental.pallas import tpu as pltpu
from jax.sharding import PartitionSpec as P

STEPS = 8
DRAG = 1.0
TIME_STEP = 1.0
LOAD_GAIN = 4.0
FACE, EDGE, CORNER = 0.5, 0.25, 0.5 / 3.0
TOTAL = 6 * FACE + 12 * EDGE + 8 * CORNER

DEPTHS = 12
PLANES = 4 * DEPTHS
COLUMN_ROW = 8 * DEPTHS
SURFACE_ROW = COLUMN_ROW + 8
GX_ROWS = SURFACE_ROW + 32

f32 = jnp.float32


def vmem():
    return pl.BlockSpec(memory_space=pltpu.VMEM)


def call(body, outs, ins, scratch=(), cost=20000, limit=8 << 20):
    return pl.pallas_call(
        body,
        out_shape=[jax.ShapeDtypeStruct(s, f32) for s in outs],
        in_specs=[vmem() for _ in ins],
        out_specs=[vmem() for _ in outs],
        scratch_shapes=list(scratch),
        compiler_params=pltpu.CompilerParams(vmem_limit_bytes=limit),
        cost_estimate=pl.CostEstimate(flops=cost * 1024, bytes_accessed=1 << 18, transcendentals=0),
    )(*ins)


def lanes(shape):
    return lax.broadcasted_iota(jnp.int32, shape, len(shape) - 1)


def rolled(x, amount, axis=1):
    amount = amount % x.shape[axis]
    return x if amount == 0 else pltpu.roll(x, amount, axis)


def own_block(
    force_hbm, visc_hbm, topo_hbm, kappa_hbm, planes_ref, left_ref, right_ref, height_ref, conduct_ref,
    force_ref, visc_ref, topo_ref, kappa_ref, sems,
):
    moves = ((topo_hbm, topo_ref), (kappa_hbm, kappa_ref), (force_hbm, force_ref), (visc_hbm, visc_ref))
    copies = [pltpu.make_async_copy(source, target, sems.at[i]) for i, (source, target) in enumerate(moves)]
    for copy in copies:
        copy.start()
    for copy in copies:
        copy.wait()
    g = lax.axis_index("gz")
    last = lax.axis_size("gz") - 1
    lane = lanes((8, 128))
    pieces = []
    for v in range(8):
        piece = topo_ref[:, 128 * v : 128 * v + 128].reshape(8, 8, 128)
        pieces.append(jnp.sum(piece, axis=1))
    stacked = jnp.concatenate(pieces, axis=0)
    pick = (
        lax.broadcasted_iota(jnp.int32, (128, 128), 0) // 8 == lax.broadcasted_iota(jnp.int32, (128, 128), 1)
    ).astype(f32)
    sums = jnp.dot(stacked, pick, precision=lax.Precision.HIGHEST, preferred_element_type=f32)
    load = jnp.zeros((8, 128), f32)
    for v in range(8):
        load = load + rolled(sums[8 * v : 8 * v + 8], 16 * v)
    load = jnp.where(g == last, load * (-LOAD_GAIN / 64.0), 0.0)
    wide = lanes((64, 128))
    own = pl.ds(pl.multiple_of(g * 128, 128), 128)
    before = pl.ds(pl.multiple_of(jnp.maximum(g - 1, 0) * 128, 128), 128)
    after = pl.ds(pl.multiple_of(jnp.minimum(g + 1, last) * 128, 128), 128)
    for source, target in ((topo_ref, height_ref), (kappa_ref, conduct_ref)):
        target[:, 0:128] = source[:, own].astype(f32)
        side = jnp.where((wide < 8) & (g < last), source[:, after].astype(f32), 0.0)
        side = jnp.where((wide >= 120) & (g > 0), source[:, before].astype(f32), side)
        target[:, 128:256] = side
    width = topo_ref.shape[1]
    left = jnp.zeros((8, 128), f32)
    right = jnp.zeros((8, 128), f32)
    slot = 0
    for source in (topo_ref, kappa_ref):
        head = source[:, 0:128].astype(f32)
        tail = source[:, width - 128 : width].astype(f32)
        for r in range(8):
            mask = lane // 8 == slot
            left = jnp.where(mask, rolled(head[8 * r : 8 * r + 8], 8 * slot), left)
            right = jnp.where(mask, rolled(tail[8 * r : 8 * r + 8], 8 * slot - 120), right)
            slot += 1
    left_ref[1] = left
    right_ref[1] = right
    left = jnp.zeros((8, 128), f32)
    right = jnp.zeros((8, 128), f32)
    depths = visc_ref.shape[0]
    for field in range(4):
        for depth in range(depths):
            plane = visc_ref[depth] if field == 3 else force_ref[field, depth]
            if field == 2 and depth == depths - 1:
                plane = plane + load
            planes_ref[field, depth] = plane
            left, right = packed(plane, depth + 2, field, left, right, lane)
    left_ref[0] = left
    right_ref[0] = right


def is_even(axis):
    return lax.rem(lax.axis_index(axis), 2) == 0


def fetch(force_ref, visc_ref, even_ref, odd_ref, sems):
    depth = visc_ref.shape[0]
    start = jnp.where(is_even("gz"), 0, depth - 2)
    moves = []
    for target, first in ((odd_ref, start), (even_ref, depth - 2 - start)):
        moves.append((force_ref.at[:, pl.ds(first, 2)], target.at[0:3]))
        moves.append((visc_ref.at[pl.ds(first, 2)], target.at[3]))
    copies = [pltpu.make_async_copy(source, target, sems.at[i]) for i, (source, target) in enumerate(moves)]
    for copy in copies:
        copy.start()
    for copy in copies:
        copy.wait()


def packed(plane, depth, field, left, right, lane):
    first = 8 * depth + 2 * field
    mask = lane // 2 == first // 2
    left = jnp.where(mask, rolled(plane, first), left)
    return left, jnp.where(mask, rolled(plane, first - 126), right)


def assemble(own_ref, even_ref, odd_ref, left_ref, right_ref, planes_ref, odd_out, even_out):
    upward = is_even("gz")
    lane = lanes((8, 128))
    left, right = left_ref[0], right_ref[0]
    for field in range(4):
        for depth in range(DEPTHS):
            p = field * DEPTHS + depth
            if 2 <= depth < DEPTHS - 2:
                planes_ref[p] = own_ref[field, depth - 2]
                continue
            if depth < 2:
                plane = jnp.where(upward, odd_ref[field, depth], even_ref[field, depth])
            else:
                i = depth - (DEPTHS - 2)
                plane = jnp.where(upward, even_ref[field, i], odd_ref[field, i])
            planes_ref[p] = plane
            left, right = packed(plane, depth, field, left, right, lane)
    rightward = is_even("gy")
    odd_out[0] = jnp.where(rightward, left, right)
    even_out[0] = jnp.where(rightward, right, left)
    odd_out[1] = jnp.where(rightward, left_ref[1], right_ref[1])
    even_out[1] = jnp.where(rightward, right_ref[1], left_ref[1])


def edge_rows(planes_ref, low_ref, high_ref):
    for depth in range(DEPTHS):
        for field in range(4):
            plane = planes_ref.at[field * DEPTHS + depth]
            near = 8 * depth + field
            low_ref[near : near + 1, :] = plane[0:1, :]
            low_ref[near + 4 : near + 5, :] = plane[1:2, :]
            high_ref[near : near + 1, :] = plane[7:8, :]
            high_ref[near + 4 : near + 5, :] = plane[6:7, :]


def prepare_rows(
    low_ref, high_ref, own_odd, own_even, odd_ref, even_ref, height_ref, conduct_ref,
    odd_out, even_out, column_ref, height_out, conduct_out,
):
    g = lax.axis_index("gz")
    last = lax.axis_size("gz") - 1
    lane = lanes((8, 128))
    rightward = is_even("gy")

    def chosen(first, second, i):
        return jnp.where(rightward, first[i], second[i])

    before, after = chosen(odd_ref, even_ref, 0), chosen(even_ref, odd_ref, 0)
    before_surface, after_surface = chosen(odd_ref, even_ref, 1), chosen(even_ref, odd_ref, 1)
    side = lax.rem(lane, 2) == 0
    levels = (
        jnp.where(side, chosen(own_odd, own_even, 0), chosen(own_even, own_odd, 0)),
        jnp.where(side, rolled(before, -1), rolled(after, 1)),
        jnp.where(side, before, after),
    )
    downward = is_even("gx")

    def send(rows, low, high):
        odd_out[rows, :] = jnp.where(downward, low, high)
        even_out[rows, :] = jnp.where(downward, high, low)

    for depth in range(DEPTHS):
        rows = slice(8 * depth, 8 * depth + 8)
        send(rows, low_ref[rows, :], high_ref[rows, :])
    pad = [jnp.zeros((2, 128), f32)]
    send(
        slice(COLUMN_ROW, SURFACE_ROW),
        jnp.concatenate([x[0:2] for x in levels] + pad, axis=0),
        jnp.concatenate([x[6:8] for x in levels] + pad, axis=0),
    )
    for i in range(3):
        column_ref[i] = levels[i]
    slot = 0
    for index, (source, target) in enumerate(((height_ref, height_out), (conduct_ref, conduct_out))):
        base = SURFACE_ROW + 16 * index
        for r in range(8):
            rows = slice(8 * r, 8 * r + 8)
            main = source[rows, 0:128]
            side = source[rows, 128:256]
            side = jnp.where((g == 0) & (lane >= 120), rolled(before_surface, 120 - 8 * slot), side)
            side = jnp.where((g == last) & (lane < 8), rolled(after_surface, -8 * slot), side)
            target[rows, 0:128] = main
            target[rows, 128:256] = side
            if r == 0:
                first = (main, side)
            if r == 7:
                send(slice(base, base + 8), first[0], main)
                send(slice(base + 8, base + 16), first[1], side)
            slot += 1


def weighted(before, here, after):
    outer = before + after
    return outer, FACE * here + EDGE * outer, EDGE * here + CORNER * outer


def pair(x):
    return rolled(x, 1, 0) + rolled(x, x.shape[0] - 1, 0)


def lane_pair(x, lane, first, last):
    return jnp.where(lane == 0, first, rolled(x, 1)) + jnp.where(lane == 127, last, rolled(x, 127))


def row_pair(x, row, edge, field):
    up = jnp.where(row == 0, rolled(edge, -field, 0), rolled(x, 1, 0))
    return up + jnp.where(row == 7, rolled(edge, 3 - field, 0), rolled(x, 7, 0))


def to_first(x, depth, field):
    return rolled(x, -(8 * depth + 2 * field))


def to_last(x, depth, field):
    return rolled(x, 126 - (8 * depth + 2 * field))


def spread_rows(x, row):
    field = lax.rem(row, 4)
    for f in range(3):
        x = jnp.where(field == f, rolled(x, f - 3, 0), x)
    return x


def spread_columns(x, lane):
    field = lax.rem(lane, 8) // 2
    for f in range(3):
        x = jnp.where(field == f, rolled(x, 2 * (f - 3)), x)
    return x


def column_sums(levels):
    parts = [weighted(rolled(x, 8), x, rolled(x, 120)) for x in levels]
    (_, ai, bi), (outer, an, bn), (_, af, bf) = parts
    beside = an + pair(bn)
    return FACE * outer + pair(an) + (ai + af) + pair(bi + bf), beside


def beside_rows(beside, depth, row):
    near = jnp.where(row < 4, jnp.broadcast_to(beside[15:16], (8, 128)), jnp.broadcast_to(beside[8:9], (8, 128)))
    field = lax.rem(row, 4)
    first, last = to_first(near, depth, 0), to_last(near, depth, 0)
    for f in range(1, 4):
        first = jnp.where(field == f, to_first(near, depth, f), first)
        last = jnp.where(field == f, to_last(near, depth, f), last)
    return first, last


def sided(odd_ref, even_ref, axis):
    first = is_even(axis)

    def before(rows):
        return jnp.where(first, odd_ref[rows, :], even_ref[rows, :])

    def after(rows):
        return jnp.where(first, even_ref[rows, :], odd_ref[rows, :])

    return before, after


def flux(conduct, slope):
    return conduct * slope * lax.rsqrt(1.0 + slope * slope)


def steps(h, k):
    rows = h.shape[0]
    inside = k > 0.0
    along = 0.5 * (k + rolled(k, 255, 1))
    along_before = rolled(along, 1, 1)
    across = 0.5 * (k + rolled(k, rows - 1, 0))
    for step in range(STEPS):
        q = flux(along, rolled(h, 255, 1) - h) - flux(along_before, h - rolled(h, 1, 1))
        r = flux(across, rolled(h, rows - 1, 0) - h)
        h = jnp.where(inside, h + TIME_STEP * (q + (r - rolled(r, 1, 0))), 0.0)
    return h


def inner_rows(height_ref, conduct_ref, out_ref):
    out_ref[...] = steps(height_ref[...], conduct_ref[...])[8:56, 0:128]


def operate(
    planes_ref, low_ref, high_ref, column_ref, odd_ref, even_ref, height_ref, conduct_ref, inner_ref,
    image_ref, sums_ref, top_ref, out_ref,
):
    lane = lanes((8, 128))
    row = lax.broadcasted_iota(jnp.int32, (8, 128), 0)
    wide = lanes((16, 128))
    before, after = sided(odd_ref, even_ref, "gx")

    def banded(source, base):
        def joined(side):
            return jnp.concatenate([side(slice(base, base + 8)), side(slice(base + 8, base + 16))], axis=1)

        return jnp.concatenate([source[48:64, :], joined(after), joined(before), source[0:16, :]], axis=0)

    band = steps(banded(height_ref, SURFACE_ROW), banded(conduct_ref, SURFACE_ROW + 16))
    out_ref[0:8, :] = band[32:40, 0:128]
    out_ref[8:56, :] = inner_ref[...]
    out_ref[56:64, :] = band[8:16, 0:128]
    columns = []
    for i in range(3):
        rows = slice(COLUMN_ROW + 2 * i, COLUMN_ROW + 2 * i + 2)
        columns.append(jnp.concatenate([column_ref[i], after(rows), jnp.zeros((4, 128), f32), before(rows)], axis=0))
    column_eta = [spread_columns(x, wide) for x in columns]
    column_sum, beside = column_sums(columns)
    column_sum_eta, beside_eta = column_sums([x * y for x, y in zip(columns, column_eta)])
    near_eta = column_eta[1]
    column_diag = DRAG + TOTAL * near_eta + spread_columns(column_sum, wide)
    column_image = columns[1] * column_diag - near_eta * column_sum - column_sum_eta
    column_image = jnp.where(near_eta > 0.0, column_image, 0.0)
    rows_of, rows_eta = [], []
    for depth in range(DEPTHS):
        rows = slice(8 * depth, 8 * depth + 8)
        b, a = before(rows), after(rows)
        found = (
            jnp.where(row < 4, low_ref[rows, :], rolled(high_ref[rows, :], 4, 0)),
            jnp.where(row < 4, b, rolled(a, 4, 0)),
            jnp.where(row < 4, rolled(b, 4, 0), a),
        )
        rows_of.append(found)
        rows_eta.append([spread_rows(x, row) for x in found])
    rows_product = [[x * y for x, y in zip(found, etas)] for found, etas in zip(rows_of, rows_eta)]

    def row_sums(levels, depth, beside_columns):
        parts = [weighted(levels[depth - 1][i], levels[depth][i], levels[depth + 1][i]) for i in range(3)]
        (_, ai, bi), (outer, an, bn), (_, af, bf) = parts
        first, last = beside_rows(beside_columns, depth, row)
        return FACE * outer + (ai + af) + lane_pair(an + (bi + bf), lane, first, last), an, bn

    def plane_sum(three, an, bn, beside_columns, depth, field):
        outer, a, b = weighted(*three)
        both = a + row_pair(b, row, bn, field)
        own = beside_columns[0:8]
        sides = lane_pair(both, lane, to_first(own, depth, field), to_last(own, depth, field))
        return FACE * outer + row_pair(a, row, an, field) + sides

    def plane(field, depth):
        return planes_ref[field * DEPTHS + depth]

    image, row_image, diagonal = {}, {}, {}
    for depth in range(1, DEPTHS - 1):
        row_sum, an, bn = row_sums(rows_of, depth, beside)
        row_sum_eta, an_eta, bn_eta = row_sums(rows_product, depth, beside_eta)
        near, eta = rows_of[depth][1], rows_eta[depth][1]
        diag = DRAG + TOTAL * eta + spread_rows(row_sum, row)
        row_image[depth] = jnp.where(eta > 0.0, near * diag - eta * row_sum - row_sum_eta, 0.0)
        e = [plane(3, depth + i) for i in (-1, 0, 1)]
        diag = DRAG + TOTAL * e[1] + plane_sum(e, an, bn, beside, depth, 3)
        diagonal[depth] = diag
        for c in range(3):
            v = [plane(c, depth + i) for i in (-1, 0, 1)]
            ev = [x * y for x, y in zip(e, v)]
            out = v[1] * diag - e[1] * plane_sum(v, an, bn, beside, depth, c)
            out = out - plane_sum(ev, an_eta, bn_eta, beside_eta, depth, c)
            image[c, depth] = jnp.where(e[1] > 0.0, out, 0.0)
    _, an, bn = weighted(rolled(column_image, 8), column_image, rolled(column_image, 120))
    beside = an + pair(bn)
    m = [jnp.zeros((8, 128), f32) for _ in range(4)]
    for depth in range(2, DEPTHS - 2):
        _, an, bn = weighted(row_image[depth - 1], row_image[depth], row_image[depth + 1])
        e = plane(3, depth)
        for c in range(3):
            s = plane_sum([image[c, depth + i] for i in (-1, 0, 1)], an, bn, beside, depth, c)
            v, q = plane(c, depth), image[c, depth]
            image_ref[c, depth - 2] = q
            m[0] = m[0] + v * v
            m[1] = m[1] + v * q
            m[2] = m[2] + q * q
            m[3] = m[3] + q * (q * diagonal[depth] - 2.0 * (e * s))
    total = jnp.zeros((8, 128), f32)
    for k in range(4):
        part = m[k]
        for amount in (64, 32, 16):
            part = part + rolled(part, amount)
        total = jnp.where(lane // 16 == 2 + k, part, total)
    for amount in (4, 2, 1):
        total = total + rolled(total, amount, 0)
    for i in range(sums_ref.shape[0] // 8):
        sums_ref[8 * i : 8 * i + 8, :] = total
    top_ref[0] = plane(2, DEPTHS - 3)
    top_ref[1] = image[2, DEPTHS - 3]


def middle(sums_ref, top_ref, out_ref):
    lane = lanes((8, 128))
    row = lax.broadcasted_iota(jnp.int32, (8, 128), 0)
    part = jnp.sum(sums_ref[...], axis=0, keepdims=True)
    flat = []
    for i in range(2):
        found = top_ref[i]
        for k in range(1, 8):
            found = jnp.where(
                lane // 16 == lax.rem(row + k, 8), rolled(rolled(top_ref[i], -k, 0), 16 * k), found
            )
        flat.append(found)
    for j in range(out_ref.shape[0]):
        out_ref[j, 0:1, :] = flat[0][j : j + 1]
        out_ref[j, 1:2, :] = flat[1][j : j + 1]
        out_ref[j, 2:3, :] = part
        out_ref[j, 3:4, :] = part


def finish(parts_ref, planes_ref, image_ref, height_ref, velocity_hbm, surface_hbm, velocity_ref, surface_ref, sems):
    count = parts_ref.shape[0]
    lane = lanes((1, 128))
    row = lax.broadcasted_iota(jnp.int32, (8, 128), 0)
    found = []
    for i in range(2):
        flat = jnp.broadcast_to(parts_ref[count - 1, i : i + 1, :], (8, 128))
        cells = flat
        for r in range(1, 8):
            cells = jnp.where(row == r, rolled(flat, -16 * r), cells)
        found.append(cells)
    top = jnp.where(lanes((16, 128)) < 16, jnp.concatenate(found, axis=0), 0.0)
    spread = (
        lax.broadcasted_iota(jnp.int32, (128, 128), 1) // 8 == lax.broadcasted_iota(jnp.int32, (128, 128), 0)
    ).astype(f32)
    wide = jnp.dot(top, spread, precision=lax.Precision.HIGHEST, preferred_element_type=f32)
    total = parts_ref[0, 2:3, :]
    for j in range(1, count):
        total = total + parts_ref[j, 2:3, :]

    def moment(k):
        return jnp.sum(jnp.where(lane // 16 == 2 + k, total, 0.0), axis=1, keepdims=True)

    m0, m1, m2, m3 = (moment(k) for k in range(4))
    first = m0 / m1
    later = first * first * m2 - m0
    gain = 1.0 + later / m0
    second = later / (gain * gain * m1 - 2.0 * first * gain * m2 + first * first * m3)
    on_force = first + second * gain
    on_image = -(second * first)
    for c in range(3):
        for depth in range(8):
            velocity_ref[c, depth] = on_force * planes_ref[c * DEPTHS + depth + 2] + on_image * image_ref[c, depth]
    velocity_copy = pltpu.make_async_copy(velocity_ref, velocity_hbm, sems.at[0])
    velocity_copy.start()
    rise = (STEPS * TIME_STEP) * (on_force * wide[0:8] + on_image * wide[8:16])
    for r in range(8):
        rows = slice(8 * r, 8 * r + 8)
        surface_ref[rows, :] = height_ref[rows, :] + jnp.broadcast_to(rise[r : r + 1, :], (8, 128))
    surface_copy = pltpu.make_async_copy(surface_ref, surface_hbm, sems.at[1])
    surface_copy.start()
    velocity_copy.wait()
    surface_copy.wait()


def swap(odd, even, axis, even_first=False):
    count = lax.axis_size(axis)

    def pairs(start):
        found = []
        for i in range(start, count - 1, 2):
            found += [(i, i + 1), (i + 1, i)]
        return found

    if even_first:
        even = lax.ppermute(even, axis, pairs(0))
        return lax.ppermute(odd, axis, pairs(1)), even
    return lax.ppermute(odd, axis, pairs(1)), lax.ppermute(even, axis, pairs(0))


def local(body_force, viscosity, topography, kappa):
    inputs = [
        pltpu.with_memory_space_constraint(x, pltpu.HBM) for x in (body_force, viscosity, topography, kappa)
    ]
    even, odd = pl.pallas_call(
        fetch,
        out_shape=[jax.ShapeDtypeStruct((4, 2, 8, 128), f32)] * 2,
        in_specs=[pl.BlockSpec(memory_space=pltpu.HBM)] * 2,
        out_specs=[vmem()] * 2,
        scratch_shapes=[pltpu.SemaphoreType.DMA((4,))],
        compiler_params=pltpu.CompilerParams(vmem_limit_bytes=1 << 20),
    )(*inputs[:2])
    odd, even = swap(odd, even, "gz", even_first=True)
    planes, left, right, height, conduct = pl.pallas_call(
        own_block,
        out_shape=[
            jax.ShapeDtypeStruct(shape, f32)
            for shape in ((4, 8, 8, 128), (2, 8, 128), (2, 8, 128), (64, 256), (64, 256))
        ],
        in_specs=[pl.BlockSpec(memory_space=pltpu.HBM)] * 4,
        out_specs=[vmem()] * 5,
        scratch_shapes=[pltpu.VMEM(x.shape, x.dtype) for x in inputs] + [pltpu.SemaphoreType.DMA((4,))],
        compiler_params=pltpu.CompilerParams(vmem_limit_bytes=8 << 20),
        cost_estimate=pl.CostEstimate(flops=20000 * 1024, bytes_accessed=1 << 18, transcendentals=0),
    )(*inputs)
    planes, odd, even = call(
        assemble,
        [(PLANES, 8, 128), (2, 8, 128), (2, 8, 128)],
        (planes, even, odd, left, right),
    )
    own = (odd, even)
    odd, even = swap(odd, even, "gy")
    low, high = call(edge_rows, [(COLUMN_ROW, 128)] * 2, (planes,))
    odd, even, columns, height, conduct = call(
        prepare_rows,
        [(GX_ROWS, 128), (GX_ROWS, 128), (3, 8, 128), (64, 256), (64, 256)],
        (low, high, *own, odd, even, height, conduct),
    )
    odd, even = swap(odd, even, "gx")
    (inner,) = call(inner_rows, [(48, 128)], (height, conduct))
    group = lax.axis_size("gx") * lax.axis_size("gy")
    image, sums, top, height = call(
        operate,
        [(3, 8, 8, 128), (group, 128), (2, 8, 128), (64, 128)],
        (planes, low, high, columns, odd, even, height, conduct, inner),
    )
    sums = lax.all_to_all(sums.reshape(group, 1, 128), ("gx", "gy"), 0, 0)
    (parts,) = call(middle, [(lax.axis_size("gz"), 4, 128)], (sums.reshape(group, 128), top))
    parts = lax.all_to_all(parts, "gz", 0, 0)
    shapes = ((3, 8, 8, 128), (64, 128))
    velocity, surface = pl.pallas_call(
        finish,
        out_shape=[jax.ShapeDtypeStruct(shape, f32) for shape in shapes],
        in_specs=[vmem()] * 4,
        out_specs=[pl.BlockSpec(memory_space=pltpu.HBM)] * 2,
        scratch_shapes=[pltpu.VMEM(shape, f32) for shape in shapes] + [pltpu.SemaphoreType.DMA((2,))],
        compiler_params=pltpu.CompilerParams(vmem_limit_bytes=8 << 20),
    )(parts, planes, image, height)
    return velocity, surface


def solution(mesh):
    in_specs = (P(None, "gz", "gx", "gy"), P("gz", "gx", "gy"), P("gx", "gy"), P("gx", "gy"))
    out_specs = (P(None, "gz", "gx", "gy"), P("gx", ("gy", "gz")))
    return jax.shard_map(local, mesh=mesh, in_specs=in_specs, out_specs=out_specs, check_vma=False)
```

```python
import jax
import jax.numpy as jnp
from jax import lax
from jax.experimental import pallas as pl
from jax.experimental.pallas import tpu as pltpu
from jax.sharding import PartitionSpec as P

STEPS = 8
DRAG = 1.0
TIME_STEP = 1.0
LOAD_GAIN = 4.0
FACE, EDGE, CORNER = 0.5, 0.25, 0.5 / 3.0
TOTAL = 6 * FACE + 12 * EDGE + 8 * CORNER

DEPTHS = 12
PLANES = 4 * DEPTHS
COLUMN_ROW = 8 * DEPTHS
SURFACE_ROW = COLUMN_ROW + 8
GX_ROWS = SURFACE_ROW + 32

f32 = jnp.float32


def vmem():
    return pl.BlockSpec(memory_space=pltpu.VMEM)


def call(body, outs, ins, scratch=(), cost=20000, limit=8 << 20):
    return pl.pallas_call(
        body,
        out_shape=[jax.ShapeDtypeStruct(s, f32) for s in outs],
        in_specs=[vmem() for _ in ins],
        out_specs=[vmem() for _ in outs],
        scratch_shapes=list(scratch),
        compiler_params=pltpu.CompilerParams(vmem_limit_bytes=limit),
        cost_estimate=pl.CostEstimate(flops=cost * 1024, bytes_accessed=1 << 18, transcendentals=0),
    )(*ins)


def lanes(shape):
    return lax.broadcasted_iota(jnp.int32, shape, len(shape) - 1)


def rolled(x, amount, axis=1):
    amount = amount % x.shape[axis]
    return x if amount == 0 else pltpu.roll(x, amount, axis)


def own_block(
    force_hbm, visc_hbm, topo_hbm, kappa_hbm, planes_ref, left_ref, right_ref, height_ref, conduct_ref,
    force_ref, visc_ref, topo_ref, kappa_ref, sems,
):
    moves = ((topo_hbm, topo_ref), (kappa_hbm, kappa_ref), (force_hbm, force_ref), (visc_hbm, visc_ref))
    copies = [pltpu.make_async_copy(source, target, sems.at[i]) for i, (source, target) in enumerate(moves)]
    for copy in copies:
        copy.start()
    for copy in copies:
        copy.wait()
    g = lax.axis_index("gz")
    last = lax.axis_size("gz") - 1
    lane = lanes((8, 128))
    pieces = []
    for v in range(8):
        piece = topo_ref[:, 128 * v : 128 * v + 128].reshape(8, 8, 128)
        pieces.append(jnp.sum(piece, axis=1))
    stacked = jnp.concatenate(pieces, axis=0)
    pick = (
        lax.broadcasted_iota(jnp.int32, (128, 128), 0) // 8 == lax.broadcasted_iota(jnp.int32, (128, 128), 1)
    ).astype(f32)
    sums = jnp.dot(stacked, pick, precision=lax.Precision.HIGHEST, preferred_element_type=f32)
    load = jnp.zeros((8, 128), f32)
    for v in range(8):
        load = load + rolled(sums[8 * v : 8 * v + 8], 16 * v)
    load = jnp.where(g == last, load * (-LOAD_GAIN / 64.0), 0.0)
    wide = lanes((64, 128))
    own = pl.ds(pl.multiple_of(g * 128, 128), 128)
    before = pl.ds(pl.multiple_of(jnp.maximum(g - 1, 0) * 128, 128), 128)
    after = pl.ds(pl.multiple_of(jnp.minimum(g + 1, last) * 128, 128), 128)
    for source, target in ((topo_ref, height_ref), (kappa_ref, conduct_ref)):
        target[:, 0:128] = source[:, own].astype(f32)
        side = jnp.where((wide < 8) & (g < last), source[:, after].astype(f32), 0.0)
        side = jnp.where((wide >= 120) & (g > 0), source[:, before].astype(f32), side)
        target[:, 128:256] = side
    width = topo_ref.shape[1]
    left = jnp.zeros((8, 128), f32)
    right = jnp.zeros((8, 128), f32)
    slot = 0
    for source in (topo_ref, kappa_ref):
        head = source[:, 0:128].astype(f32)
        tail = source[:, width - 128 : width].astype(f32)
        for r in range(8):
            mask = lane // 8 == slot
            left = jnp.where(mask, rolled(head[8 * r : 8 * r + 8], 8 * slot), left)
            right = jnp.where(mask, rolled(tail[8 * r : 8 * r + 8], 8 * slot - 120), right)
            slot += 1
    left_ref[1] = left
    right_ref[1] = right
    left = jnp.zeros((8, 128), f32)
    right = jnp.zeros((8, 128), f32)
    depths = visc_ref.shape[0]
    for field in range(4):
        for depth in range(depths):
            plane = visc_ref[depth] if field == 3 else force_ref[field, depth]
            if field == 2 and depth == depths - 1:
                plane = plane + load
            planes_ref[field, depth] = plane
            left, right = packed(plane, depth + 2, field, left, right, lane)
    left_ref[0] = left
    right_ref[0] = right


def is_even(axis):
    return lax.rem(lax.axis_index(axis), 2) == 0


def fetch(force_ref, visc_ref, odd_ref, even_ref, sems):
    depth = visc_ref.shape[0]
    start = jnp.where(is_even("gz"), 0, depth - 2)
    moves = []
    for target, first in ((odd_ref, start), (even_ref, depth - 2 - start)):
        moves.append((force_ref.at[:, pl.ds(first, 2)], target.at[0:3]))
        moves.append((visc_ref.at[pl.ds(first, 2)], target.at[3]))
    copies = [pltpu.make_async_copy(source, target, sems.at[i]) for i, (source, target) in enumerate(moves)]
    for copy in copies:
        copy.start()
    for copy in copies:
        copy.wait()


def packed(plane, depth, field, left, right, lane):
    first = 8 * depth + 2 * field
    mask = lane // 2 == first // 2
    left = jnp.where(mask, rolled(plane, first), left)
    return left, jnp.where(mask, rolled(plane, first - 126), right)


def assemble(own_ref, odd_ref, even_ref, left_ref, right_ref, planes_ref, even_out, odd_out):
    upward = is_even("gz")
    lane = lanes((8, 128))
    left, right = left_ref[0], right_ref[0]
    for field in range(4):
        for depth in range(DEPTHS):
            p = field * DEPTHS + depth
            if 2 <= depth < DEPTHS - 2:
                planes_ref[p] = own_ref[field, depth - 2]
                continue
            if depth < 2:
                plane = jnp.where(upward, odd_ref[field, depth], even_ref[field, depth])
            else:
                i = depth - (DEPTHS - 2)
                plane = jnp.where(upward, even_ref[field, i], odd_ref[field, i])
            planes_ref[p] = plane
            left, right = packed(plane, depth, field, left, right, lane)
    rightward = is_even("gy")
    odd_out[0] = jnp.where(rightward, left, right)
    even_out[0] = jnp.where(rightward, right, left)
    odd_out[1] = jnp.where(rightward, left_ref[1], right_ref[1])
    even_out[1] = jnp.where(rightward, right_ref[1], left_ref[1])


def edge_rows(planes_ref, low_ref, high_ref):
    for depth in range(DEPTHS):
        for field in range(4):
            plane = planes_ref.at[field * DEPTHS + depth]
            near = 8 * depth + field
            low_ref[near : near + 1, :] = plane[0:1, :]
            low_ref[near + 4 : near + 5, :] = plane[1:2, :]
            high_ref[near : near + 1, :] = plane[7:8, :]
            high_ref[near + 4 : near + 5, :] = plane[6:7, :]


def prepare_rows(
    low_ref, high_ref, own_odd, own_even, even_ref, odd_ref, height_ref, conduct_ref,
    odd_out, even_out, column_ref, height_out, conduct_out,
):
    g = lax.axis_index("gz")
    last = lax.axis_size("gz") - 1
    lane = lanes((8, 128))
    rightward = is_even("gy")

    def chosen(first, second, i):
        return jnp.where(rightward, first[i], second[i])

    before, after = chosen(odd_ref, even_ref, 0), chosen(even_ref, odd_ref, 0)
    before_surface, after_surface = chosen(odd_ref, even_ref, 1), chosen(even_ref, odd_ref, 1)
    side = lax.rem(lane, 2) == 0
    levels = (
        jnp.where(side, chosen(own_odd, own_even, 0), chosen(own_even, own_odd, 0)),
        jnp.where(side, rolled(before, -1), rolled(after, 1)),
        jnp.where(side, before, after),
    )
    downward = is_even("gx")

    def send(rows, low, high):
        odd_out[rows, :] = jnp.where(downward, low, high)
        even_out[rows, :] = jnp.where(downward, high, low)

    for depth in range(DEPTHS):
        rows = slice(8 * depth, 8 * depth + 8)
        send(rows, low_ref[rows, :], high_ref[rows, :])
    pad = [jnp.zeros((2, 128), f32)]
    send(
        slice(COLUMN_ROW, SURFACE_ROW),
        jnp.concatenate([x[0:2] for x in levels] + pad, axis=0),
        jnp.concatenate([x[6:8] for x in levels] + pad, axis=0),
    )
    for i in range(3):
        column_ref[i] = levels[i]
    slot = 0
    for index, (source, target) in enumerate(((height_ref, height_out), (conduct_ref, conduct_out))):
        base = SURFACE_ROW + 16 * index
        for r in range(8):
            rows = slice(8 * r, 8 * r + 8)
            main = source[rows, 0:128]
            side = source[rows, 128:256]
            side = jnp.where((g == 0) & (lane >= 120), rolled(before_surface, 120 - 8 * slot), side)
            side = jnp.where((g == last) & (lane < 8), rolled(after_surface, -8 * slot), side)
            target[rows, 0:128] = main
            target[rows, 128:256] = side
            if r == 0:
                first = (main, side)
            if r == 7:
                send(slice(base, base + 8), first[0], main)
                send(slice(base + 8, base + 16), first[1], side)
            slot += 1


def weighted(before, here, after):
    outer = before + after
    return outer, FACE * here + EDGE * outer, EDGE * here + CORNER * outer


def pair(x):
    return rolled(x, 1, 0) + rolled(x, x.shape[0] - 1, 0)


def lane_pair(x, lane, first, last):
    return jnp.where(lane == 0, first, rolled(x, 1)) + jnp.where(lane == 127, last, rolled(x, 127))


def row_pair(x, row, edge, field):
    up = jnp.where(row == 0, rolled(edge, -field, 0), rolled(x, 1, 0))
    return up + jnp.where(row == 7, rolled(edge, 3 - field, 0), rolled(x, 7, 0))


def to_first(x, depth, field):
    return rolled(x, -(8 * depth + 2 * field))


def to_last(x, depth, field):
    return rolled(x, 126 - (8 * depth + 2 * field))


def spread_rows(x, row):
    field = lax.rem(row, 4)
    for f in range(3):
        x = jnp.where(field == f, rolled(x, f - 3, 0), x)
    return x


def spread_columns(x, lane):
    field = lax.rem(lane, 8) // 2
    for f in range(3):
        x = jnp.where(field == f, rolled(x, 2 * (f - 3)), x)
    return x


def column_sums(levels):
    parts = [weighted(rolled(x, 8), x, rolled(x, 120)) for x in levels]
    (_, ai, bi), (outer, an, bn), (_, af, bf) = parts
    beside = an + pair(bn)
    return FACE * outer + pair(an) + (ai + af) + pair(bi + bf), beside


def beside_rows(beside, depth, row):
    near = jnp.where(row < 4, jnp.broadcast_to(beside[15:16], (8, 128)), jnp.broadcast_to(beside[8:9], (8, 128)))
    field = lax.rem(row, 4)
    first, last = to_first(near, depth, 0), to_last(near, depth, 0)
    for f in range(1, 4):
        first = jnp.where(field == f, to_first(near, depth, f), first)
        last = jnp.where(field == f, to_last(near, depth, f), last)
    return first, last


def sided(odd_ref, even_ref, axis):
    first = is_even(axis)

    def before(rows):
        return jnp.where(first, odd_ref[rows, :], even_ref[rows, :])

    def after(rows):
        return jnp.where(first, even_ref[rows, :], odd_ref[rows, :])

    return before, after


def flux(conduct, slope):
    return conduct * slope * lax.rsqrt(1.0 + slope * slope)


def steps(h, k):
    rows = h.shape[0]
    inside = k > 0.0
    along = 0.5 * (k + rolled(k, 255, 1))
    along_before = rolled(along, 1, 1)
    across = 0.5 * (k + rolled(k, rows - 1, 0))
    for step in range(STEPS):
        q = flux(along, rolled(h, 255, 1) - h) - flux(along_before, h - rolled(h, 1, 1))
        r = flux(across, rolled(h, rows - 1, 0) - h)
        h = jnp.where(inside, h + TIME_STEP * (q + (r - rolled(r, 1, 0))), 0.0)
    return h


def inner_rows(height_ref, conduct_ref, out_ref):
    out_ref[...] = steps(height_ref[...], conduct_ref[...])[8:56, 0:128]


def operate(
    planes_ref, low_ref, high_ref, column_ref, odd_ref, even_ref, height_ref, conduct_ref, inner_ref,
    image_ref, sums_ref, top_ref, out_ref,
):
    lane = lanes((8, 128))
    row = lax.broadcasted_iota(jnp.int32, (8, 128), 0)
    wide = lanes((16, 128))
    before, after = sided(odd_ref, even_ref, "gx")

    def banded(source, base):
        def joined(side):
            return jnp.concatenate([side(slice(base, base + 8)), side(slice(base + 8, base + 16))], axis=1)

        return jnp.concatenate([source[48:64, :], joined(after), joined(before), source[0:16, :]], axis=0)

    band = steps(banded(height_ref, SURFACE_ROW), banded(conduct_ref, SURFACE_ROW + 16))
    out_ref[0:8, :] = band[32:40, 0:128]
    out_ref[8:56, :] = inner_ref[...]
    out_ref[56:64, :] = band[8:16, 0:128]
    columns = []
    for i in range(3):
        rows = slice(COLUMN_ROW + 2 * i, COLUMN_ROW + 2 * i + 2)
        columns.append(jnp.concatenate([column_ref[i], after(rows), jnp.zeros((4, 128), f32), before(rows)], axis=0))
    column_eta = [spread_columns(x, wide) for x in columns]
    column_sum, beside = column_sums(columns)
    column_sum_eta, beside_eta = column_sums([x * y for x, y in zip(columns, column_eta)])
    near_eta = column_eta[1]
    column_diag = DRAG + TOTAL * near_eta + spread_columns(column_sum, wide)
    column_image = columns[1] * column_diag - near_eta * column_sum - column_sum_eta
    column_image = jnp.where(near_eta > 0.0, column_image, 0.0)
    rows_of, rows_eta = [], []
    for depth in range(DEPTHS):
        rows = slice(8 * depth, 8 * depth + 8)
        b, a = before(rows), after(rows)
        found = (
            jnp.where(row < 4, low_ref[rows, :], rolled(high_ref[rows, :], 4, 0)),
            jnp.where(row < 4, b, rolled(a, 4, 0)),
            jnp.where(row < 4, rolled(b, 4, 0), a),
        )
        rows_of.append(found)
        rows_eta.append([spread_rows(x, row) for x in found])
    rows_product = [[x * y for x, y in zip(found, etas)] for found, etas in zip(rows_of, rows_eta)]

    def row_sums(levels, depth, beside_columns):
        parts = [weighted(levels[depth - 1][i], levels[depth][i], levels[depth + 1][i]) for i in range(3)]
        (_, ai, bi), (outer, an, bn), (_, af, bf) = parts
        first, last = beside_rows(beside_columns, depth, row)
        return FACE * outer + (ai + af) + lane_pair(an + (bi + bf), lane, first, last), an, bn

    def plane_sum(three, an, bn, beside_columns, depth, field):
        outer, a, b = weighted(*three)
        both = a + row_pair(b, row, bn, field)
        own = beside_columns[0:8]
        sides = lane_pair(both, lane, to_first(own, depth, field), to_last(own, depth, field))
        return FACE * outer + row_pair(a, row, an, field) + sides

    def plane(field, depth):
        return planes_ref[field * DEPTHS + depth]

    image, row_image, diagonal = {}, {}, {}
    for depth in range(1, DEPTHS - 1):
        row_sum, an, bn = row_sums(rows_of, depth, beside)
        row_sum_eta, an_eta, bn_eta = row_sums(rows_product, depth, beside_eta)
        near, eta = rows_of[depth][1], rows_eta[depth][1]
        diag = DRAG + TOTAL * eta + spread_rows(row_sum, row)
        row_image[depth] = jnp.where(eta > 0.0, near * diag - eta * row_sum - row_sum_eta, 0.0)
        e = [plane(3, depth + i) for i in (-1, 0, 1)]
        diag = DRAG + TOTAL * e[1] + plane_sum(e, an, bn, beside, depth, 3)
        diagonal[depth] = diag
        for c in range(3):
            v = [plane(c, depth + i) for i in (-1, 0, 1)]
            ev = [x * y for x, y in zip(e, v)]
            out = v[1] * diag - e[1] * plane_sum(v, an, bn, beside, depth, c)
            out = out - plane_sum(ev, an_eta, bn_eta, beside_eta, depth, c)
            image[c, depth] = jnp.where(e[1] > 0.0, out, 0.0)
    _, an, bn = weighted(rolled(column_image, 8), column_image, rolled(column_image, 120))
    beside = an + pair(bn)
    m = [jnp.zeros((8, 128), f32) for _ in range(4)]
    for depth in range(2, DEPTHS - 2):
        _, an, bn = weighted(row_image[depth - 1], row_image[depth], row_image[depth + 1])
        e = plane(3, depth)
        for c in range(3):
            s = plane_sum([image[c, depth + i] for i in (-1, 0, 1)], an, bn, beside, depth, c)
            v, q = plane(c, depth), image[c, depth]
            image_ref[c, depth - 2] = q
            m[0] = m[0] + v * v
            m[1] = m[1] + v * q
            m[2] = m[2] + q * q
            m[3] = m[3] + q * (q * diagonal[depth] - 2.0 * (e * s))
    total = jnp.zeros((8, 128), f32)
    for k in range(4):
        part = m[k]
        for amount in (64, 32, 16):
            part = part + rolled(part, amount)
        total = jnp.where(lane // 16 == 2 + k, part, total)
    for amount in (4, 2, 1):
        total = total + rolled(total, amount, 0)
    for i in range(sums_ref.shape[0] // 8):
        sums_ref[8 * i : 8 * i + 8, :] = total
    top_ref[0] = plane(2, DEPTHS - 3)
    top_ref[1] = image[2, DEPTHS - 3]


def middle(sums_ref, top_ref, out_ref):
    lane = lanes((8, 128))
    row = lax.broadcasted_iota(jnp.int32, (8, 128), 0)
    part = jnp.sum(sums_ref[...], axis=0, keepdims=True)
    flat = []
    for i in range(2):
        found = top_ref[i]
        for k in range(1, 8):
            found = jnp.where(
                lane // 16 == lax.rem(row + k, 8), rolled(rolled(top_ref[i], -k, 0), 16 * k), found
            )
        flat.append(found)
    for j in range(out_ref.shape[0]):
        out_ref[j, 0:1, :] = flat[0][j : j + 1]
        out_ref[j, 1:2, :] = flat[1][j : j + 1]
        out_ref[j, 2:3, :] = part
        out_ref[j, 3:4, :] = part


def finish(parts_ref, planes_ref, image_ref, height_ref, velocity_hbm, surface_hbm, velocity_ref, surface_ref, sems):
    count = parts_ref.shape[0]
    lane = lanes((1, 128))
    row = lax.broadcasted_iota(jnp.int32, (8, 128), 0)
    found = []
    for i in range(2):
        flat = jnp.broadcast_to(parts_ref[count - 1, i : i + 1, :], (8, 128))
        cells = flat
        for r in range(1, 8):
            cells = jnp.where(row == r, rolled(flat, -16 * r), cells)
        found.append(cells)
    top = jnp.where(lanes((16, 128)) < 16, jnp.concatenate(found, axis=0), 0.0)
    spread = (
        lax.broadcasted_iota(jnp.int32, (128, 128), 1) // 8 == lax.broadcasted_iota(jnp.int32, (128, 128), 0)
    ).astype(f32)
    wide = jnp.dot(top, spread, precision=lax.Precision.HIGHEST, preferred_element_type=f32)
    total = parts_ref[0, 2:3, :]
    for j in range(1, count):
        total = total + parts_ref[j, 2:3, :]

    def moment(k):
        return jnp.sum(jnp.where(lane // 16 == 2 + k, total, 0.0), axis=1, keepdims=True)

    m0, m1, m2, m3 = (moment(k) for k in range(4))
    first = m0 / m1
    later = first * first * m2 - m0
    gain = 1.0 + later / m0
    second = later / (gain * gain * m1 - 2.0 * first * gain * m2 + first * first * m3)
    on_force = first + second * gain
    on_image = -(second * first)
    for c in range(3):
        for depth in range(8):
            velocity_ref[c, depth] = on_force * planes_ref[c * DEPTHS + depth + 2] + on_image * image_ref[c, depth]
    velocity_copy = pltpu.make_async_copy(velocity_ref, velocity_hbm, sems.at[0])
    velocity_copy.start()
    rise = (STEPS * TIME_STEP) * (on_force * wide[0:8] + on_image * wide[8:16])
    for r in range(8):
        rows = slice(8 * r, 8 * r + 8)
        surface_ref[rows, :] = height_ref[rows, :] + jnp.broadcast_to(rise[r : r + 1, :], (8, 128))
    surface_copy = pltpu.make_async_copy(surface_ref, surface_hbm, sems.at[1])
    surface_copy.start()
    velocity_copy.wait()
    surface_copy.wait()


def swap(odd, even, axis, even_first=False):
    count = lax.axis_size(axis)

    def pairs(start):
        found = []
        for i in range(start, count - 1, 2):
            found += [(i, i + 1), (i + 1, i)]
        return found

    if even_first:
        even = lax.ppermute(even, axis, pairs(0))
        return lax.ppermute(odd, axis, pairs(1)), even
    return lax.ppermute(odd, axis, pairs(1)), lax.ppermute(even, axis, pairs(0))


def local(body_force, viscosity, topography, kappa):
    inputs = [
        pltpu.with_memory_space_constraint(x, pltpu.HBM) for x in (body_force, viscosity, topography, kappa)
    ]
    odd, even = pl.pallas_call(
        fetch,
        out_shape=[jax.ShapeDtypeStruct((4, 2, 8, 128), f32)] * 2,
        in_specs=[pl.BlockSpec(memory_space=pltpu.HBM)] * 2,
        out_specs=[vmem()] * 2,
        scratch_shapes=[pltpu.SemaphoreType.DMA((4,))],
        compiler_params=pltpu.CompilerParams(vmem_limit_bytes=1 << 20),
    )(*inputs[:2])
    odd, even = swap(odd, even, "gz")
    planes, left, right, height, conduct = pl.pallas_call(
        own_block,
        out_shape=[
            jax.ShapeDtypeStruct(shape, f32)
            for shape in ((4, 8, 8, 128), (2, 8, 128), (2, 8, 128), (64, 256), (64, 256))
        ],
        in_specs=[pl.BlockSpec(memory_space=pltpu.HBM)] * 4,
        out_specs=[vmem()] * 5,
        scratch_shapes=[pltpu.VMEM(x.shape, x.dtype) for x in inputs] + [pltpu.SemaphoreType.DMA((4,))],
        compiler_params=pltpu.CompilerParams(vmem_limit_bytes=8 << 20),
        cost_estimate=pl.CostEstimate(flops=20000 * 1024, bytes_accessed=1 << 18, transcendentals=0),
    )(*inputs)
    planes, even, odd = call(
        assemble,
        [(PLANES, 8, 128), (2, 8, 128), (2, 8, 128)],
        (planes, odd, even, left, right),
    )
    own = (odd, even)
    odd, even = swap(odd, even, "gy", even_first=True)
    low, high = call(edge_rows, [(COLUMN_ROW, 128)] * 2, (planes,))
    odd, even, columns, height, conduct = call(
        prepare_rows,
        [(GX_ROWS, 128), (GX_ROWS, 128), (3, 8, 128), (64, 256), (64, 256)],
        (low, high, *own, even, odd, height, conduct),
    )
    odd, even = swap(odd, even, "gx")
    (inner,) = call(inner_rows, [(48, 128)], (height, conduct))
    group = lax.axis_size("gx") * lax.axis_size("gy")
    image, sums, top, height = call(
        operate,
        [(3, 8, 8, 128), (group, 128), (2, 8, 128), (64, 128)],
        (planes, low, high, columns, odd, even, height, conduct, inner),
    )
    sums = lax.all_to_all(sums.reshape(group, 1, 128), ("gx", "gy"), 0, 0)
    (parts,) = call(middle, [(lax.axis_size("gz"), 4, 128)], (sums.reshape(group, 128), top))
    parts = lax.all_to_all(parts, "gz", 0, 0)
    shapes = ((3, 8, 8, 128), (64, 128))
    velocity, surface = pl.pallas_call(
        finish,
        out_shape=[jax.ShapeDtypeStruct(shape, f32) for shape in shapes],
        in_specs=[vmem()] * 4,
        out_specs=[pl.BlockSpec(memory_space=pltpu.HBM)] * 2,
        scratch_shapes=[pltpu.VMEM(shape, f32) for shape in shapes] + [pltpu.SemaphoreType.DMA((2,))],
        compiler_params=pltpu.CompilerParams(vmem_limit_bytes=8 << 20),
    )(parts, planes, image, height)
    return velocity, surface


def solution(mesh):
    in_specs = (P(None, "gz", "gx", "gy"), P("gz", "gx", "gy"), P("gx", "gy"), P("gx", "gy"))
    out_specs = (P(None, "gz", "gx", "gy"), P("gx", ("gy", "gz")))
    return jax.shard_map(local, mesh=mesh, in_specs=in_specs, out_specs=out_specs, check_vma=False)
```

```python
import jax
import jax.numpy as jnp
from jax import lax
from jax.experimental import pallas as pl
from jax.experimental.pallas import tpu as pltpu
from jax.sharding import PartitionSpec as P

STEPS = 8
DRAG = 1.0
TIME_STEP = 1.0
LOAD_GAIN = 4.0
FACE, EDGE, CORNER = 0.5, 0.25, 0.5 / 3.0
TOTAL = 6 * FACE + 12 * EDGE + 8 * CORNER

DEPTHS = 12
PLANES = 4 * DEPTHS
COLUMN_ROW = 8 * DEPTHS
SURFACE_ROW = COLUMN_ROW + 8
GX_ROWS = SURFACE_ROW + 32

f32 = jnp.float32


def vmem():
    return pl.BlockSpec(memory_space=pltpu.VMEM)


def call(body, outs, ins, scratch=(), cost=20000, limit=8 << 20):
    return pl.pallas_call(
        body,
        out_shape=[jax.ShapeDtypeStruct(s, f32) for s in outs],
        in_specs=[vmem() for _ in ins],
        out_specs=[vmem() for _ in outs],
        scratch_shapes=list(scratch),
        compiler_params=pltpu.CompilerParams(vmem_limit_bytes=limit),
        cost_estimate=pl.CostEstimate(flops=cost * 1024, bytes_accessed=1 << 18, transcendentals=0),
    )(*ins)


def lanes(shape):
    return lax.broadcasted_iota(jnp.int32, shape, len(shape) - 1)


def rolled(x, amount, axis=1):
    amount = amount % x.shape[axis]
    return x if amount == 0 else pltpu.roll(x, amount, axis)


def own_block(
    force_hbm, visc_hbm, topo_hbm, kappa_hbm, planes_ref, left_ref, right_ref, height_ref, conduct_ref,
    force_ref, visc_ref, topo_ref, kappa_ref, sems,
):
    moves = ((topo_hbm, topo_ref), (kappa_hbm, kappa_ref), (force_hbm, force_ref), (visc_hbm, visc_ref))
    copies = [pltpu.make_async_copy(source, target, sems.at[i]) for i, (source, target) in enumerate(moves)]
    for copy in copies:
        copy.start()
    for copy in copies:
        copy.wait()
    g = lax.axis_index("gz")
    last = lax.axis_size("gz") - 1
    lane = lanes((8, 128))
    pieces = []
    for v in range(8):
        piece = topo_ref[:, 128 * v : 128 * v + 128].reshape(8, 8, 128)
        pieces.append(jnp.sum(piece, axis=1))
    stacked = jnp.concatenate(pieces, axis=0)
    pick = (
        lax.broadcasted_iota(jnp.int32, (128, 128), 0) // 8 == lax.broadcasted_iota(jnp.int32, (128, 128), 1)
    ).astype(f32)
    sums = jnp.dot(stacked, pick, precision=lax.Precision.HIGHEST, preferred_element_type=f32)
    load = jnp.zeros((8, 128), f32)
    for v in range(8):
        load = load + rolled(sums[8 * v : 8 * v + 8], 16 * v)
    load = jnp.where(g == last, load * (-LOAD_GAIN / 64.0), 0.0)
    wide = lanes((64, 128))
    own = pl.ds(pl.multiple_of(g * 128, 128), 128)
    before = pl.ds(pl.multiple_of(jnp.maximum(g - 1, 0) * 128, 128), 128)
    after = pl.ds(pl.multiple_of(jnp.minimum(g + 1, last) * 128, 128), 128)
    for source, target in ((topo_ref, height_ref), (kappa_ref, conduct_ref)):
        target[:, 0:128] = source[:, own].astype(f32)
        side = jnp.where((wide < 8) & (g < last), source[:, after].astype(f32), 0.0)
        side = jnp.where((wide >= 120) & (g > 0), source[:, before].astype(f32), side)
        target[:, 128:256] = side
    width = topo_ref.shape[1]
    left = jnp.zeros((8, 128), f32)
    right = jnp.zeros((8, 128), f32)
    slot = 0
    for source in (topo_ref, kappa_ref):
        head = source[:, 0:128].astype(f32)
        tail = source[:, width - 128 : width].astype(f32)
        for r in range(8):
            mask = lane // 8 == slot
            left = jnp.where(mask, rolled(head[8 * r : 8 * r + 8], 8 * slot), left)
            right = jnp.where(mask, rolled(tail[8 * r : 8 * r + 8], 8 * slot - 120), right)
            slot += 1
    left_ref[1] = left
    right_ref[1] = right
    left = jnp.zeros((8, 128), f32)
    right = jnp.zeros((8, 128), f32)
    depths = visc_ref.shape[0]
    for field in range(4):
        for depth in range(depths):
            plane = visc_ref[depth] if field == 3 else force_ref[field, depth]
            if field == 2 and depth == depths - 1:
                plane = plane + load
            planes_ref[field, depth] = plane
            left, right = packed(plane, depth + 2, field, left, right, lane)
    left_ref[0] = left
    right_ref[0] = right


def is_even(axis):
    return lax.rem(lax.axis_index(axis), 2) == 0


def fetch(force_ref, visc_ref, odd_ref, even_ref, sems):
    depth = visc_ref.shape[0]
    start = jnp.where(is_even("gz"), 0, depth - 2)
    moves = []
    for target, first in ((odd_ref, start), (even_ref, depth - 2 - start)):
        moves.append((force_ref.at[:, pl.ds(first, 2)], target.at[0:3]))
        moves.append((visc_ref.at[pl.ds(first, 2)], target.at[3]))
    copies = [pltpu.make_async_copy(source, target, sems.at[i]) for i, (source, target) in enumerate(moves)]
    for copy in copies:
        copy.start()
    for copy in copies:
        copy.wait()


def packed(plane, depth, field, left, right, lane):
    first = 8 * depth + 2 * field
    mask = lane // 2 == first // 2
    left = jnp.where(mask, rolled(plane, first), left)
    return left, jnp.where(mask, rolled(plane, first - 126), right)


def assemble(own_ref, odd_ref, even_ref, left_ref, right_ref, planes_ref, even_out, odd_out):
    upward = is_even("gz")
    lane = lanes((8, 128))
    left, right = left_ref[0], right_ref[0]
    for field in range(4):
        for depth in range(DEPTHS):
            p = field * DEPTHS + depth
            if 2 <= depth < DEPTHS - 2:
                planes_ref[p] = own_ref[field, depth - 2]
                continue
            if depth < 2:
                plane = jnp.where(upward, odd_ref[field, depth], even_ref[field, depth])
            else:
                i = depth - (DEPTHS - 2)
                plane = jnp.where(upward, even_ref[field, i], odd_ref[field, i])
            planes_ref[p] = plane
            left, right = packed(plane, depth, field, left, right, lane)
    rightward = is_even("gy")
    odd_out[0] = jnp.where(rightward, left, right)
    even_out[0] = jnp.where(rightward, right, left)
    odd_out[1] = jnp.where(rightward, left_ref[1], right_ref[1])
    even_out[1] = jnp.where(rightward, right_ref[1], left_ref[1])


def edge_rows(planes_ref, low_ref, high_ref):
    for depth in range(DEPTHS):
        for field in range(4):
            plane = planes_ref.at[field * DEPTHS + depth]
            near = 8 * depth + field
            low_ref[near : near + 1, :] = plane[0:1, :]
            low_ref[near + 4 : near + 5, :] = plane[1:2, :]
            high_ref[near : near + 1, :] = plane[7:8, :]
            high_ref[near + 4 : near + 5, :] = plane[6:7, :]


def prepare_rows(
    low_ref, high_ref, own_even, own_odd, even_ref, odd_ref, height_ref, conduct_ref,
    odd_out, even_out, column_ref, height_out, conduct_out,
):
    g = lax.axis_index("gz")
    last = lax.axis_size("gz") - 1
    lane = lanes((8, 128))
    rightward = is_even("gy")

    def chosen(first, second, i):
        return jnp.where(rightward, first[i], second[i])

    before, after = chosen(odd_ref, even_ref, 0), chosen(even_ref, odd_ref, 0)
    before_surface, after_surface = chosen(odd_ref, even_ref, 1), chosen(even_ref, odd_ref, 1)
    side = lax.rem(lane, 2) == 0
    levels = (
        jnp.where(side, chosen(own_odd, own_even, 0), chosen(own_even, own_odd, 0)),
        jnp.where(side, rolled(before, -1), rolled(after, 1)),
        jnp.where(side, before, after),
    )
    downward = is_even("gx")

    def send(rows, low, high):
        odd_out[rows, :] = jnp.where(downward, low, high)
        even_out[rows, :] = jnp.where(downward, high, low)

    for depth in range(DEPTHS):
        rows = slice(8 * depth, 8 * depth + 8)
        send(rows, low_ref[rows, :], high_ref[rows, :])
    pad = [jnp.zeros((2, 128), f32)]
    send(
        slice(COLUMN_ROW, SURFACE_ROW),
        jnp.concatenate([x[0:2] for x in levels] + pad, axis=0),
        jnp.concatenate([x[6:8] for x in levels] + pad, axis=0),
    )
    for i in range(3):
        column_ref[i] = levels[i]
    slot = 0
    for index, (source, target) in enumerate(((height_ref, height_out), (conduct_ref, conduct_out))):
        base = SURFACE_ROW + 16 * index
        for r in range(8):
            rows = slice(8 * r, 8 * r + 8)
            main = source[rows, 0:128]
            side = source[rows, 128:256]
            side = jnp.where((g == 0) & (lane >= 120), rolled(before_surface, 120 - 8 * slot), side)
            side = jnp.where((g == last) & (lane < 8), rolled(after_surface, -8 * slot), side)
            target[rows, 0:128] = main
            target[rows, 128:256] = side
            if r == 0:
                first = (main, side)
            if r == 7:
                send(slice(base, base + 8), first[0], main)
                send(slice(base + 8, base + 16), first[1], side)
            slot += 1


def weighted(before, here, after):
    outer = before + after
    return outer, FACE * here + EDGE * outer, EDGE * here + CORNER * outer


def pair(x):
    return rolled(x, 1, 0) + rolled(x, x.shape[0] - 1, 0)


def lane_pair(x, lane, first, last):
    return jnp.where(lane == 0, first, rolled(x, 1)) + jnp.where(lane == 127, last, rolled(x, 127))


def row_pair(x, row, edge, field):
    up = jnp.where(row == 0, rolled(edge, -field, 0), rolled(x, 1, 0))
    return up + jnp.where(row == 7, rolled(edge, 3 - field, 0), rolled(x, 7, 0))


def to_first(x, depth, field):
    return rolled(x, -(8 * depth + 2 * field))


def to_last(x, depth, field):
    return rolled(x, 126 - (8 * depth + 2 * field))


def spread_rows(x, row):
    field = lax.rem(row, 4)
    for f in range(3):
        x = jnp.where(field == f, rolled(x, f - 3, 0), x)
    return x


def spread_columns(x, lane):
    field = lax.rem(lane, 8) // 2
    for f in range(3):
        x = jnp.where(field == f, rolled(x, 2 * (f - 3)), x)
    return x


def column_sums(levels):
    parts = [weighted(rolled(x, 8), x, rolled(x, 120)) for x in levels]
    (_, ai, bi), (outer, an, bn), (_, af, bf) = parts
    beside = an + pair(bn)
    return FACE * outer + pair(an) + (ai + af) + pair(bi + bf), beside


def beside_rows(beside, depth, row):
    near = jnp.where(row < 4, jnp.broadcast_to(beside[15:16], (8, 128)), jnp.broadcast_to(beside[8:9], (8, 128)))
    field = lax.rem(row, 4)
    first, last = to_first(near, depth, 0), to_last(near, depth, 0)
    for f in range(1, 4):
        first = jnp.where(field == f, to_first(near, depth, f), first)
        last = jnp.where(field == f, to_last(near, depth, f), last)
    return first, last


def sided(odd_ref, even_ref, axis):
    first = is_even(axis)

    def before(rows):
        return jnp.where(first, odd_ref[rows, :], even_ref[rows, :])

    def after(rows):
        return jnp.where(first, even_ref[rows, :], odd_ref[rows, :])

    return before, after


def flux(conduct, slope):
    return conduct * slope * lax.rsqrt(1.0 + slope * slope)


def steps(h, k):
    rows = h.shape[0]
    inside = k > 0.0
    along = 0.5 * (k + rolled(k, 255, 1))
    along_before = rolled(along, 1, 1)
    across = 0.5 * (k + rolled(k, rows - 1, 0))
    for step in range(STEPS):
        q = flux(along, rolled(h, 255, 1) - h) - flux(along_before, h - rolled(h, 1, 1))
        r = flux(across, rolled(h, rows - 1, 0) - h)
        h = jnp.where(inside, h + TIME_STEP * (q + (r - rolled(r, 1, 0))), 0.0)
    return h


def inner_rows(height_ref, conduct_ref, out_ref):
    out_ref[...] = steps(height_ref[...], conduct_ref[...])[8:56, 0:128]


def operate(
    planes_ref, low_ref, high_ref, column_ref, odd_ref, even_ref, height_ref, conduct_ref, inner_ref,
    image_ref, sums_ref, top_ref, out_ref,
):
    lane = lanes((8, 128))
    row = lax.broadcasted_iota(jnp.int32, (8, 128), 0)
    wide = lanes((16, 128))
    before, after = sided(odd_ref, even_ref, "gx")

    def banded(source, base):
        def joined(side):
            return jnp.concatenate([side(slice(base, base + 8)), side(slice(base + 8, base + 16))], axis=1)

        return jnp.concatenate([source[48:64, :], joined(after), joined(before), source[0:16, :]], axis=0)

    band = steps(banded(height_ref, SURFACE_ROW), banded(conduct_ref, SURFACE_ROW + 16))
    out_ref[0:8, :] = band[32:40, 0:128]
    out_ref[8:56, :] = inner_ref[...]
    out_ref[56:64, :] = band[8:16, 0:128]
    columns = []
    for i in range(3):
        rows = slice(COLUMN_ROW + 2 * i, COLUMN_ROW + 2 * i + 2)
        columns.append(jnp.concatenate([column_ref[i], after(rows), jnp.zeros((4, 128), f32), before(rows)], axis=0))
    column_eta = [spread_columns(x, wide) for x in columns]
    column_sum, beside = column_sums(columns)
    column_sum_eta, beside_eta = column_sums([x * y for x, y in zip(columns, column_eta)])
    near_eta = column_eta[1]
    column_diag = DRAG + TOTAL * near_eta + spread_columns(column_sum, wide)
    column_image = columns[1] * column_diag - near_eta * column_sum - column_sum_eta
    column_image = jnp.where(near_eta > 0.0, column_image, 0.0)
    rows_of, rows_eta = [], []
    for depth in range(DEPTHS):
        rows = slice(8 * depth, 8 * depth + 8)
        b, a = before(rows), after(rows)
        found = (
            jnp.where(row < 4, low_ref[rows, :], rolled(high_ref[rows, :], 4, 0)),
            jnp.where(row < 4, b, rolled(a, 4, 0)),
            jnp.where(row < 4, rolled(b, 4, 0), a),
        )
        rows_of.append(found)
        rows_eta.append([spread_rows(x, row) for x in found])
    rows_product = [[x * y for x, y in zip(found, etas)] for found, etas in zip(rows_of, rows_eta)]

    def row_sums(levels, depth, beside_columns):
        parts = [weighted(levels[depth - 1][i], levels[depth][i], levels[depth + 1][i]) for i in range(3)]
        (_, ai, bi), (outer, an, bn), (_, af, bf) = parts
        first, last = beside_rows(beside_columns, depth, row)
        return FACE * outer + (ai + af) + lane_pair(an + (bi + bf), lane, first, last), an, bn

    def plane_sum(three, an, bn, beside_columns, depth, field):
        outer, a, b = weighted(*three)
        both = a + row_pair(b, row, bn, field)
        own = beside_columns[0:8]
        sides = lane_pair(both, lane, to_first(own, depth, field), to_last(own, depth, field))
        return FACE * outer + row_pair(a, row, an, field) + sides

    def plane(field, depth):
        return planes_ref[field * DEPTHS + depth]

    image, row_image, diagonal = {}, {}, {}
    for depth in range(1, DEPTHS - 1):
        row_sum, an, bn = row_sums(rows_of, depth, beside)
        row_sum_eta, an_eta, bn_eta = row_sums(rows_product, depth, beside_eta)
        near, eta = rows_of[depth][1], rows_eta[depth][1]
        diag = DRAG + TOTAL * eta + spread_rows(row_sum, row)
        row_image[depth] = jnp.where(eta > 0.0, near * diag - eta * row_sum - row_sum_eta, 0.0)
        e = [plane(3, depth + i) for i in (-1, 0, 1)]
        diag = DRAG + TOTAL * e[1] + plane_sum(e, an, bn, beside, depth, 3)
        diagonal[depth] = diag
        for c in range(3):
            v = [plane(c, depth + i) for i in (-1, 0, 1)]
            ev = [x * y for x, y in zip(e, v)]
            out = v[1] * diag - e[1] * plane_sum(v, an, bn, beside, depth, c)
            out = out - plane_sum(ev, an_eta, bn_eta, beside_eta, depth, c)
            image[c, depth] = jnp.where(e[1] > 0.0, out, 0.0)
    _, an, bn = weighted(rolled(column_image, 8), column_image, rolled(column_image, 120))
    beside = an + pair(bn)
    m = [jnp.zeros((8, 128), f32) for _ in range(4)]
    for depth in range(2, DEPTHS - 2):
        _, an, bn = weighted(row_image[depth - 1], row_image[depth], row_image[depth + 1])
        e = plane(3, depth)
        for c in range(3):
            s = plane_sum([image[c, depth + i] for i in (-1, 0, 1)], an, bn, beside, depth, c)
            v, q = plane(c, depth), image[c, depth]
            image_ref[c, depth - 2] = q
            m[0] = m[0] + v * v
            m[1] = m[1] + v * q
            m[2] = m[2] + q * q
            m[3] = m[3] + q * (q * diagonal[depth] - 2.0 * (e * s))
    total = jnp.zeros((8, 128), f32)
    for k in range(4):
        part = m[k]
        for amount in (64, 32, 16):
            part = part + rolled(part, amount)
        total = jnp.where(lane // 16 == 2 + k, part, total)
    for amount in (4, 2, 1):
        total = total + rolled(total, amount, 0)
    for i in range(sums_ref.shape[0] // 8):
        sums_ref[8 * i : 8 * i + 8, :] = total
    top_ref[0] = plane(2, DEPTHS - 3)
    top_ref[1] = image[2, DEPTHS - 3]


def middle(sums_ref, top_ref, out_ref):
    lane = lanes((8, 128))
    row = lax.broadcasted_iota(jnp.int32, (8, 128), 0)
    part = jnp.sum(sums_ref[...], axis=0, keepdims=True)
    flat = []
    for i in range(2):
        found = top_ref[i]
        for k in range(1, 8):
            found = jnp.where(
                lane // 16 == lax.rem(row + k, 8), rolled(rolled(top_ref[i], -k, 0), 16 * k), found
            )
        flat.append(found)
    for j in range(out_ref.shape[0]):
        out_ref[j, 0:1, :] = flat[0][j : j + 1]
        out_ref[j, 1:2, :] = flat[1][j : j + 1]
        out_ref[j, 2:3, :] = part
        out_ref[j, 3:4, :] = part


def finish(parts_ref, planes_ref, image_ref, height_ref, velocity_hbm, surface_hbm, velocity_ref, surface_ref, sems):
    count = parts_ref.shape[0]
    lane = lanes((1, 128))
    row = lax.broadcasted_iota(jnp.int32, (8, 128), 0)
    found = []
    for i in range(2):
        flat = jnp.broadcast_to(parts_ref[count - 1, i : i + 1, :], (8, 128))
        cells = flat
        for r in range(1, 8):
            cells = jnp.where(row == r, rolled(flat, -16 * r), cells)
        found.append(cells)
    top = jnp.where(lanes((16, 128)) < 16, jnp.concatenate(found, axis=0), 0.0)
    spread = (
        lax.broadcasted_iota(jnp.int32, (128, 128), 1) // 8 == lax.broadcasted_iota(jnp.int32, (128, 128), 0)
    ).astype(f32)
    wide = jnp.dot(top, spread, precision=lax.Precision.HIGHEST, preferred_element_type=f32)
    total = parts_ref[0, 2:3, :]
    for j in range(1, count):
        total = total + parts_ref[j, 2:3, :]

    def moment(k):
        return jnp.sum(jnp.where(lane // 16 == 2 + k, total, 0.0), axis=1, keepdims=True)

    m0, m1, m2, m3 = (moment(k) for k in range(4))
    first = m0 / m1
    later = first * first * m2 - m0
    gain = 1.0 + later / m0
    second = later / (gain * gain * m1 - 2.0 * first * gain * m2 + first * first * m3)
    on_force = first + second * gain
    on_image = -(second * first)
    for c in range(3):
        for depth in range(8):
            velocity_ref[c, depth] = on_force * planes_ref[c * DEPTHS + depth + 2] + on_image * image_ref[c, depth]
    velocity_copy = pltpu.make_async_copy(velocity_ref, velocity_hbm, sems.at[0])
    velocity_copy.start()
    rise = (STEPS * TIME_STEP) * (on_force * wide[0:8] + on_image * wide[8:16])
    for r in range(8):
        rows = slice(8 * r, 8 * r + 8)
        surface_ref[rows, :] = height_ref[rows, :] + jnp.broadcast_to(rise[r : r + 1, :], (8, 128))
    surface_copy = pltpu.make_async_copy(surface_ref, surface_hbm, sems.at[1])
    surface_copy.start()
    velocity_copy.wait()
    surface_copy.wait()


def swap(odd, even, axis, even_first=False):
    count = lax.axis_size(axis)

    def pairs(start):
        found = []
        for i in range(start, count - 1, 2):
            found += [(i, i + 1), (i + 1, i)]
        return found

    if even_first:
        even = lax.ppermute(even, axis, pairs(0))
        return lax.ppermute(odd, axis, pairs(1)), even
    return lax.ppermute(odd, axis, pairs(1)), lax.ppermute(even, axis, pairs(0))


def local(body_force, viscosity, topography, kappa):
    inputs = [
        pltpu.with_memory_space_constraint(x, pltpu.HBM) for x in (body_force, viscosity, topography, kappa)
    ]
    odd, even = pl.pallas_call(
        fetch,
        out_shape=[jax.ShapeDtypeStruct((4, 2, 8, 128), f32)] * 2,
        in_specs=[pl.BlockSpec(memory_space=pltpu.HBM)] * 2,
        out_specs=[vmem()] * 2,
        scratch_shapes=[pltpu.SemaphoreType.DMA((4,))],
        compiler_params=pltpu.CompilerParams(vmem_limit_bytes=1 << 20),
    )(*inputs[:2])
    odd, even = swap(odd, even, "gz")
    planes, left, right, height, conduct = pl.pallas_call(
        own_block,
        out_shape=[
            jax.ShapeDtypeStruct(shape, f32)
            for shape in ((4, 8, 8, 128), (2, 8, 128), (2, 8, 128), (64, 256), (64, 256))
        ],
        in_specs=[pl.BlockSpec(memory_space=pltpu.HBM)] * 4,
        out_specs=[vmem()] * 5,
        scratch_shapes=[pltpu.VMEM(x.shape, x.dtype) for x in inputs] + [pltpu.SemaphoreType.DMA((4,))],
        compiler_params=pltpu.CompilerParams(vmem_limit_bytes=8 << 20),
        cost_estimate=pl.CostEstimate(flops=20000 * 1024, bytes_accessed=1 << 18, transcendentals=0),
    )(*inputs)
    planes, even, odd = call(
        assemble,
        [(PLANES, 8, 128), (2, 8, 128), (2, 8, 128)],
        (planes, odd, even, left, right),
    )
    own = (even, odd)
    odd, even = swap(odd, even, "gy", even_first=True)
    low, high = call(edge_rows, [(COLUMN_ROW, 128)] * 2, (planes,))
    odd, even, columns, height, conduct = call(
        prepare_rows,
        [(GX_ROWS, 128), (GX_ROWS, 128), (3, 8, 128), (64, 256), (64, 256)],
        (low, high, *own, even, odd, height, conduct),
    )
    odd, even = swap(odd, even, "gx")
    (inner,) = call(inner_rows, [(48, 128)], (height, conduct))
    group = lax.axis_size("gx") * lax.axis_size("gy")
    image, sums, top, height = call(
        operate,
        [(3, 8, 8, 128), (group, 128), (2, 8, 128), (64, 128)],
        (planes, low, high, columns, odd, even, height, conduct, inner),
    )
    sums = lax.all_to_all(sums.reshape(group, 1, 128), ("gx", "gy"), 0, 0)
    (parts,) = call(middle, [(lax.axis_size("gz"), 4, 128)], (sums.reshape(group, 128), top))
    parts = lax.all_to_all(parts, "gz", 0, 0)
    shapes = ((3, 8, 8, 128), (64, 128))
    velocity, surface = pl.pallas_call(
        finish,
        out_shape=[jax.ShapeDtypeStruct(shape, f32) for shape in shapes],
        in_specs=[vmem()] * 4,
        out_specs=[pl.BlockSpec(memory_space=pltpu.HBM)] * 2,
        scratch_shapes=[pltpu.VMEM(shape, f32) for shape in shapes] + [pltpu.SemaphoreType.DMA((2,))],
        compiler_params=pltpu.CompilerParams(vmem_limit_bytes=8 << 20),
    )(parts, planes, image, height)
    return velocity, surface


def solution(mesh):
    in_specs = (P(None, "gz", "gx", "gy"), P("gz", "gx", "gy"), P("gx", "gy"), P("gx", "gy"))
    out_specs = (P(None, "gz", "gx", "gy"), P("gx", ("gy", "gz")))
    return jax.shard_map(local, mesh=mesh, in_specs=in_specs, out_specs=out_specs, check_vma=False)
```
